32 devices in a mesh: dp: 16 (over z, x, core), tensor: 2 (over y).
Axes of the slice: x: 2, y: 2, z: 4, core: 2. Of those that a mesh axis runs over, the one named last changes fastest.
Arguments:
- hidden_in: bfloat16 [16, 561, 1024], P('dp', None, 'tensor'), may hold values from -6 to 6
- lengths: int32 [16], P('dp'), may hold values from 52 to 512, as said below
- boxes: int32 [16, 561, 2], P('dp'), may hold values from 0 to 1000
- w_qkv: bfloat16 [1024, 3, 1024], P(None, None, 'tensor'), may hold values from -0.1875 to 0.1875
- w_out: bfloat16 [1024, 1024], P('tensor'), may hold values from -1 to 1
- w_up: bfloat16 [1024, 4096], P(None, 'tensor'), may hold values from -0.1875 to 0.1875
- w_down: bfloat16 [4096, 1024], P('tensor'), may hold values from -0.09375 to 0.09375
- rel_keys: bfloat16 [3, 128, 1024], P(None, None, 'tensor'), may hold values from -6 to 6
- rel_queries: bfloat16 [3, 128, 1024], P(None, None, 'tensor'), may hold values from -6 to 6
- norm_gains: float32 [2, 1024], P(None, 'tensor'), may hold values from 0.25 to 1.75
- norm_shifts: float32 [2, 1024], P(None, 'tensor'), may hold values from -3 to 3
- out_grad: bfloat16 [16, 561, 1024], P('dp', None, 'tensor'), may hold values from -6 to 6
Outputs:
- hidden_out: bfloat16 [16, 561, 1024], P('dp', None, 'tensor')
- input_grad: bfloat16 [16, 561, 1024], P('dp', None, 'tensor')
- qkv_grad: float32 [1024, 3, 1024], P(None, None, 'tensor')
- out_weight_grad: float32 [1024, 1024], P('tensor')
- up_grad: float32 [1024, 4096], P(None, 'tensor')
- down_grad: float32 [4096, 1024], P('tensor')
- rel_keys_grad: float32 [3, 128, 1024], P(None, None, 'tensor')
- rel_queries_grad: float32 [3, 128, 1024], P(None, None, 'tensor')
- gains_grad: float32 [2, 1024], P(None, 'tensor')
- shifts_grad: float32 [2, 1024], P(None, 'tensor')
The draws below stay inside these ranges and needn't reach their ends.
Inputs may be any that keep to these rules, and one draw needn't show every extreme that they name: `lengths`: text slot s of a document holds a real token when s is under its count; in every draw some document has all 512 text slots real.
All inputs are finite; a program needn't handle non-finite values.
Results may differ from the reference program's by a relative error of at most 0.02.
Values may be sent and summed in bfloat16 or wider, within the bound.
No kernel may reach another device: no remote copies, remote signals or barrier semaphores. Data moves between devices by JAX's collectives and lax.ppermute only.
A program may use at most 512 MiB of HBM per device.

```python
import math
from functools import partial
import jax
import jax.numpy as jnp
from jax import lax

D = 1024
HEADS = 16
HEAD_DIM = 64
FF = 4096
BUCKETS = 128
TEXT = 512
SEQ = 561
DOCS = 16
BOX_STEP = 16


def draw_lengths(key, part):
    drawn = jax.random.randint(key, (DOCS,), TEXT // 10 + 1, TEXT + 1)
    chosen = jax.random.randint(jax.random.fold_in(key, 7), (), 0, DOCS)
    return drawn.at[chosen].set(TEXT).astype(jnp.int32)


def plant(array, key, low, top_value):
    extent = array.shape
    place = [jax.random.randint(jax.random.fold_in(key, axis), (), 0, extent[axis]) for axis in range(len(extent))]
    array = array.at[tuple(place)].set(low)
    longest = extent.index(max(extent))
    place[longest] = (place[longest] + 1) % extent[longest]
    return array.at[tuple(place)].set(top_value)


def block_levels(rng, shape, pieces, smallest, largest):
    def one(axis_at, parts):
        heights = jax.random.uniform(jax.random.fold_in(jax.random.fold_in(rng, 6), axis_at), (parts,), jnp.float32, smallest / len(pieces), largest / len(pieces))
        return jnp.repeat(jnp.exp(heights), shape[axis_at] // parts).reshape((-1,) + (1,) * (len(shape) - axis_at - 1))

    factor_of = one(*pieces[0])
    for cut in pieces[1:]:
        factor_of = factor_of * one(*cut)
    return factor_of


def noise(rng, extent, scale, most, cuts=(), held_as=jnp.bfloat16):
    array = jax.random.normal(rng, extent, jnp.float32) * scale
    if len(cuts) > 0:
        array = block_levels(rng, extent, cuts, -0.22, 0.18) * array
    return jnp.clip(array, min=-most, max=most).astype(held_as)


def setup_inputs(seed: int = 0) -> dict:
    streams_of = jax.random.split(jax.random.key(seed), 13)
    return {
        "hidden_in": noise(streams_of[0], (DOCS, SEQ, D), 1.0, 6.0, ((0, 16), (2, 2))),
        "lengths": draw_lengths(jax.random.fold_in(streams_of[12], 71), 0),
        "boxes": plant(jax.random.randint(streams_of[2], (DOCS, SEQ, 2), 0, 1001), jax.random.fold_in(streams_of[2], 1), 0, 1000).astype(jnp.int32),
        "w_qkv": noise(streams_of[3], (D, 3, D), D ** -0.5, 0.1875, ((2, 2),)),
        "w_out": noise(streams_of[4], (D, D), (D // 32) ** -0.5, 1.0, ((0, 2),)),
        "w_up": noise(streams_of[5], (D, FF), D ** -0.5, 0.1875, ((1, 2),)),
        "w_down": noise(streams_of[6], (FF, D), FF ** -0.5, 0.09375, ((0, 2),)),
        "rel_keys": noise(streams_of[7], (3, BUCKETS, D), 1.0, 6.0, ((2, 2),)),
        "rel_queries": noise(streams_of[8], (3, BUCKETS, D), 1.0, 6.0, ((2, 2),)),
        "norm_gains": jnp.clip(1.0 + 0.15 * jax.random.normal(streams_of[9], (2, D), jnp.float32), 0.25, 1.75),
        "norm_shifts": noise(streams_of[10], (2, D), 0.5, 3.0, ((1, 2),), jnp.float32),
        "out_grad": noise(streams_of[11], (DOCS, SEQ, D), 1.0, 6.0, ((0, 16), (2, 2))),
    }


@jax.custom_vjp
def low(v):
    return lax.optimization_barrier(v.astype(jnp.bfloat16)).astype(jnp.float32)

@jax.custom_vjp
def low_back(v):
    return v

def low_keep(v):
    return (low(v), None)

def low_pass(kept, grad):
    return (grad,)

def back_keep(v):
    return (v, None)

def back_low(kept, grad):
    return (low(grad),)
low.defvjp(low_keep, low_pass)
low_back.defvjp(back_keep, back_low)
PRECISE = lax.Precision.HIGHEST
NEG_LARGE = -1e+30
EPSILON = 1e-05

def relative_buckets(box_doc):
    middle = BUCKETS // 2
    places = jnp.arange(SEQ, dtype=jnp.int32)
    linear = jnp.clip(places[None, :] - places[:, None], -middle, middle - 1) + middle
    across = jnp.clip((box_doc[None, :, 0] - box_doc[:, None, 0]) // BOX_STEP, -middle, middle - 1) + middle
    upward = jnp.clip((box_doc[None, :, 1] - box_doc[:, None, 1]) // BOX_STEP, -middle, middle - 1) + middle
    return jnp.stack([linear, across, upward]).astype(jnp.int32)

def attend_doc(inputs, rel_k, rel_q):
    queries, keys_doc, values_doc, box_doc, length = inputs
    buckets = relative_buckets(box_doc)
    index = jnp.broadcast_to(buckets[:, None], (3, HEADS, SEQ, SEQ))
    content = jnp.einsum('ihe,jhe->hij', queries, keys_doc, precision=PRECISE)
    near_query = low_back(jnp.einsum('ihe,tbhe->thib', queries, rel_k, precision=PRECISE))
    near_key = low_back(jnp.einsum('jhe,tbhe->thjb', keys_doc, rel_q, precision=PRECISE))
    from_query = lax.optimization_barrier(jnp.sum(jnp.take_along_axis(near_query, index, axis=3), axis=0))
    from_key = lax.optimization_barrier(jnp.sum(jnp.take_along_axis(near_key, index, axis=3), axis=0))
    raw = content + from_query + jnp.swapaxes(from_key, 1, 2)
    places = jnp.arange(SEQ, dtype=jnp.int32)
    valid = (places < length) | (places >= TEXT)
    score_scale = 1.0 / math.sqrt(3 * HEAD_DIM)
    scores = low_back(jnp.where(valid[None, None, :], score_scale * raw, NEG_LARGE))
    probs = jax.nn.softmax(scores, axis=-1)
    return jnp.einsum('hij,jhe->ihe', low(probs), values_doc, precision=PRECISE)

def layer_norm(values_in, gain, shift):
    mean_row = lax.optimization_barrier(jnp.mean(values_in, axis=-1, keepdims=True))
    square_row = lax.optimization_barrier(jnp.mean(values_in * values_in, axis=-1, keepdims=True))
    scale_row = lax.rsqrt(square_row - mean_row * mean_row + EPSILON)
    return (values_in - mean_row) * scale_row * gain + shift

def reference(hidden_in, lengths, boxes, w_qkv, w_out, w_up, w_down, rel_keys, rel_queries, norm_gains, norm_shifts, out_grad):

    def forward(inputs_f, qkv_f, out_f, up_f, down_f, relk_f, relq_f, gains_f, shifts_f):
        row_data = inputs_f.reshape(DOCS * SEQ, D)
        projected = jnp.dot(row_data, qkv_f.reshape(D, 3 * D), precision=PRECISE)
        projected = low_back(low(projected)).reshape(DOCS, SEQ, 3, HEADS, HEAD_DIM)
        rel_k = relk_f.reshape(3, BUCKETS, HEADS, HEAD_DIM)
        rel_q = relq_f.reshape(3, BUCKETS, HEADS, HEAD_DIM)
        attend = jax.checkpoint(partial(attend_doc, rel_k=rel_k, rel_q=rel_q))
        context = lax.map(attend, (projected[:, :, 0], projected[:, :, 1], projected[:, :, 2], boxes, lengths))
        context = low_back(low(context)).reshape(DOCS * SEQ, D)
        attn = low_back(jnp.dot(context, out_f, precision=PRECISE))
        normed_first = layer_norm(row_data + attn, gains_f[0], shifts_f[0])
        upper = low_back(jnp.dot(low(normed_first), up_f, precision=PRECISE))
        active = low(jax.nn.gelu(upper, approximate=False))
        ffn = low_back(jnp.dot(active, down_f, precision=PRECISE))
        result = layer_norm(normed_first + ffn, gains_f[1], shifts_f[1])
        return result.reshape(DOCS, SEQ, D)
    primals = tuple((entry.astype(jnp.float32) for entry in (hidden_in, w_qkv, w_out, w_up, w_down, rel_keys, rel_queries, norm_gains, norm_shifts)))
    result, pullback = jax.vjp(forward, *primals)
    grads = pullback(out_grad.astype(jnp.float32))
    return (result.astype(jnp.bfloat16), grads[0].astype(jnp.bfloat16), grads[1], grads[2], grads[3], grads[4], grads[5], grads[6], grads[7], grads[8])
```

```python
import math, functools
import jax, jax.numpy as jnp
from jax import lax
from jax.sharding import PartitionSpec as P
from jax.experimental import pallas as pl
from jax.experimental.pallas import tpu as pltpu

HEAD_DIM = 64
BUCKETS = 128
TEXT = 512
NEG = -1e30
SCALE = 1.0 / math.sqrt(3 * HEAD_DIM)
F32 = jnp.float32
BF16 = jnp.bfloat16


def nt(a, b):
    return lax.dot_general(a, b, (((1,), (1,)), ((), ())), preferred_element_type=F32)


def nn(a, b):
    return lax.dot_general(a, b, (((1,), (0,)), ((), ())), preferred_element_type=F32)


def iota(shape, d):
    return lax.broadcasted_iota(jnp.int32, shape, d)


def lane_pick(table, index):
    return jnp.take_along_axis(table, index, axis=1, mode="promise_in_bounds")


def fwd_kernel(slots, sp, len_ref, q_ref, k_ref, v_ref, relk_ref, relq_ref, bc_ref, br_ref,
               ctx_ref, p_ref, qs, ks, vs, idx, nq, nk, fk):
    pair = pl.program_id(1)
    nb = sp // 128

    @pl.when(pair == 0)
    def _():
        qs[...] = jnp.zeros_like(qs)
        ks[...] = jnp.zeros_like(ks)
        vs[...] = jnp.zeros_like(vs)

        def rows(b, c):
            r0 = pl.multiple_of(b * 128, 128)
            row = iota((128, sp), 0) + r0
            col = iota((128, sp), 1)
            idx[0, pl.ds(r0, 128), :] = jnp.clip(col - row, -64, 63) + 64
            for t in range(2):
                x_i = bc_ref[pl.ds(r0, 128), t:t + 1]
                x_j = br_ref[t:t + 1, :]
                idx[t + 1, pl.ds(r0, 128), :] = jnp.clip((x_j - x_i) >> 4, -64, 63) + 64
            return c
        lax.fori_loop(0, nb, rows, 0)

    qs[0:slots, :] = q_ref[...]
    ks[0:slots, :] = k_ref[...]
    vs[0:slots, :] = v_ref[...]
    place = iota((1, sp), 1)
    length = len_ref[pl.program_id(0)]
    valid = (place < length) | ((place >= TEXT) & (place < slots))
    half = iota((1, 128), 1) < 64

    for h in range(2):
        mine = half if h == 0 else jnp.logical_not(half)
        qm = jnp.where(mine, qs[...], 0)
        km = jnp.where(mine, ks[...], 0)
        nq[...] = nt(qm, relk_ref[...])
        nk[...] = nt(km, relq_ref[...])

        def key_side(b, c):
            r0 = pl.multiple_of(b * 128, 128)
            for ib in range(nb):
                g = None
                for t in range(3):
                    e = lane_pick(nk[pl.ds(r0, 128), t * 128:(t + 1) * 128],
                                  idx[t, pl.ds(r0, 128), ib * 128:(ib + 1) * 128])
                    g = e if g is None else g + e
                fk[ib * 128:(ib + 1) * 128, pl.ds(r0, 128)] = g.T
            return c
        lax.fori_loop(0, nb, key_side, 0)

        def query_side(b, c):
            r0 = pl.multiple_of(b * 128, 128)
            q_b = jnp.where(mine, qs[pl.ds(r0, 128), :], 0)
            s = nt(q_b, ks[...]) + fk[pl.ds(r0, 128), :]
            parts = []
            for jb in range(nb):
                g = s[:, jb * 128:(jb + 1) * 128]
                for t in range(3):
                    g = g + lane_pick(nq[pl.ds(r0, 128), t * 128:(t + 1) * 128],
                                      idx[t, pl.ds(r0, 128), jb * 128:(jb + 1) * 128])
                parts.append(g)
            s = jnp.concatenate(parts, axis=1)
            s = jnp.where(valid, s * SCALE, NEG)
            m = jnp.max(s, axis=1, keepdims=True)
            e = jnp.exp(s - m)
            tot = jnp.sum(e, axis=1, keepdims=True)
            p = (e * (1.0 / tot)).astype(BF16)
            p_ref[h, pl.ds(r0, 128), :] = p
            c_b = nn(p, vs[...])
            fk[pl.ds(r0, 128), 0:128] = c_b
            return c
        lax.fori_loop(0, nb, query_side, 0)
        if h == 0:
            ctx_ref[...] = fk[0:slots, 0:128].astype(BF16)
        else:
            ctx_ref[...] = jnp.where(mine, fk[0:slots, 0:128].astype(BF16), ctx_ref[...])


def attend_forward(lengths, qkv, relk, relq, boxes_col, boxes_row, heads):
    docs, slots, width = qkv.shape
    width = width // 3
    sp = boxes_row.shape[2]
    pairs = heads // 2

    def part(t):
        return pl.BlockSpec((None, slots, 128), lambda d, p, ln: (d, 0, t * pairs + p))
    grid_spec = pltpu.PrefetchScalarGridSpec(
        num_scalar_prefetch=1, grid=(docs, pairs),
        in_specs=[part(0), part(1), part(2),
                  pl.BlockSpec((3 * BUCKETS, 128), lambda d, p, ln: (0, p)),
                  pl.BlockSpec((3 * BUCKETS, 128), lambda d, p, ln: (0, p)),
                  pl.BlockSpec((None, sp, 2), lambda d, p, ln: (d, 0, 0)),
                  pl.BlockSpec((None, 2, sp), lambda d, p, ln: (d, 0, 0))],
        out_specs=[pl.BlockSpec((None, slots, 128), lambda d, p, ln: (d, 0, p)),
                   pl.BlockSpec((None, 2, sp, sp), lambda d, p, ln: (d, p, 0, 0))],
        scratch_shapes=[pltpu.VMEM((sp, 128), BF16)] * 3
        + [pltpu.VMEM((3, sp, sp), jnp.int32), pltpu.VMEM((sp, 384), F32), pltpu.VMEM((sp, 384), F32),
           pltpu.VMEM((sp, sp), F32)])
    return pl.pallas_call(
        functools.partial(fwd_kernel, slots, sp),
        out_shape=[jax.ShapeDtypeStruct((docs, slots, width), BF16),
                   jax.ShapeDtypeStruct((docs, heads, sp, sp), BF16)],
        grid_spec=grid_spec, name="attend_forward",
        compiler_params=pltpu.CompilerParams(vmem_limit_bytes=56 << 20),
    )(lengths, qkv, qkv, qkv, relk, relq, boxes_col, boxes_row)


def bwd_kernel(slots, sp, width, q_ref, k_ref, v_ref, dc_ref, p_ref, relk_ref, relq_ref, bc_ref, br_ref,
               dqkv_ref, gk_ref, gq_ref,
               qs, ks, vs, dcs, base, ex, ey, mx, my, ds, dst, gt, acc):
    pair = pl.program_id(1)
    nb = sp // 128

    @pl.when(pair == 0)
    def _():
        for r in (qs, ks, vs, dcs, ds, dst):
            r[...] = jnp.zeros_like(r)
        lane = iota((sp, 128), 1)
        ax = bc_ref[:, 0:1] >> 4
        ay = bc_ref[:, 1:2] >> 4
        left = lane < 64
        c = lane & 63
        a = jnp.where(left, ax, ay)
        one = jnp.where(c == a, 1.0, 0.0)
        nxt = jnp.where(c == a + 1, 1.0, 0.0)
        base[...] = one.astype(BF16)
        e = nxt - one
        ex[...] = jnp.where(left, e, 0.0).astype(BF16)
        ey[...] = jnp.where(left, 0.0, e).astype(BF16)

        def rows(b, c):
            r0 = pl.multiple_of(b * 128, 128)
            for t, m in ((0, mx), (1, my)):
                r_i = bc_ref[pl.ds(r0, 128), t:t + 1] & 15
                r_j = br_ref[t:t + 1, :] & 15
                m[pl.ds(r0, 128), :] = jnp.where(r_j >= r_i, 1.0, 0.0).astype(BF16)
            return c
        lax.fori_loop(0, nb, rows, 0)

    qs[0:slots, :] = q_ref[...]
    ks[0:slots, :] = k_ref[...]
    vs[0:slots, :] = v_ref[...]
    dcs[0:slots, :] = dc_ref[...]
    half = iota((1, 128), 1) < 64
    lane1 = iota((128, 128), 1)
    row1 = iota((128, 128), 0)

    for h in range(2):
        mine = half if h == 0 else jnp.logical_not(half)

        def grad_scores(b, c):
            r0 = pl.multiple_of(b * 128, 128)
            d_b = jnp.where(mine, dcs[pl.ds(r0, 128), :], 0)
            dp = nt(d_b, vs[...])
            p = p_ref[h, pl.ds(r0, 128), :].astype(F32)
            inner = jnp.sum(p * dp, axis=1, keepdims=True)
            d = p * (dp - inner)
            ds[pl.ds(r0, 128), 128:128 + sp] = d.astype(BF16)
            for jb in range(nb):
                dst[jb * 128:(jb + 1) * 128, pl.ds(pl.multiple_of(r0 + 128, 128), 128)] = \
                    d[:, jb * 128:(jb + 1) * 128].T.astype(BF16)
            return c
        lax.fori_loop(0, nb, grad_scores, 0)

        dct = jnp.where(mine, dcs[...], 0).astype(F32).T.astype(BF16)
        dvt = nn(dct, p_ref[h, :, :])
        if h == 0:
            gt[...] = dvt
        else:
            gt[...] += dvt

        for side in range(2):
            mat = ds if side == 0 else dst
            other = ks if side == 0 else qs
            own = qs if side == 0 else ks
            rel_ref = relk_ref if side == 0 else relq_ref
            g_ref = gk_ref if side == 0 else gq_ref
            blk = iota((sp, 128), 0) >> 7
            lane_sp = iota((sp, 128), 1) & 63
            w = jnp.where(mine, other[...].astype(F32), jnp.where(blk == lane_sp, 1.0, 0.0)).astype(BF16)
            w2 = jnp.concatenate([w, base[...]], axis=1)
            relm = jnp.where(mine, rel_ref[...], 0)
            acc[...] = jnp.zeros_like(acc)

            def rows(b, c):
                r0 = pl.multiple_of(b * 128, 128)
                d_b = mat[pl.ds(r0, 128), 128:128 + sp]
                out = nn(d_b, w2)
                hist = out[:, 128:] + nn(d_b * mx[pl.ds(r0, 128), :], ex[...]) \
                    + nn(d_b * my[pl.ds(r0, 128), :], ey[...])
                before = mat[pl.ds(r0, 128), pl.ds(r0, 128)].astype(F32)
                here = mat[pl.ds(r0, 128), pl.ds(pl.multiple_of(r0 + 128, 128), 128)].astype(F32)
                after = mat[pl.ds(r0, 128), pl.ds(pl.multiple_of(r0 + 256, 128), 128)].astype(F32)
                sums = jnp.where(mine, 0.0, out[:, :128])
                blkno = lane1 & 63
                low = jnp.where(blkno <= b - 2, sums, 0.0) + jnp.where(lane1 <= row1 + 64, before, 0.0) \
                    + jnp.where(lane1 <= row1 - 64, here, 0.0)
                high = jnp.where(blkno >= b + 2, sums, 0.0) + jnp.where(lane1 >= row1 + 63, here, 0.0) \
                    + jnp.where(lane1 >= row1 - 65, after, 0.0)
                low = jnp.sum(low, axis=1, keepdims=True)
                high = jnp.sum(high, axis=1, keepdims=True)
                at = lane1 + row1 + 64
                place = at & 127
                mid = jnp.where(at < 128, lane_pick(before, place),
                                jnp.where(at < 256, lane_pick(here, place), lane_pick(after, place)))
                dn0 = jnp.where(lane1 == 0, low, jnp.where(lane1 == 127, high, mid))
                ax = bc_ref[pl.ds(r0, 128), 0:1] >> 4
                ay = bc_ref[pl.ds(r0, 128), 1:2] >> 4
                c1 = lane1 + ax - 63
                c2 = lane1 + ay - 63
                dn1 = jnp.where((c1 >= 0) & (c1 < 64), lane_pick(hist, c1 & 127), 0.0)
                dn2 = jnp.where((c2 >= 0) & (c2 < 64), lane_pick(hist, (c2 + 64) & 127), 0.0)
                dn = jnp.concatenate([dn0, dn1, dn2], axis=1).astype(BF16)
                g = (out[:, :128] + nn(dn, relm)) * SCALE
                o_b = jnp.where(mine, own[pl.ds(r0, 128), :], 0)
                acc[...] += nn(o_b.astype(F32).T.astype(BF16), dn)
                return c, g
            for b in range(nb):
                _, g = rows(b, 0)
                n = min(128, slots - b * 128)
                at = pl.ds(pl.multiple_of(side * width + pair * 128, 128), 128)
                if h == 0:
                    dqkv_ref[b * 128:b * 128 + n, at] = g[0:n].astype(BF16)
                else:
                    dqkv_ref[b * 128:b * 128 + n, at] = jnp.where(
                        mine, g[0:n].astype(BF16), dqkv_ref[b * 128:b * 128 + n, at])
            if h == 0:
                g_ref[...] = acc[...] * SCALE
            else:
                g_ref[...] += acc[...] * SCALE
    dv = gt[...].T
    dqkv_ref[:, pl.ds(pl.multiple_of(2 * width + pair * 128, 128), 128)] = dv[0:slots, :].astype(BF16)


def attend_backward(qkv, dctx, probs, relk, relq, boxes_col, boxes_row, heads):
    docs, slots, width = qkv.shape
    width = width // 3
    sp = boxes_row.shape[2]
    pairs = heads // 2

    def part(t):
        return pl.BlockSpec((None, slots, 128), lambda d, p: (d, 0, t * pairs + p))
    rel = pl.BlockSpec((3 * BUCKETS, 128), lambda d, p: (0, p))
    grel = pl.BlockSpec((None, 128, 3 * BUCKETS), lambda d, p: (d, p, 0))
    return pl.pallas_call(
        functools.partial(bwd_kernel, slots, sp, width),
        grid=(docs, pairs),
        in_specs=[part(0), part(1), part(2),
                  pl.BlockSpec((None, slots, 128), lambda d, p: (d, 0, p)),
                  pl.BlockSpec((None, 2, sp, sp), lambda d, p: (d, p, 0, 0)),
                  rel, rel,
                  pl.BlockSpec((None, sp, 2), lambda d, p: (d, 0, 0)),
                  pl.BlockSpec((None, 2, sp), lambda d, p: (d, 0, 0))],
        out_specs=[pl.BlockSpec((None, slots, 3 * width), lambda d, p: (d, 0, 0)), grel, grel],
        out_shape=[jax.ShapeDtypeStruct((docs, slots, 3 * width), BF16),
                   jax.ShapeDtypeStruct((docs, width, 3 * BUCKETS), F32),
                   jax.ShapeDtypeStruct((docs, width, 3 * BUCKETS), F32)],
        scratch_shapes=[pltpu.VMEM((sp, 128), BF16)] * 7
        + [pltpu.VMEM((sp, sp), BF16)] * 2 + [pltpu.VMEM((sp, sp + 256), BF16)] * 2
        + [pltpu.VMEM((128, sp), F32), pltpu.VMEM((128, 384), F32)],
        name="attend_backward",
        compiler_params=pltpu.CompilerParams(vmem_limit_bytes=56 << 20),
    )(qkv, qkv, qkv, dctx, probs, relk, relq, boxes_col, boxes_row)


def norm_forward(values_in, gain, shift, model_width):
    row_total, row_square = lax.psum(
        (jnp.sum(values_in, axis=1), jnp.sum(values_in * values_in, axis=1)), "tensor"
    )
    mean_row = row_total / model_width
    scale_row = lax.rsqrt(row_square / model_width - mean_row * mean_row + 1e-05)
    normed = (values_in - mean_row[:, None]) * scale_row[:, None]
    return (normed * gain + shift, normed, scale_row)


def norm_backward(upstream, normed, scale_row, gain, model_width):
    scaled_up = upstream * gain
    first_sum, second_sum = lax.psum(
        (jnp.sum(scaled_up, axis=1), jnp.sum(scaled_up * normed, axis=1)), "tensor"
    )
    centered = (
        scaled_up - first_sum[:, None] / model_width - normed * second_sum[:, None] / model_width
    )
    return scale_row[:, None] * centered


def on_device(
    hidden_in,
    lengths,
    boxes,
    w_qkv,
    w_out,
    w_up,
    w_down,
    rel_keys,
    rel_queries,
    norm_gains,
    norm_shifts,
    out_grad,
):
    doc_count, slot_count, local_width = hidden_in.shape
    row_count = doc_count * slot_count
    model_width = w_qkv.shape[0]
    heads_here = local_width // HEAD_DIM
    rel_k = rel_keys.reshape(3 * BUCKETS, local_width)
    rel_q = rel_queries.reshape(3 * BUCKETS, local_width)
    padded = -(-slot_count // 128) * 128
    boxes_col = jnp.pad(boxes, ((0, 0), (0, padded - slot_count), (0, 0)))
    boxes_row = jnp.swapaxes(boxes_col, 1, 2)
    local_rows = hidden_in.reshape(row_count, local_width)
    full_rows = lax.all_gather(local_rows, "tensor", axis=1, tiled=True)
    weight_qkv = w_qkv.reshape(model_width, 3 * local_width)
    projected = jnp.dot(full_rows, weight_qkv, preferred_element_type=jnp.float32).astype(
        jnp.bfloat16
    )
    projected = projected.reshape(doc_count, slot_count, 3 * local_width)
    context, probs = attend_forward(lengths, projected, rel_k, rel_q, boxes_col, boxes_row, heads_here)
    context_rows = context.reshape(row_count, local_width)
    attn_terms = jnp.dot(context_rows, w_out, preferred_element_type=jnp.float32)
    attn_out = lax.psum_scatter(attn_terms, "tensor", scatter_dimension=1, tiled=True)
    first_sum_in = local_rows.astype(jnp.float32) + attn_out
    normed_first, unit_first, scale_first = norm_forward(
        first_sum_in, norm_gains[0], norm_shifts[0], model_width
    )
    normed_full = lax.all_gather(normed_first.astype(jnp.bfloat16), "tensor", axis=1, tiled=True)
    upper = jnp.dot(normed_full, w_up, preferred_element_type=jnp.float32)
    active = jax.nn.gelu(upper, approximate=False).astype(jnp.bfloat16)
    ffn_out = lax.psum_scatter(
        jnp.dot(active, w_down, preferred_element_type=jnp.float32).astype(jnp.bfloat16),
        "tensor",
        scatter_dimension=1,
        tiled=True,
    ).astype(jnp.float32)
    result, unit_second, scale_second = norm_forward(
        normed_first + ffn_out, norm_gains[1], norm_shifts[1], model_width
    )
    hidden_out = result.astype(jnp.bfloat16).reshape(doc_count, slot_count, local_width)
    upstream = out_grad.reshape(row_count, local_width).astype(jnp.float32)
    gain_second = jnp.sum(upstream * unit_second, axis=0)
    shift_second = jnp.sum(upstream, axis=0)
    grad_second = norm_backward(upstream, unit_second, scale_second, norm_gains[1], model_width)
    ffn_grad_full = lax.all_gather(grad_second.astype(jnp.bfloat16), "tensor", axis=1, tiled=True)
    down_grad = jnp.einsum("rf,rd->fd", active, ffn_grad_full, preferred_element_type=jnp.float32)
    grad_active = jnp.einsum("rd,fd->rf", ffn_grad_full, w_down, preferred_element_type=jnp.float32)
    _, gelu_pull = jax.vjp(lambda entry: jax.nn.gelu(entry, approximate=False), upper)
    grad_upper = gelu_pull(grad_active)[0].astype(jnp.bfloat16)
    up_grad = jnp.einsum("rd,rf->df", normed_full, grad_upper, preferred_element_type=jnp.float32)
    hidden_terms = jnp.einsum("rf,df->rd", grad_upper, w_up, preferred_element_type=jnp.float32)
    grad_hidden = grad_second + lax.psum_scatter(
        hidden_terms.astype(jnp.bfloat16), "tensor", scatter_dimension=1, tiled=True
    ).astype(jnp.float32)
    gain_first = jnp.sum(grad_hidden * unit_first, axis=0)
    shift_first = jnp.sum(grad_hidden, axis=0)
    grad_first = norm_backward(grad_hidden, unit_first, scale_first, norm_gains[0], model_width)
    attn_grad_full = lax.all_gather(grad_first.astype(jnp.bfloat16), "tensor", axis=1, tiled=True)
    out_weight_grad = jnp.einsum(
        "rc,rd->cd", context_rows, attn_grad_full, preferred_element_type=jnp.float32
    )
    grad_context = jnp.einsum(
        "rd,cd->rc", attn_grad_full, w_out, preferred_element_type=jnp.float32
    ).astype(jnp.bfloat16)
    grad_context = grad_context.reshape(doc_count, slot_count, local_width)
    grad_projected, rel_k_sum, rel_q_sum = attend_backward(
        projected, grad_context, probs, rel_k, rel_q, boxes_col, boxes_row, heads_here
    )
    rel_keys_grad = jnp.sum(rel_k_sum, axis=0).T.reshape(3, BUCKETS, local_width)
    rel_queries_grad = jnp.sum(rel_q_sum, axis=0).T.reshape(3, BUCKETS, local_width)
    grad_rows = grad_projected.reshape(row_count, 3 * local_width)
    qkv_grad = jnp.einsum(
        "rd,rc->dc", full_rows, grad_rows, preferred_element_type=jnp.float32
    ).reshape(model_width, 3, local_width)
    input_terms = jnp.einsum("rc,dc->rd", grad_rows, weight_qkv, preferred_element_type=jnp.float32)
    input_grad = grad_first + lax.psum_scatter(
        input_terms.astype(jnp.bfloat16), "tensor", scatter_dimension=1, tiled=True
    ).astype(jnp.float32)
    input_grad = input_grad.astype(jnp.bfloat16).reshape(doc_count, slot_count, local_width)
    (
        qkv_grad,
        out_weight_grad,
        up_grad,
        down_grad,
        rel_keys_grad,
        rel_queries_grad,
        gain_first,
        shift_first,
        gain_second,
        shift_second,
    ) = (
        lax.psum(qkv_grad.astype(jnp.bfloat16), "dp").astype(jnp.float32),
        lax.psum(out_weight_grad.astype(jnp.bfloat16), "dp").astype(jnp.float32),
        lax.psum(up_grad.astype(jnp.bfloat16), "dp").astype(jnp.float32),
        lax.psum(down_grad.astype(jnp.bfloat16), "dp").astype(jnp.float32),
        lax.psum(rel_keys_grad.astype(jnp.bfloat16), "dp").astype(jnp.float32),
        lax.psum(rel_queries_grad.astype(jnp.bfloat16), "dp").astype(jnp.float32),
        lax.psum(gain_first.astype(jnp.bfloat16), "dp").astype(jnp.float32),
        lax.psum(shift_first.astype(jnp.bfloat16), "dp").astype(jnp.float32),
        lax.psum(gain_second.astype(jnp.bfloat16), "dp").astype(jnp.float32),
        lax.psum(shift_second.astype(jnp.bfloat16), "dp").astype(jnp.float32),
    )
    gains_grad = jnp.stack([gain_first, gain_second])
    shifts_grad = jnp.stack([shift_first, shift_second])
    return (
        hidden_out,
        input_grad,
        qkv_grad,
        out_weight_grad,
        up_grad,
        down_grad,
        rel_keys_grad,
        rel_queries_grad,
        gains_grad,
        shifts_grad,
    )


def solution(mesh):
    in_specs = (
        P("dp", None, "tensor"),
        P("dp"),
        P("dp", None, None),
        P(None, None, "tensor"),
        P("tensor", None),
        P(None, "tensor"),
        P("tensor", None),
        P(None, None, "tensor"),
        P(None, None, "tensor"),
        P(None, "tensor"),
        P(None, "tensor"),
        P("dp", None, "tensor"),
    )
    out_specs = (
        P("dp", None, "tensor"),
        P("dp", None, "tensor"),
        P(None, None, "tensor"),
        P("tensor", None),
        P(None, "tensor"),
        P("tensor", None),
        P(None, None, "tensor"),
        P(None, None, "tensor"),
        P(None, "tensor"),
        P(None, "tensor"),
    )
    return jax.shard_map(
        on_device, mesh=mesh, in_specs=in_specs, out_specs=out_specs, check_vma=False
    )
```

```python
import math, functools
import jax, jax.numpy as jnp
from jax import lax
from jax.sharding import PartitionSpec as P
from jax.experimental import pallas as pl
from jax.experimental.pallas import tpu as pltpu

HEAD_DIM = 64
BUCKETS = 128
TEXT = 512
NEG = -1e30
SCALE = 1.0 / math.sqrt(3 * HEAD_DIM)
F32 = jnp.float32
BF16 = jnp.bfloat16


def nt(a, b):
    return lax.dot_general(a, b, (((1,), (1,)), ((), ())), preferred_element_type=F32)


def nn(a, b):
    return lax.dot_general(a, b, (((1,), (0,)), ((), ())), preferred_element_type=F32)


def iota(shape, d):
    return lax.broadcasted_iota(jnp.int32, shape, d)


def lane_pick(table, index):
    return jnp.take_along_axis(table, index, axis=1, mode="promise_in_bounds")


def fwd_kernel(slots, sp, len_ref, q_ref, k_ref, v_ref, relk_ref, relq_ref, bc_ref, br_ref,
               ctx_ref, p_ref, qs, ks, vs, idx, nq, nk, fk):
    pair = pl.program_id(1)
    nb = sp // 128

    @pl.when(pair == 0)
    def _():
        qs[...] = jnp.zeros_like(qs)
        ks[...] = jnp.zeros_like(ks)
        vs[...] = jnp.zeros_like(vs)

        def rows(b, c):
            r0 = pl.multiple_of(b * 128, 128)
            row = iota((128, sp), 0) + r0
            col = iota((128, sp), 1)
            idx[0, pl.ds(r0, 128), :] = jnp.clip(col - row, -64, 63) + 64
            for t in range(2):
                x_i = bc_ref[pl.ds(r0, 128), t:t + 1]
                x_j = br_ref[t:t + 1, :]
                idx[t + 1, pl.ds(r0, 128), :] = jnp.clip((x_j - x_i) >> 4, -64, 63) + 64
            return c
        lax.fori_loop(0, nb, rows, 0)

    qs[0:slots, :] = q_ref[...]
    ks[0:slots, :] = k_ref[...]
    vs[0:slots, :] = v_ref[...]
    place = iota((1, sp), 1)
    length = len_ref[pl.program_id(0)]
    valid = (place < length) | ((place >= TEXT) & (place < slots))
    half = iota((1, 128), 1) < 64

    for h in range(2):
        mine = half if h == 0 else jnp.logical_not(half)
        qm = jnp.where(mine, qs[...], 0)
        km = jnp.where(mine, ks[...], 0)
        nq[...] = nt(qm, relk_ref[...])
        nk[...] = nt(km, relq_ref[...])

        def key_side(b, c):
            r0 = pl.multiple_of(b * 128, 128)
            for ib in range(nb):
                g = None
                for t in range(3):
                    e = lane_pick(nk[pl.ds(r0, 128), t * 128:(t + 1) * 128],
                                  idx[t, pl.ds(r0, 128), ib * 128:(ib + 1) * 128])
                    g = e if g is None else g + e
                fk[ib * 128:(ib + 1) * 128, pl.ds(r0, 128)] = g.T
            return c
        lax.fori_loop(0, nb, key_side, 0)

        def query_side(b, c):
            r0 = pl.multiple_of(b * 128, 128)
            q_b = jnp.where(mine, qs[pl.ds(r0, 128), :], 0)
            s = nt(q_b, ks[...]) + fk[pl.ds(r0, 128), :]
            parts = []
            for jb in range(nb):
                g = s[:, jb * 128:(jb + 1) * 128]
                for t in range(3):
                    g = g + lane_pick(nq[pl.ds(r0, 128), t * 128:(t + 1) * 128],
                                      idx[t, pl.ds(r0, 128), jb * 128:(jb + 1) * 128])
                parts.append(g)
            s = jnp.concatenate(parts, axis=1)
            s = jnp.where(valid, s * SCALE, NEG)
            m = jnp.max(s, axis=1, keepdims=True)
            e = jnp.exp(s - m)
            tot = jnp.sum(e, axis=1, keepdims=True)
            p = (e * (1.0 / tot)).astype(BF16)
            p_ref[h, pl.ds(r0, 128), :] = p
            c_b = nn(p, vs[...])
            fk[pl.ds(r0, 128), 0:128] = c_b
            return c
        lax.fori_loop(0, nb, query_side, 0)
        if h == 0:
            ctx_ref[...] = fk[0:slots, 0:128].astype(BF16)
        else:
            ctx_ref[...] = jnp.where(mine, fk[0:slots, 0:128].astype(BF16), ctx_ref[...])


def attend_forward(lengths, qkv, relk, relq, boxes_col, boxes_row, heads):
    docs, slots, width = qkv.shape
    width = width // 3
    sp = boxes_row.shape[2]
    pairs = heads // 2

    def part(t):
        return pl.BlockSpec((None, slots, 128), lambda d, p, ln: (d, 0, t * pairs + p))
    grid_spec = pltpu.PrefetchScalarGridSpec(
        num_scalar_prefetch=1, grid=(docs, pairs),
        in_specs=[part(0), part(1), part(2),
                  pl.BlockSpec((3 * BUCKETS, 128), lambda d, p, ln: (0, p)),
                  pl.BlockSpec((3 * BUCKETS, 128), lambda d, p, ln: (0, p)),
                  pl.BlockSpec((None, sp, 2), lambda d, p, ln: (d, 0, 0)),
                  pl.BlockSpec((None, 2, sp), lambda d, p, ln: (d, 0, 0))],
        out_specs=[pl.BlockSpec((None, slots, 128), lambda d, p, ln: (d, 0, p)),
                   pl.BlockSpec((None, 2, sp, sp), lambda d, p, ln: (d, p, 0, 0))],
        scratch_shapes=[pltpu.VMEM((sp, 128), BF16)] * 3
        + [pltpu.VMEM((3, sp, sp), jnp.int32), pltpu.VMEM((sp, 384), F32), pltpu.VMEM((sp, 384), F32),
           pltpu.VMEM((sp, sp), F32)])
    return pl.pallas_call(
        functools.partial(fwd_kernel, slots, sp),
        out_shape=[jax.ShapeDtypeStruct((docs, slots, width), BF16),
                   jax.ShapeDtypeStruct((docs, heads, sp, sp), BF16)],
        grid_spec=grid_spec, name="attend_forward",
        compiler_params=pltpu.CompilerParams(vmem_limit_bytes=56 << 20),
    )(lengths, qkv, qkv, qkv, relk, relq, boxes_col, boxes_row)


def bwd_kernel(slots, sp, width, q_ref, k_ref, v_ref, dc_ref, p_ref, relk_ref, relq_ref, bc_ref, br_ref,
               dqkv_ref, gk_ref, gq_ref,
               qs, ks, vs, dcs, base, ex, ey, mx, my, ds, dst, gt, acc):
    pair = pl.program_id(1)
    nb = sp // 128

    @pl.when(pair == 0)
    def _():
        for r in (qs, ks, vs, dcs, ds, dst):
            r[...] = jnp.zeros_like(r)
        lane = iota((sp, 128), 1)
        ax = bc_ref[:, 0:1] >> 4
        ay = bc_ref[:, 1:2] >> 4
        left = lane < 64
        c = lane & 63
        a = jnp.where(left, ax, ay)
        one = jnp.where(c == a, 1.0, 0.0)
        nxt = jnp.where(c == a + 1, 1.0, 0.0)
        base[...] = one.astype(BF16)
        e = nxt - one
        ex[...] = jnp.where(left, e, 0.0).astype(BF16)
        ey[...] = jnp.where(left, 0.0, e).astype(BF16)

        def rows(b, c):
            r0 = pl.multiple_of(b * 128, 128)
            for t, m in ((0, mx), (1, my)):
                r_i = bc_ref[pl.ds(r0, 128), t:t + 1] & 15
                r_j = br_ref[t:t + 1, :] & 15
                m[pl.ds(r0, 128), :] = jnp.where(r_j >= r_i, 1.0, 0.0).astype(BF16)
            return c
        lax.fori_loop(0, nb, rows, 0)

    qs[0:slots, :] = q_ref[...]
    ks[0:slots, :] = k_ref[...]
    vs[0:slots, :] = v_ref[...]
    dcs[0:slots, :] = dc_ref[...]
    half = iota((1, 128), 1) < 64
    lane1 = iota((128, 128), 1)
    row1 = iota((128, 128), 0)

    for h in range(2):
        mine = half if h == 0 else jnp.logical_not(half)

        def grad_scores(b, c):
            r0 = pl.multiple_of(b * 128, 128)
            d_b = jnp.where(mine, dcs[pl.ds(r0, 128), :], 0)
            dp = nt(d_b, vs[...])
            p = p_ref[h, pl.ds(r0, 128), :].astype(F32)
            inner = jnp.sum(p * dp, axis=1, keepdims=True)
            d = p * (dp - inner)
            ds[pl.ds(r0, 128), 128:128 + sp] = d.astype(BF16)
            for jb in range(nb):
                dst[jb * 128:(jb + 1) * 128, pl.ds(pl.multiple_of(r0 + 128, 128), 128)] = \
                    d[:, jb * 128:(jb + 1) * 128].T.astype(BF16)
            return c
        lax.fori_loop(0, nb, grad_scores, 0)

        dct = jnp.where(mine, dcs[...], 0).astype(F32).T.astype(BF16)
        dvt = nn(dct, p_ref[h, :, :])
        if h == 0:
            gt[...] = dvt
        else:
            gt[...] += dvt

        for side in range(2):
            mat = ds if side == 0 else dst
            other = ks if side == 0 else qs
            own = qs if side == 0 else ks
            rel_ref = relk_ref if side == 0 else relq_ref
            g_ref = gk_ref if side == 0 else gq_ref
            blk = iota((sp, 128), 0) >> 7
            lane_sp = iota((sp, 128), 1) & 63
            w = jnp.where(mine, other[...].astype(F32), jnp.where(blk == lane_sp, 1.0, 0.0)).astype(BF16)
            w2 = jnp.concatenate([w, base[...]], axis=1)
            relm = jnp.where(mine, rel_ref[...], 0)
            acc[...] = jnp.zeros_like(acc)

            def rows(b, c):
                r0 = pl.multiple_of(b * 128, 128)
                d_b = mat[pl.ds(r0, 128), 128:128 + sp]
                out = nn(d_b, w2)
                hist = out[:, 128:] + nn(d_b * mx[pl.ds(r0, 128), :], ex[...]) \
                    + nn(d_b * my[pl.ds(r0, 128), :], ey[...])
                before = mat[pl.ds(r0, 128), pl.ds(r0, 128)].astype(F32)
                here = mat[pl.ds(r0, 128), pl.ds(pl.multiple_of(r0 + 128, 128), 128)].astype(F32)
                after = mat[pl.ds(r0, 128), pl.ds(pl.multiple_of(r0 + 256, 128), 128)].astype(F32)
                sums = jnp.where(mine, 0.0, out[:, :128])
                blkno = lane1 & 63
                low = jnp.where(blkno <= b - 2, sums, 0.0) + jnp.where(lane1 <= row1 + 64, before, 0.0) \
                    + jnp.where(lane1 <= row1 - 64, here, 0.0)
                high = jnp.where(blkno >= b + 2, sums, 0.0) + jnp.where(lane1 >= row1 + 63, here, 0.0) \
                    + jnp.where(lane1 >= row1 - 65, after, 0.0)
                low = jnp.sum(low, axis=1, keepdims=True)
                high = jnp.sum(high, axis=1, keepdims=True)
                at = lane1 + row1 + 64
                place = at & 127
                mid = jnp.where(at < 128, lane_pick(before, place),
                                jnp.where(at < 256, lane_pick(here, place), lane_pick(after, place)))
                dn0 = jnp.where(lane1 == 0, low, jnp.where(lane1 == 127, high, mid))
                ax = bc_ref[pl.ds(r0, 128), 0:1] >> 4
                ay = bc_ref[pl.ds(r0, 128), 1:2] >> 4
                c1 = lane1 + ax - 63
                c2 = lane1 + ay - 63
                dn1 = jnp.where((c1 >= 0) & (c1 < 64), lane_pick(hist, c1 & 127), 0.0)
                dn2 = jnp.where((c2 >= 0) & (c2 < 64), lane_pick(hist, (c2 + 64) & 127), 0.0)
                dn = jnp.concatenate([dn0, dn1, dn2], axis=1).astype(BF16)
                g = (out[:, :128] + nn(dn, relm)) * SCALE
                o_b = jnp.where(mine, own[pl.ds(r0, 128), :], 0)
                acc[...] += nn(o_b.astype(F32).T.astype(BF16), dn)
                return c, g
            for b in range(nb):
                _, g = rows(b, 0)
                n = min(128, slots - b * 128)
                at = pl.ds(pl.multiple_of(side * width + pair * 128, 128), 128)
                if h == 0:
                    dqkv_ref[b * 128:b * 128 + n, at] = g[0:n].astype(BF16)
                else:
                    dqkv_ref[b * 128:b * 128 + n, at] = jnp.where(
                        mine, g[0:n].astype(BF16), dqkv_ref[b * 128:b * 128 + n, at])
            turned = acc[...].T * SCALE
            if h == 0:
                g_ref[...] = turned
            else:
                g_ref[...] += turned
    dv = gt[...].T
    dqkv_ref[:, pl.ds(pl.multiple_of(2 * width + pair * 128, 128), 128)] = dv[0:slots, :].astype(BF16)


def attend_backward(qkv, dctx, probs, relk, relq, boxes_col, boxes_row, heads):
    docs, slots, width = qkv.shape
    width = width // 3
    sp = boxes_row.shape[2]
    pairs = heads // 2

    def part(t):
        return pl.BlockSpec((None, slots, 128), lambda d, p: (d, 0, t * pairs + p))
    rel = pl.BlockSpec((3 * BUCKETS, 128), lambda d, p: (0, p))
    grel = pl.BlockSpec((None, 3 * BUCKETS, 128), lambda d, p: (d, 0, p))
    return pl.pallas_call(
        functools.partial(bwd_kernel, slots, sp, width),
        grid=(docs, pairs),
        in_specs=[part(0), part(1), part(2),
                  pl.BlockSpec((None, slots, 128), lambda d, p: (d, 0, p)),
                  pl.BlockSpec((None, 2, sp, sp), lambda d, p: (d, p, 0, 0)),
                  rel, rel,
                  pl.BlockSpec((None, sp, 2), lambda d, p: (d, 0, 0)),
                  pl.BlockSpec((None, 2, sp), lambda d, p: (d, 0, 0))],
        out_specs=[pl.BlockSpec((None, slots, 3 * width), lambda d, p: (d, 0, 0)), grel, grel],
        out_shape=[jax.ShapeDtypeStruct((docs, slots, 3 * width), BF16),
                   jax.ShapeDtypeStruct((docs, 3 * BUCKETS, width), F32),
                   jax.ShapeDtypeStruct((docs, 3 * BUCKETS, width), F32)],
        scratch_shapes=[pltpu.VMEM((sp, 128), BF16)] * 7
        + [pltpu.VMEM((sp, sp), BF16)] * 2 + [pltpu.VMEM((sp, sp + 256), BF16)] * 2
        + [pltpu.VMEM((128, sp), F32), pltpu.VMEM((128, 384), F32)],
        name="attend_backward",
        compiler_params=pltpu.CompilerParams(vmem_limit_bytes=56 << 20),
    )(qkv, qkv, qkv, dctx, probs, relk, relq, boxes_col, boxes_row)


EPSILON = 1e-05
ROOT_HALF = math.sqrt(0.5)
PDF_SCALE = 1.0 / math.sqrt(2.0 * math.pi)


def dot_nt(a, b):
    return lax.dot_general(a, b, (((1,), (1,)), ((), ())), preferred_element_type=F32)


def dot_tn(a, b):
    return lax.dot_general(a, b, (((0,), (0,)), ((), ())), preferred_element_type=F32)


def norm_rows(values, gain, shift):
    mean = jnp.mean(values, axis=1, keepdims=True)
    scale = lax.rsqrt(jnp.mean(values * values, axis=1, keepdims=True) - mean * mean + EPSILON)
    unit = (values - mean) * scale
    return unit * gain + shift, unit, scale


def norm_pull(upstream, unit, scale, gain):
    scaled = upstream * gain
    first = jnp.mean(scaled, axis=1, keepdims=True)
    second = jnp.mean(scaled * unit, axis=1, keepdims=True)
    return scale * (scaled - first - unit * second)


def exchange_sum(parts, bits, size):
    place = lax.axis_index("dp")

    def swap(array, bit):
        return lax.ppermute(array, "dp", [(i, i ^ bit) for i in range(size)])

    def fold(array, bit):
        half = array.shape[0] // 2
        low = (place & bit) == 0
        keep = jnp.where(low, array[:half], array[half:])
        send = jnp.where(low, array[half:], array[:half])
        return (keep.astype(F32) + swap(send, bit).astype(F32)).astype(BF16)

    def unfold(array, bit):
        low = (place & bit) == 0
        other = swap(array, bit)
        return jnp.concatenate([jnp.where(low, array, other), jnp.where(low, other, array)], axis=0)

    arrays = [a for a, _ in parts]
    for step in range(len(bits)):
        arrays = [fold(a, order[step]) for a, (_, order) in zip(arrays, parts)]
    for step in reversed(range(len(bits))):
        arrays = [unfold(a, order[step]) for a, (_, order) in zip(arrays, parts)]
    return arrays


def sum_over_documents(table, size):
    if size != 16:
        return lax.psum(table, "dp")
    rows = table.shape[0]
    grain = 256
    pieces = 4
    step = -(-rows // (pieces * grain)) * grain
    padded = jnp.pad(table, ((0, pieces * step - rows), (0, 0)))
    orders = ((1, 2, 4, 8), (1, 4, 8, 2))
    parts = [(padded[i * step:(i + 1) * step], orders[i % 2]) for i in range(pieces)]
    return jnp.concatenate(exchange_sum(parts, orders[0], size), axis=0)[:rows]


def on_device(
    documents,
    shards,
    hidden_in,
    lengths,
    boxes,
    w_qkv,
    w_out,
    w_up,
    w_down,
    rel_keys,
    rel_queries,
    norm_gains,
    norm_shifts,
    out_grad,
):
    doc_count, slot_count, width = hidden_in.shape
    row_count = doc_count * slot_count
    model_width = w_qkv.shape[0]
    heads_here = width // HEAD_DIM
    me = lax.axis_index("tensor")
    pair = [(0, 1), (1, 0)]

    def join(array, axis):
        if shards != 2:
            return lax.all_gather(array, "tensor", axis=axis, tiled=True)
        other = lax.ppermute(array, "tensor", pair)
        first = me == 0
        return jnp.concatenate(
            [jnp.where(first, array, other), jnp.where(first, other, array)], axis=axis)

    def total(partial):
        if shards != 2:
            return lax.psum(partial, "tensor").astype(F32)
        return partial.astype(F32) + lax.ppermute(partial, "tensor", pair).astype(F32)

    def own(array):
        return lax.dynamic_slice_in_dim(array, me * width, width, axis=array.ndim - 1)

    def own_total(partial):
        if shards != 2:
            return lax.psum_scatter(partial, "tensor", scatter_dimension=1, tiled=True).astype(F32)
        send = lax.dynamic_slice_in_dim(partial, (1 - me) * width, width, axis=1)
        return own(partial).astype(F32) + lax.ppermute(send, "tensor", pair).astype(F32)

    rel_k = rel_keys.reshape(3 * BUCKETS, width)
    rel_q = rel_queries.reshape(3 * BUCKETS, width)
    padded = -(-slot_count // 128) * 128
    boxes_col = jnp.pad(boxes, ((0, 0), (0, padded - slot_count), (0, 0)))
    boxes_row = jnp.swapaxes(boxes_col, 1, 2)

    rows = join(hidden_in.reshape(row_count, width), 1)
    weight_qkv = w_qkv.reshape(model_width, 3 * width)
    projected = jnp.dot(rows, weight_qkv, preferred_element_type=F32).astype(BF16)
    norms = join(jnp.concatenate([norm_gains, norm_shifts], axis=0), 1)
    upstream = join(out_grad.reshape(row_count, width), 1)
    out_whole = join(w_out, 0)
    projected = projected.reshape(doc_count, slot_count, 3 * width)
    context, probs = attend_forward(lengths, projected, rel_k, rel_q, boxes_col, boxes_row, heads_here)
    context = context.reshape(row_count, width)

    attn = jnp.dot(join(context, 1), out_whole, preferred_element_type=F32)
    h1, unit_first, scale_first = norm_rows(rows.astype(F32) + attn, norms[0:1], norms[2:3])
    h1_low = h1.astype(BF16)
    upper = jnp.dot(h1_low, w_up, preferred_element_type=F32)
    chance = 0.5 * (1.0 + lax.erf(upper * ROOT_HALF))
    active = (upper * chance).astype(BF16)
    slope = (chance + upper * (PDF_SCALE * jnp.exp(-0.5 * upper * upper))).astype(BF16)
    ffn = total(jnp.dot(active, w_down, preferred_element_type=F32).astype(BF16))
    result, unit_second, scale_second = norm_rows(h1 + ffn, norms[1:2], norms[3:4])
    hidden_out = own(result.astype(BF16)).reshape(doc_count, slot_count, width)

    upstream = upstream.astype(F32)
    grad_second = norm_pull(upstream, unit_second, scale_second, norms[1:2])
    ffn_grad = grad_second.astype(BF16)
    grad_upper = (dot_nt(ffn_grad, w_down) * slope.astype(F32)).astype(BF16)
    hidden_part = dot_nt(grad_upper, w_up).astype(BF16)
    units = w_up.shape[1]
    down_grad = dot_tn(active, ffn_grad).astype(BF16)
    early = documents == 16 and units % model_width == 0
    if early:
        ffn_table = jnp.concatenate([down_grad] + [
            dot_tn(h1_low, grad_upper[:, t:t + model_width]).astype(BF16)
            for t in range(0, units, model_width)], axis=0)
        ffn_shard = lax.psum_scatter(ffn_table, "dp", scatter_dimension=0, tiled=True)
    else:
        up_grad = dot_tn(h1_low, grad_upper).astype(BF16)
        down_grad, up_grad = lax.psum((down_grad, up_grad), "dp")
    grad_hidden = grad_second + total(hidden_part)
    grad_first = norm_pull(grad_hidden, unit_first, scale_first, norms[0:1])
    attn_grad = grad_first.astype(BF16)
    norm_grads = own(jnp.stack([
        jnp.sum(grad_hidden * unit_first, axis=0),
        jnp.sum(upstream * unit_second, axis=0),
        jnp.sum(grad_hidden, axis=0),
        jnp.sum(upstream, axis=0)]))

    out_weight_grad = dot_tn(context, attn_grad)
    grad_context = dot_nt(attn_grad, w_out).astype(BF16).reshape(doc_count, slot_count, width)
    grad_projected, rel_k_sum, rel_q_sum = attend_backward(
        projected, grad_context, probs, rel_k, rel_q, boxes_col, boxes_row, heads_here
    )
    if early:
        grad_projected, ffn_shard = lax.optimization_barrier((grad_projected, ffn_shard))
        ffn_table = lax.all_gather(ffn_shard, "dp", axis=0, tiled=True)
        down_grad = ffn_table[:units]
        up_grad = jnp.concatenate([
            ffn_table[units + t:units + t + model_width] for t in range(0, units, model_width)], axis=1)
    grad_rows = grad_projected.reshape(row_count, 3 * width)
    input_part = dot_nt(grad_rows, weight_qkv).astype(BF16)
    input_grad = own(grad_first) + own_total(input_part)
    input_grad = input_grad.astype(BF16).reshape(doc_count, slot_count, width)
    qkv_grads = [dot_tn(rows, grad_rows[:, t * width:(t + 1) * width]) for t in range(3)]
    pieces = qkv_grads + [jnp.sum(rel_k_sum, axis=0), jnp.sum(rel_q_sum, axis=0)]
    pieces += [out_weight_grad[:, t * width:(t + 1) * width] for t in range(shards)]
    pieces += [norm_grads]
    table = sum_over_documents(jnp.concatenate([p.astype(BF16) for p in pieces], axis=0), documents)
    table = table.astype(F32)
    found = []
    at = 0
    for p in pieces:
        found.append(table[at:at + p.shape[0]])
        at += p.shape[0]
    qkv_grad = jnp.stack(found[0:3], axis=1)
    rel_keys_grad = found[3].reshape(3, BUCKETS, width)
    rel_queries_grad = found[4].reshape(3, BUCKETS, width)
    out_weight_grad = jnp.concatenate(found[5:5 + shards], axis=1)
    norm_grads = found[5 + shards]
    return (
        hidden_out,
        input_grad,
        qkv_grad,
        out_weight_grad,
        up_grad.astype(F32),
        down_grad.astype(F32),
        rel_keys_grad,
        rel_queries_grad,
        norm_grads[0:2],
        norm_grads[2:4],
    )


def solution(mesh):
    in_specs = (
        P("dp", None, "tensor"),
        P("dp"),
        P("dp", None, None),
        P(None, None, "tensor"),
        P("tensor", None),
        P(None, "tensor"),
        P("tensor", None),
        P(None, None, "tensor"),
        P(None, None, "tensor"),
        P(None, "tensor"),
        P(None, "tensor"),
        P("dp", None, "tensor"),
    )
    out_specs = (
        P("dp", None, "tensor"),
        P("dp", None, "tensor"),
        P(None, None, "tensor"),
        P("tensor", None),
        P(None, "tensor"),
        P("tensor", None),
        P(None, None, "tensor"),
        P(None, None, "tensor"),
        P(None, "tensor"),
        P(None, "tensor"),
    )
    body = functools.partial(on_device, mesh.shape["dp"], mesh.shape["tensor"])
    return jax.shard_map(body, mesh=mesh, in_specs=in_specs, out_specs=out_specs, check_vma=False)
```

```python
import math, functools
import jax, jax.numpy as jnp
from jax import lax
from jax.sharding import PartitionSpec as P
from jax.experimental import pallas as pl
from jax.experimental.pallas import tpu as pltpu

HEAD_DIM = 64
BUCKETS = 128
TEXT = 512
NEG = -1e30
SCALE = 1.0 / math.sqrt(3 * HEAD_DIM)
F32 = jnp.float32
BF16 = jnp.bfloat16


def nt(a, b):
    return lax.dot_general(a, b, (((1,), (1,)), ((), ())), preferred_element_type=F32)


def nn(a, b):
    return lax.dot_general(a, b, (((1,), (0,)), ((), ())), preferred_element_type=F32)


def iota(shape, d):
    return lax.broadcasted_iota(jnp.int32, shape, d)


def lane_pick(table, index):
    return jnp.take_along_axis(table, index, axis=1, mode="promise_in_bounds")


def fwd_kernel(slots, sp, len_ref, q_ref, k_ref, v_ref, relk_ref, relq_ref, bc_ref, br_ref,
               ctx_ref, p_ref, qs, ks, vs, idx, nq, nk, fk):
    pair = pl.program_id(1)
    nb = sp // 128

    @pl.when(pair == 0)
    def _():
        qs[...] = jnp.zeros_like(qs)
        ks[...] = jnp.zeros_like(ks)
        vs[...] = jnp.zeros_like(vs)

        def rows(b, c):
            r0 = pl.multiple_of(b * 128, 128)
            row = iota((128, sp), 0) + r0
            col = iota((128, sp), 1)
            idx[0, pl.ds(r0, 128), :] = jnp.clip(col - row, -64, 63) + 64
            for t in range(2):
                x_i = bc_ref[pl.ds(r0, 128), t:t + 1]
                x_j = br_ref[t:t + 1, :]
                idx[t + 1, pl.ds(r0, 128), :] = jnp.clip((x_j - x_i) >> 4, -64, 63) + 64
            return c
        lax.fori_loop(0, nb, rows, 0)

    qs[0:slots, :] = q_ref[...]
    ks[0:slots, :] = k_ref[...]
    vs[0:slots, :] = v_ref[...]
    place = iota((1, sp), 1)
    length = len_ref[pl.program_id(0)]
    valid = (place < length) | ((place >= TEXT) & (place < slots))
    half = iota((1, 128), 1) < 64

    for h in range(2):
        mine = half if h == 0 else jnp.logical_not(half)
        qm = jnp.where(mine, qs[...], 0)
        km = jnp.where(mine, ks[...], 0)
        nq[...] = nt(qm, relk_ref[...])
        nk[...] = nt(km, relq_ref[...])

        def key_side(b, c):
            r0 = pl.multiple_of(b * 128, 128)
            for ib in range(nb):
                g = None
                for t in range(3):
                    e = lane_pick(nk[pl.ds(r0, 128), t * 128:(t + 1) * 128],
                                  idx[t, pl.ds(r0, 128), ib * 128:(ib + 1) * 128])
                    g = e if g is None else g + e
                fk[ib * 128:(ib + 1) * 128, pl.ds(r0, 128)] = g.T
            return c
        lax.fori_loop(0, nb, key_side, 0)

        def query_side(b, c):
            r0 = pl.multiple_of(b * 128, 128)
            q_b = jnp.where(mine, qs[pl.ds(r0, 128), :], 0)
            s = nt(q_b, ks[...]) + fk[pl.ds(r0, 128), :]
            parts = []
            for jb in range(nb):
                g = s[:, jb * 128:(jb + 1) * 128]
                for t in range(3):
                    g = g + lane_pick(nq[pl.ds(r0, 128), t * 128:(t + 1) * 128],
                                      idx[t, pl.ds(r0, 128), jb * 128:(jb + 1) * 128])
                parts.append(g)
            s = jnp.concatenate(parts, axis=1)
            s = jnp.where(valid, s * SCALE, NEG)
            m = jnp.max(s, axis=1, keepdims=True)
            e = jnp.exp(s - m)
            tot = jnp.sum(e, axis=1, keepdims=True)
            p = (e * (1.0 / tot)).astype(BF16)
            p_ref[h, pl.ds(r0, 128), :] = p
            c_b = nn(p, vs[...])
            fk[pl.ds(r0, 128), 0:128] = c_b
            return c
        lax.fori_loop(0, nb, query_side, 0)
        if h == 0:
            ctx_ref[...] = fk[0:slots, 0:128].astype(BF16)
        else:
            ctx_ref[...] = jnp.where(mine, fk[0:slots, 0:128].astype(BF16), ctx_ref[...])


def attend_forward(lengths, qkv, relk, relq, boxes_col, boxes_row, heads):
    docs, slots, width = qkv.shape
    width = width // 3
    sp = boxes_row.shape[2]
    pairs = heads // 2

    def part(t):
        return pl.BlockSpec((None, slots, 128), lambda d, p, ln: (d, 0, t * pairs + p))
    grid_spec = pltpu.PrefetchScalarGridSpec(
        num_scalar_prefetch=1, grid=(docs, pairs),
        in_specs=[part(0), part(1), part(2),
                  pl.BlockSpec((3 * BUCKETS, 128), lambda d, p, ln: (0, p)),
                  pl.BlockSpec((3 * BUCKETS, 128), lambda d, p, ln: (0, p)),
                  pl.BlockSpec((None, sp, 2), lambda d, p, ln: (d, 0, 0)),
                  pl.BlockSpec((None, 2, sp), lambda d, p, ln: (d, 0, 0))],
        out_specs=[pl.BlockSpec((None, slots, 128), lambda d, p, ln: (d, 0, p)),
                   pl.BlockSpec((None, 2, sp, sp), lambda d, p, ln: (d, p, 0, 0))],
        scratch_shapes=[pltpu.VMEM((sp, 128), BF16)] * 3
        + [pltpu.VMEM((3, sp, sp), jnp.int32), pltpu.VMEM((sp, 384), F32), pltpu.VMEM((sp, 384), F32),
           pltpu.VMEM((sp, sp), F32)])
    return pl.pallas_call(
        functools.partial(fwd_kernel, slots, sp),
        out_shape=[jax.ShapeDtypeStruct((docs, slots, width), BF16),
                   jax.ShapeDtypeStruct((docs, heads, sp, sp), BF16)],
        grid_spec=grid_spec, name="attend_forward",
        compiler_params=pltpu.CompilerParams(vmem_limit_bytes=56 << 20),
    )(lengths, qkv, qkv, qkv, relk, relq, boxes_col, boxes_row)


def bwd_kernel(slots, sp, width, q_ref, k_ref, v_ref, dc_ref, p_ref, relk_ref, relq_ref, bc_ref, br_ref,
               dqkv_ref, gk_ref, gq_ref,
               qs, ks, vs, dcs, base, ex, ey, mx, my, ds, dst, gt, acc):
    pair = pl.program_id(1)
    nb = sp // 128

    @pl.when(pair == 0)
    def _():
        for r in (qs, ks, vs, dcs, ds, dst):
            r[...] = jnp.zeros_like(r)
        lane = iota((sp, 128), 1)
        ax = bc_ref[:, 0:1] >> 4
        ay = bc_ref[:, 1:2] >> 4
        left = lane < 64
        c = lane & 63
        a = jnp.where(left, ax, ay)
        one = jnp.where(c == a, 1.0, 0.0)
        nxt = jnp.where(c == a + 1, 1.0, 0.0)
        base[...] = one.astype(BF16)
        e = nxt - one
        ex[...] = jnp.where(left, e, 0.0).astype(BF16)
        ey[...] = jnp.where(left, 0.0, e).astype(BF16)

        def rows(b, c):
            r0 = pl.multiple_of(b * 128, 128)
            for t, m in ((0, mx), (1, my)):
                r_i = bc_ref[pl.ds(r0, 128), t:t + 1] & 15
                r_j = br_ref[t:t + 1, :] & 15
                m[pl.ds(r0, 128), :] = jnp.where(r_j >= r_i, 1.0, 0.0).astype(BF16)
            return c
        lax.fori_loop(0, nb, rows, 0)

    qs[0:slots, :] = q_ref[...]
    ks[0:slots, :] = k_ref[...]
    vs[0:slots, :] = v_ref[...]
    dcs[0:slots, :] = dc_ref[...]
    half = iota((1, 128), 1) < 64
    lane1 = iota((128, 128), 1)
    row1 = iota((128, 128), 0)

    for h in range(2):
        mine = half if h == 0 else jnp.logical_not(half)

        def grad_scores(b, c):
            r0 = pl.multiple_of(b * 128, 128)
            d_b = jnp.where(mine, dcs[pl.ds(r0, 128), :], 0)
            dp = nt(d_b, vs[...])
            p = p_ref[h, pl.ds(r0, 128), :].astype(F32)
            inner = jnp.sum(p * dp, axis=1, keepdims=True)
            d = p * (dp - inner)
            ds[pl.ds(r0, 128), 128:128 + sp] = d.astype(BF16)
            for jb in range(nb):
                dst[jb * 128:(jb + 1) * 128, pl.ds(pl.multiple_of(r0 + 128, 128), 128)] = \
                    d[:, jb * 128:(jb + 1) * 128].T.astype(BF16)
            return c
        lax.fori_loop(0, nb, grad_scores, 0)

        dct = jnp.where(mine, dcs[...], 0).astype(F32).T.astype(BF16)
        dvt = nn(dct, p_ref[h, :, :])
        if h == 0:
            gt[...] = dvt
        else:
            gt[...] += dvt

        for side in range(2):
            mat = ds if side == 0 else dst
            other = ks if side == 0 else qs
            own = qs if side == 0 else ks
            rel_ref = relk_ref if side == 0 else relq_ref
            g_ref = gk_ref if side == 0 else gq_ref
            blk = iota((sp, 128), 0) >> 7
            lane_sp = iota((sp, 128), 1) & 63
            w = jnp.where(mine, other[...].astype(F32), jnp.where(blk == lane_sp, 1.0, 0.0)).astype(BF16)
            w2 = jnp.concatenate([w, base[...]], axis=1)
            relm = jnp.where(mine, rel_ref[...], 0)
            acc[...] = jnp.zeros_like(acc)

            def rows(b, c):
                r0 = pl.multiple_of(b * 128, 128)
                d_b = mat[pl.ds(r0, 128), 128:128 + sp]
                out = nn(d_b, w2)
                hist = out[:, 128:] + nn(d_b * mx[pl.ds(r0, 128), :], ex[...]) \
                    + nn(d_b * my[pl.ds(r0, 128), :], ey[...])
                before = mat[pl.ds(r0, 128), pl.ds(r0, 128)].astype(F32)
                here = mat[pl.ds(r0, 128), pl.ds(pl.multiple_of(r0 + 128, 128), 128)].astype(F32)
                after = mat[pl.ds(r0, 128), pl.ds(pl.multiple_of(r0 + 256, 128), 128)].astype(F32)
                sums = jnp.where(mine, 0.0, out[:, :128])
                blkno = lane1 & 63
                low = jnp.where(blkno <= b - 2, sums, 0.0) + jnp.where(lane1 <= row1 + 64, before, 0.0) \
                    + jnp.where(lane1 <= row1 - 64, here, 0.0)
                high = jnp.where(blkno >= b + 2, sums, 0.0) + jnp.where(lane1 >= row1 + 63, here, 0.0) \
                    + jnp.where(lane1 >= row1 - 65, after, 0.0)
                low = jnp.sum(low, axis=1, keepdims=True)
                high = jnp.sum(high, axis=1, keepdims=True)
                at = lane1 + row1 + 64
                place = at & 127
                mid = jnp.where(at < 128, lane_pick(before, place),
                                jnp.where(at < 256, lane_pick(here, place), lane_pick(after, place)))
                dn0 = jnp.where(lane1 == 0, low, jnp.where(lane1 == 127, high, mid))
                ax = bc_ref[pl.ds(r0, 128), 0:1] >> 4
                ay = bc_ref[pl.ds(r0, 128), 1:2] >> 4
                c1 = lane1 + ax - 63
                c2 = lane1 + ay - 63
                dn1 = jnp.where((c1 >= 0) & (c1 < 64), lane_pick(hist, c1 & 127), 0.0)
                dn2 = jnp.where((c2 >= 0) & (c2 < 64), lane_pick(hist, (c2 + 64) & 127), 0.0)
                dn = jnp.concatenate([dn0, dn1, dn2], axis=1).astype(BF16)
                g = (out[:, :128] + nn(dn, relm)) * SCALE
                o_b = jnp.where(mine, own[pl.ds(r0, 128), :], 0)
                acc[...] += nn(o_b.astype(F32).T.astype(BF16), dn)
                return c, g
            for b in range(nb):
                _, g = rows(b, 0)
                n = min(128, slots - b * 128)
                at = pl.ds(pl.multiple_of(side * width + pair * 128, 128), 128)
                if h == 0:
                    dqkv_ref[b * 128:b * 128 + n, at] = g[0:n].astype(BF16)
                else:
                    dqkv_ref[b * 128:b * 128 + n, at] = jnp.where(
                        mine, g[0:n].astype(BF16), dqkv_ref[b * 128:b * 128 + n, at])
            turned = acc[...].T * SCALE
            if h == 0:
                g_ref[...] = turned
            else:
                g_ref[...] += turned
    dv = gt[...].T
    dqkv_ref[:, pl.ds(pl.multiple_of(2 * width + pair * 128, 128), 128)] = dv[0:slots, :].astype(BF16)


def attend_backward(qkv, dctx, probs, relk, relq, boxes_col, boxes_row, heads):
    docs, slots, width = qkv.shape
    width = width // 3
    sp = boxes_row.shape[2]
    pairs = heads // 2

    def part(t):
        return pl.BlockSpec((None, slots, 128), lambda d, p: (d, 0, t * pairs + p))
    rel = pl.BlockSpec((3 * BUCKETS, 128), lambda d, p: (0, p))
    grel = pl.BlockSpec((None, 3 * BUCKETS, 128), lambda d, p: (d, 0, p))
    return pl.pallas_call(
        functools.partial(bwd_kernel, slots, sp, width),
        grid=(docs, pairs),
        in_specs=[part(0), part(1), part(2),
                  pl.BlockSpec((None, slots, 128), lambda d, p: (d, 0, p)),
                  pl.BlockSpec((None, 2, sp, sp), lambda d, p: (d, p, 0, 0)),
                  rel, rel,
                  pl.BlockSpec((None, sp, 2), lambda d, p: (d, 0, 0)),
                  pl.BlockSpec((None, 2, sp), lambda d, p: (d, 0, 0))],
        out_specs=[pl.BlockSpec((None, slots, 3 * width), lambda d, p: (d, 0, 0)), grel, grel],
        out_shape=[jax.ShapeDtypeStruct((docs, slots, 3 * width), BF16),
                   jax.ShapeDtypeStruct((docs, 3 * BUCKETS, width), F32),
                   jax.ShapeDtypeStruct((docs, 3 * BUCKETS, width), F32)],
        scratch_shapes=[pltpu.VMEM((sp, 128), BF16)] * 7
        + [pltpu.VMEM((sp, sp), BF16)] * 2 + [pltpu.VMEM((sp, sp + 256), BF16)] * 2
        + [pltpu.VMEM((128, sp), F32), pltpu.VMEM((128, 384), F32)],
        name="attend_backward",
        compiler_params=pltpu.CompilerParams(vmem_limit_bytes=56 << 20),
    )(qkv, qkv, qkv, dctx, probs, relk, relq, boxes_col, boxes_row)


EPSILON = 1e-05
ROOT_HALF = math.sqrt(0.5)
PDF_SCALE = 1.0 / math.sqrt(2.0 * math.pi)


def dot_nt(a, b):
    return lax.dot_general(a, b, (((1,), (1,)), ((), ())), preferred_element_type=F32)


def dot_tn(a, b):
    return lax.dot_general(a, b, (((0,), (0,)), ((), ())), preferred_element_type=F32)


def norm_rows(values, gain, shift):
    mean = jnp.mean(values, axis=1, keepdims=True)
    scale = lax.rsqrt(jnp.mean(values * values, axis=1, keepdims=True) - mean * mean + EPSILON)
    unit = (values - mean) * scale
    return unit * gain + shift, unit, scale


def norm_pull(upstream, unit, scale, gain):
    scaled = upstream * gain
    first = jnp.mean(scaled, axis=1, keepdims=True)
    second = jnp.mean(scaled * unit, axis=1, keepdims=True)
    return scale * (scaled - first - unit * second)


def exchange_sum(parts, bits, size, beside):
    place = lax.axis_index("dp")

    def swap(array, bit):
        return lax.ppermute(array, "dp", [(i, i ^ bit) for i in range(size)])

    def fold(array, bit):
        half = array.shape[0] // 2
        low = (place & bit) == 0
        keep = jnp.where(low, array[:half], array[half:])
        send = jnp.where(low, array[half:], array[:half])
        return (keep.astype(F32) + swap(send, bit).astype(F32)).astype(BF16)

    def unfold(array, bit):
        low = (place & bit) == 0
        other = swap(array, bit)
        return jnp.concatenate([jnp.where(low, array, other), jnp.where(low, other, array)], axis=0)

    arrays = [a for a, _ in parts]
    for step in range(len(bits)):
        arrays = [fold(a, order[step]) for a, (_, order) in zip(arrays, parts)]
    for step in reversed(range(len(bits))):
        if step == 0:
            arrays, beside = lax.optimization_barrier((arrays, beside))
        arrays = [unfold(a, order[step]) for a, (_, order) in zip(arrays, parts)]
    return arrays, beside


def sum_over_documents(table, size, beside):
    if size != 16:
        return lax.psum(table, "dp"), beside
    rows = table.shape[0]
    grain = 256
    pieces = 4
    step = -(-rows // (pieces * grain)) * grain
    padded = jnp.pad(table, ((0, pieces * step - rows), (0, 0)))
    orders = ((1, 2, 4, 8), (1, 4, 8, 2))
    parts = [(padded[i * step:(i + 1) * step], orders[i % 2]) for i in range(pieces)]
    arrays, beside = exchange_sum(parts, orders[0], size, beside)
    return jnp.concatenate(arrays, axis=0)[:rows], beside


def on_device(
    documents,
    shards,
    hidden_in,
    lengths,
    boxes,
    w_qkv,
    w_out,
    w_up,
    w_down,
    rel_keys,
    rel_queries,
    norm_gains,
    norm_shifts,
    out_grad,
):
    doc_count, slot_count, width = hidden_in.shape
    row_count = doc_count * slot_count
    model_width = w_qkv.shape[0]
    heads_here = width // HEAD_DIM
    me = lax.axis_index("tensor")
    pair = [(0, 1), (1, 0)]

    def join(array, axis):
        if shards != 2:
            return lax.all_gather(array, "tensor", axis=axis, tiled=True)
        other = lax.ppermute(array, "tensor", pair)
        first = me == 0
        return jnp.concatenate(
            [jnp.where(first, array, other), jnp.where(first, other, array)], axis=axis)

    def total(partial):
        if shards != 2:
            return lax.psum(partial, "tensor").astype(F32)
        return partial.astype(F32) + lax.ppermute(partial, "tensor", pair).astype(F32)

    def own(array):
        return lax.dynamic_slice_in_dim(array, me * width, width, axis=array.ndim - 1)

    def own_total(partial):
        if shards != 2:
            return lax.psum_scatter(partial, "tensor", scatter_dimension=1, tiled=True).astype(F32)
        send = lax.dynamic_slice_in_dim(partial, (1 - me) * width, width, axis=1)
        return own(partial).astype(F32) + lax.ppermute(send, "tensor", pair).astype(F32)

    rel_k = rel_keys.reshape(3 * BUCKETS, width)
    rel_q = rel_queries.reshape(3 * BUCKETS, width)
    padded = -(-slot_count // 128) * 128
    boxes_col = jnp.pad(boxes, ((0, 0), (0, padded - slot_count), (0, 0)))
    boxes_row = jnp.swapaxes(boxes_col, 1, 2)

    rows = join(hidden_in.reshape(row_count, width), 1)
    weight_qkv = w_qkv.reshape(model_width, 3 * width)
    projected = jnp.dot(rows, weight_qkv, preferred_element_type=F32).astype(BF16)
    norms = join(jnp.concatenate([norm_gains, norm_shifts], axis=0), 1)
    rows, out_rows = lax.optimization_barrier((rows, out_grad.reshape(row_count, width)))
    upstream = join(out_rows, 1)
    out_whole = join(w_out, 0)
    projected = projected.reshape(doc_count, slot_count, 3 * width)
    context, probs = attend_forward(lengths, projected, rel_k, rel_q, boxes_col, boxes_row, heads_here)
    context, upstream, norms, out_whole = lax.optimization_barrier((context, upstream, norms, out_whole))
    context = context.reshape(row_count, width)

    attn = jnp.dot(join(context, 1), out_whole, preferred_element_type=F32)
    h1, unit_first, scale_first = norm_rows(rows.astype(F32) + attn, norms[0:1], norms[2:3])
    h1_low = h1.astype(BF16)
    upper = jnp.dot(h1_low, w_up, preferred_element_type=F32)
    chance = 0.5 * (1.0 + lax.erf(upper * ROOT_HALF))
    active = (upper * chance).astype(BF16)
    slope = (chance + upper * (PDF_SCALE * jnp.exp(-0.5 * upper * upper))).astype(BF16)
    ffn = total(jnp.dot(active, w_down, preferred_element_type=F32).astype(BF16))
    result, unit_second, scale_second = norm_rows(h1 + ffn, norms[1:2], norms[3:4])
    hidden_out = own(result.astype(BF16)).reshape(doc_count, slot_count, width)

    upstream = upstream.astype(F32)
    grad_second = norm_pull(upstream, unit_second, scale_second, norms[1:2])
    grad_second, ffn_grad = lax.optimization_barrier((grad_second, grad_second.astype(BF16)))
    grad_upper = (dot_nt(ffn_grad, w_down) * slope.astype(F32)).astype(BF16)
    hidden_part = dot_nt(grad_upper, w_up).astype(BF16)
    down_grad = dot_tn(active, ffn_grad).astype(BF16)
    up_grad = dot_tn(h1_low, grad_upper).astype(BF16)
    ffn_sums = lax.psum((down_grad, up_grad), "dp")
    grad_hidden = grad_second + total(hidden_part)
    grad_first = norm_pull(grad_hidden, unit_first, scale_first, norms[0:1])
    attn_grad = grad_first.astype(BF16)
    norm_grads = own(jnp.stack([
        jnp.sum(grad_hidden * unit_first, axis=0),
        jnp.sum(upstream * unit_second, axis=0),
        jnp.sum(grad_hidden, axis=0),
        jnp.sum(upstream, axis=0)]))

    out_weight_grad = dot_tn(context, attn_grad)
    grad_context = dot_nt(attn_grad, w_out).astype(BF16).reshape(doc_count, slot_count, width)
    grad_projected, rel_k_sum, rel_q_sum = attend_backward(
        projected, grad_context, probs, rel_k, rel_q, boxes_col, boxes_row, heads_here
    )
    grad_rows = grad_projected.reshape(row_count, 3 * width)
    input_part = dot_nt(grad_rows, weight_qkv).astype(BF16)
    input_grad = own(grad_first) + own_total(input_part)
    input_grad = input_grad.astype(BF16).reshape(doc_count, slot_count, width)
    qkv_grads = [dot_tn(rows, grad_rows[:, t * width:(t + 1) * width]) for t in range(3)]
    pieces = qkv_grads + [jnp.sum(rel_k_sum, axis=0), jnp.sum(rel_q_sum, axis=0)]
    pieces += [out_weight_grad[:, t * width:(t + 1) * width] for t in range(shards)]
    pieces += [norm_grads]
    table, (down_grad, up_grad) = sum_over_documents(
        jnp.concatenate([p.astype(BF16) for p in pieces], axis=0), documents, ffn_sums)
    table = table.astype(F32)
    found = []
    at = 0
    for p in pieces:
        found.append(table[at:at + p.shape[0]])
        at += p.shape[0]
    qkv_grad = jnp.stack(found[0:3], axis=1)
    rel_keys_grad = found[3].reshape(3, BUCKETS, width)
    rel_queries_grad = found[4].reshape(3, BUCKETS, width)
    out_weight_grad = jnp.concatenate(found[5:5 + shards], axis=1)
    norm_grads = found[5 + shards]
    return (
        hidden_out,
        input_grad,
        qkv_grad,
        out_weight_grad,
        up_grad.astype(F32),
        down_grad.astype(F32),
        rel_keys_grad,
        rel_queries_grad,
        norm_grads[0:2],
        norm_grads[2:4],
    )


def solution(mesh):
    in_specs = (
        P("dp", None, "tensor"),
        P("dp"),
        P("dp", None, None),
        P(None, None, "tensor"),
        P("tensor", None),
        P(None, "tensor"),
        P("tensor", None),
        P(None, None, "tensor"),
        P(None, None, "tensor"),
        P(None, "tensor"),
        P(None, "tensor"),
        P("dp", None, "tensor"),
    )
    out_specs = (
        P("dp", None, "tensor"),
        P("dp", None, "tensor"),
        P(None, None, "tensor"),
        P("tensor", None),
        P(None, "tensor"),
        P("tensor", None),
        P(None, None, "tensor"),
        P(None, None, "tensor"),
        P(None, "tensor"),
        P(None, "tensor"),
    )
    body = functools.partial(on_device, mesh.shape["dp"], mesh.shape["tensor"])
    return jax.shard_map(body, mesh=mesh, in_specs=in_specs, out_specs=out_specs, check_vma=False)
```

```python
import math, functools
import jax, jax.numpy as jnp
from jax import lax
from jax.sharding import PartitionSpec as P
from jax.experimental import pallas as pl
from jax.experimental.pallas import tpu as pltpu

HEAD_DIM = 64
BUCKETS = 128
TEXT = 512
NEG = -1e30
LOG2E = math.log2(math.e)
SCALE = 1.0 / math.sqrt(3 * HEAD_DIM)
F32 = jnp.float32
BF16 = jnp.bfloat16


def nt(a, b):
    return lax.dot_general(a, b, (((1,), (1,)), ((), ())), preferred_element_type=F32)


def nn(a, b):
    return lax.dot_general(a, b, (((1,), (0,)), ((), ())), preferred_element_type=F32)


def iota(shape, d):
    return lax.broadcasted_iota(jnp.int32, shape, d)


def pick(table, index):
    return jnp.take_along_axis(table, index, axis=1, mode="promise_in_bounds")


def pick(table, index):
    dims = lax.GatherDimensionNumbers(
        offset_dims=(), collapsed_slice_dims=(1,), start_index_map=(1,),
        operand_batching_dims=(0,), start_indices_batching_dims=(0,))
    return lax.gather(table, index[..., None], dims, slice_sizes=(1, 1),
                      mode=lax.GatherScatterMode.PROMISE_IN_BOUNDS)


LEVELS = 10900.0
HALF_WORD = 65536.0


def tall_block(rows):
    return next(n for n in (288, 192, 128, 64) if rows % n == 0)


def fwd_kernel(slots, sp, rp, len_ref, q_ref, k_ref, v_ref, relk_ref, relq_ref, bc_ref, br_ref,
               ctx_ref, p_ref, qs, ks, vs, kt, idx, nq, nk, sq, fq, fk, gk, cs):
    pair = pl.program_id(1)
    nb = sp // 128
    tall = tall_block(rp)

    @pl.when(pair == 0)
    def _():
        qs[...] = jnp.zeros_like(qs)
        ks[...] = jnp.zeros_like(ks)
        vs[...] = jnp.zeros_like(vs)

        def rows(b, c):
            r0 = pl.multiple_of(b * 128, 128)
            row = iota((128, sp), 0) + r0
            col = iota((128, sp), 1)
            idx[0, pl.ds(r0, 128), :] = jnp.clip(col - row, -64, 63) + 64
            for t in range(2):
                x_i = bc_ref[pl.ds(r0, 128), t:t + 1]
                x_j = br_ref[t:t + 1, :]
                idx[t + 1, pl.ds(r0, 128), :] = jnp.clip((x_j - x_i) >> 4, -64, 63) + 64
            return c
        lax.fori_loop(0, nb, rows, 0)

    qs[0:slots, :] = q_ref[...]
    ks[0:slots, :] = k_ref[...]
    vs[0:slots, :] = v_ref[...]
    kt[...] = ks[...].astype(F32).T.astype(BF16)
    place = iota((1, sp), 1)
    length = len_ref[pl.program_id(0)]
    barred = jnp.where((place < length) | ((place >= TEXT) & (place < slots)), 0.0, NEG)
    half = iota((1, 128), 1) < 64

    def longest(rel_ref, h):
        rel = rel_ref[h * 64:(h + 1) * 64, :].astype(F32)
        return jnp.max(jnp.sum(rel * rel, axis=0, keepdims=True), axis=1, keepdims=True) * 1.03

    def bound(squares, most):
        return jnp.maximum(squares * most, 1e-30)

    member = jnp.where((iota((128, 256), 0) < 64) == (iota((128, 256), 1) < 128), 1.0, 0.0).astype(BF16)
    for side, (rows_ref, rel_ref, table) in enumerate(((qs, relk_ref, nq), (ks, relq_ref, nk))):
        most = [longest(rel_ref, h) for h in range(2)]
        if side == 1:
            most_k = most

        def pack(b, c):
            r0 = pl.multiple_of(b * tall, tall)
            here = rows_ref[pl.ds(r0, tall), :]
            wide = here.astype(F32)
            squares = nn((wide * wide).astype(BF16), member)
            words = []
            for h in range(2):
                mine = half if h == 0 else jnp.logical_not(half)
                top = bound(squares[:, h * 128:(h + 1) * 128], most[h])
                inverse = lax.rsqrt(top)
                if side == 0:
                    sq[h, pl.ds(r0, tall), :] = top * inverse * (1.0 / (LEVELS * HALF_WORD))
                inverse = inverse * LEVELS
                near = nn(jnp.where(mine, here, 0), rel_ref[...])
                words.append(jnp.round(near * jnp.concatenate([inverse] * 3, axis=1)).astype(jnp.int32))
            table[pl.ds(r0, tall), :] = (words[0] << 16) + words[1]
            return c
        lax.fori_loop(0, rp // tall, pack, 0)

    turned = kt[...].astype(F32)
    turned = (turned * turned).astype(BF16)
    pick_head = jnp.where((iota((16, 128), 0) < 8) == (iota((16, 128), 1) < 64), 1.0, 0.0).astype(BF16)
    squares = nn(pick_head, turned)
    step_k = [jnp.sqrt(bound(squares[h * 8:h * 8 + 1, :], most_k[h])) * (1.0 / (LEVELS * HALF_WORD)) for h in range(2)]

    def near(r0, count):
        for r in range(0, count, 8):
            here = pl.ds(pl.multiple_of(r0 + r, 8), 8)
            for jb in range(nb):
                at = slice(jb * 128, (jb + 1) * 128)
                sums = [None] * 2
                for t in range(3):
                    ix = idx[t, here, at]
                    kind = slice(t * 128, (t + 1) * 128)
                    for n, table in enumerate((nq, nk)):
                        e = pick(table[here, kind], ix)
                        sums[n] = e if sums[n] is None else sums[n] + e
                fq[here, at] = sums[0]
                gk[r:r + 8, at] = sums[1]
        for jb in range(nb):
            at = slice(jb * 128, (jb + 1) * 128)
            fk[at, pl.ds(r0, 128)] = gk[:, at].T

    def near_block(b, c):
        near(pl.multiple_of(b * 128, 128), 128)
        return c
    lax.fori_loop(0, rp // 128, near_block, 0)
    if rp % 128:
        gk[rp % 128:, :] = jnp.zeros((128 - rp % 128, sp), jnp.int32)
        near(rp // 128 * 128, rp % 128)

    def soft(b, c):
        r0 = pl.multiple_of(b * tall, tall)
        for h in range(2):
            mine = half if h == 0 else jnp.logical_not(half)
            q_b = jnp.where(mine, qs[pl.ds(r0, tall), :], 0)
            from_q = fq[pl.ds(r0, tall), :]
            from_k = fk[pl.ds(r0, tall), :]
            if h == 1:
                from_q = from_q << 16
                from_k = from_k << 16
            step_q = jnp.concatenate([sq[h, pl.ds(r0, tall), :]] * nb, axis=1)
            s = (nn(q_b, kt[...]) + barred) + (from_q.astype(F32) * step_q + from_k.astype(F32) * step_k[h])
            m = jnp.max(s, axis=1, keepdims=True)
            e = jnp.exp2((s - m) * (SCALE * LOG2E))
            tot = jnp.sum(e, axis=1, keepdims=True)
            p = (e * (1.0 / tot)).astype(BF16)
            p_ref[h, pl.ds(r0, tall), :] = p
            got = nn(p, vs[...])
            if h == 0:
                first = got
            else:
                cs[pl.ds(r0, tall), :] = jnp.where(mine, got, first).astype(BF16)
        return c
    lax.fori_loop(0, rp // tall, soft, 0)
    ctx_ref[...] = cs[0:slots, :]


def attend_forward(lengths, qkv, relk, relq, boxes_col, boxes_row, heads):
    docs, slots, width = qkv.shape
    width = width // 3
    sp = boxes_row.shape[2]
    rp = -(-slots // 64) * 64
    pairs = heads // 2

    def part(t):
        return pl.BlockSpec((None, slots, 128), lambda d, p, ln: (d, 0, t * pairs + p))
    rel = pl.BlockSpec((128, 3 * BUCKETS), lambda d, p, ln: (p, 0))
    grid_spec = pltpu.PrefetchScalarGridSpec(
        num_scalar_prefetch=1, grid=(docs, pairs),
        in_specs=[part(0), part(1), part(2), rel, rel,
                  pl.BlockSpec((None, sp, 2), lambda d, p, ln: (d, 0, 0)),
                  pl.BlockSpec((None, 2, sp), lambda d, p, ln: (d, 0, 0))],
        out_specs=[pl.BlockSpec((None, slots, 128), lambda d, p, ln: (d, 0, p)),
                   pl.BlockSpec((None, 2, rp, sp), lambda d, p, ln: (d, p, 0, 0))],
        scratch_shapes=[pltpu.VMEM((sp, 128), BF16)] * 3 + [pltpu.VMEM((128, sp), BF16)]
        + [pltpu.VMEM((3, sp, sp), jnp.int32), pltpu.VMEM((sp, 384), jnp.int32), pltpu.VMEM((sp, 384), jnp.int32),
           pltpu.VMEM((2, sp, 128), F32), pltpu.VMEM((sp, sp), jnp.int32), pltpu.VMEM((sp, sp), jnp.int32),
           pltpu.VMEM((128, sp), jnp.int32), pltpu.VMEM((rp, 128), BF16)])
    return pl.pallas_call(
        functools.partial(fwd_kernel, slots, sp, rp),
        out_shape=[jax.ShapeDtypeStruct((docs, slots, width), BF16),
                   jax.ShapeDtypeStruct((docs, heads, rp, sp), BF16)],
        grid_spec=grid_spec, name="attend_forward",
        compiler_params=pltpu.CompilerParams(vmem_limit_bytes=56 << 20),
    )(lengths, qkv, qkv, qkv, relk, relq, boxes_col, boxes_row)


def bwd_kernel(slots, sp, rp, width, q_ref, k_ref, v_ref, dc_ref, p_ref, relk_ref, relq_ref, bc_ref, br_ref,
               dqkv_ref, gk_ref, gq_ref,
               qs, ks, dcs, base, ex, ey, vt, qt, kt, dct, mx, my, ds, dst, w2, o1, hs, dns, gs, gt, acc):
    pair = pl.program_id(1)
    nb = sp // 128
    tall = tall_block(rp)

    @pl.when(pair == 0)
    def _():
        for r in (qs, ks, dcs, ds, dst):
            r[...] = jnp.zeros_like(r)
        lane = iota((sp, 128), 1)
        ax = bc_ref[:, 0:1] >> 4
        ay = bc_ref[:, 1:2] >> 4
        left = lane < 64
        c = lane & 63
        a = jnp.where(left, ax, ay)
        one = jnp.where(c == a, 1.0, 0.0)
        nxt = jnp.where(c == a + 1, 1.0, 0.0)
        base[...] = one.astype(BF16)
        e = nxt - one
        ex[...] = jnp.where(left, e, 0.0).astype(BF16)
        ey[...] = jnp.where(left, 0.0, e).astype(BF16)

        def rows(b, c):
            r0 = pl.multiple_of(b * 128, 128)
            for t, m in ((0, mx), (1, my)):
                r_i = bc_ref[pl.ds(r0, 128), t:t + 1] & 15
                r_j = br_ref[t:t + 1, :] & 15
                m[pl.ds(r0, 128), :] = jnp.where(r_j >= r_i, 1.0, 0.0).astype(BF16)
            return c
        lax.fori_loop(0, nb, rows, 0)

    qs[0:slots, :] = v_ref[...]
    vt[...] = qs[...].astype(F32).T.astype(BF16)
    qs[0:slots, :] = q_ref[...]
    ks[0:slots, :] = k_ref[...]
    dcs[0:slots, :] = dc_ref[...]
    qt[...] = qs[...].astype(F32).T.astype(BF16)
    kt[...] = ks[...].astype(F32).T.astype(BF16)
    dct[...] = dcs[...].astype(F32).T.astype(BF16)

    def head(h, carry):
        mine = (iota((1, 128), 1) < 64) == (h == 0)
        mine_down = (iota((128, 1), 0) < 64) == (h == 0)

        def grad_scores(b, c):
            r0 = pl.multiple_of(b * tall, tall)
            d_b = jnp.where(mine, dcs[pl.ds(r0, tall), :], 0)
            dp = nn(d_b, vt[...])
            p = p_ref[h, pl.ds(r0, tall), :].astype(F32)
            inner = jnp.sum(p * dp, axis=1, keepdims=True)
            ds[pl.ds(r0, tall), 128:128 + sp] = (p * (dp - inner)).astype(BF16)
            return c
        lax.fori_loop(0, rp // tall, grad_scores, 0)

        def turn(b, c):
            r0 = pl.multiple_of(b * 128, 128)
            for jb in range(nb):
                dst[jb * 128:(jb + 1) * 128, pl.ds(pl.multiple_of(r0 + 128, 128), 128)] = \
                    ds[pl.ds(r0, 128), (jb + 1) * 128:(jb + 2) * 128].T
            return c
        lax.fori_loop(0, nb, turn, 0)

        dvt = nn(dct[:, 0:rp], p_ref[h, :, :])
        gt[...] = jnp.where(mine_down, dvt, gt[...])

        for side in range(2):
            mat = ds if side == 0 else dst
            other = ks if side == 0 else qs
            own_t = qt if side == 0 else kt
            rel_ref = relk_ref if side == 0 else relq_ref
            blk = iota((sp, 128), 0) >> 7
            lane_sp = iota((sp, 128), 1) & 63
            w2[:, 0:128] = jnp.where(mine, other[...].astype(F32), jnp.where(blk == lane_sp, 1.0, 0.0)).astype(BF16)
            w2[:, 128:256] = base[...]

            def spread(b, c):
                r0 = pl.multiple_of(b * tall, tall)
                d_b = mat[pl.ds(r0, tall), 128:128 + sp]
                out = nn(d_b, w2[...])
                o1[pl.ds(r0, tall), :] = out[:, :128]
                hs[pl.ds(r0, tall), :] = out[:, 128:] + nn(d_b * mx[pl.ds(r0, tall), :], ex[...]) \
                    + nn(d_b * my[pl.ds(r0, tall), :], ey[...])
                return c
            lax.fori_loop(0, rp // tall, spread, 0)

            def buckets(b, r0, n):
                lane = iota((n, 128), 1)
                row = iota((n, 128), 0)
                before = mat[pl.ds(r0, n), pl.ds(r0, 128)].astype(F32)
                here = mat[pl.ds(r0, n), pl.ds(r0 + 128, 128)].astype(F32)
                after = mat[pl.ds(r0, n), pl.ds(r0 + 256, 128)].astype(F32)
                sums = jnp.where(mine, 0.0, o1[pl.ds(r0, n), :])
                blkno = lane & 63
                low = jnp.where(blkno <= b - 2, sums, 0.0) + jnp.where(lane <= row + 64, before, 0.0) \
                    + jnp.where(lane <= row - 64, here, 0.0)
                high = jnp.where(blkno >= b + 2, sums, 0.0) + jnp.where(lane >= row + 63, here, 0.0) \
                    + jnp.where(lane >= row - 65, after, 0.0)
                low = jnp.sum(low, axis=1, keepdims=True)
                high = jnp.sum(high, axis=1, keepdims=True)
                near = jnp.where(lane >= row + 64, before, jnp.where(lane <= row - 65, after, here))
                mid = pick(near, (lane + row + 64) & 127)
                dn0 = jnp.where(lane == 0, low, jnp.where(lane == 127, high, mid))
                hist = hs[pl.ds(r0, n), :]
                c1 = lane + (bc_ref[pl.ds(r0, n), 0:1] >> 4) - 63
                c2 = lane + (bc_ref[pl.ds(r0, n), 1:2] >> 4) - 63
                dn1 = jnp.where((c1 >= 0) & (c1 < 64), pick(hist, c1 & 127), 0.0)
                dn2 = jnp.where((c2 >= 0) & (c2 < 64), pick(hist, (c2 + 64) & 127), 0.0)
                dns[pl.ds(r0, n), :] = jnp.concatenate([dn0, dn1, dn2], axis=1).astype(BF16)

            def bucket_block(b, c):
                buckets(b, pl.multiple_of(b * 128, 128), 128)
                return c
            lax.fori_loop(0, rp // 128, bucket_block, 0)
            if rp % 128:
                buckets(rp // 128, rp // 128 * 128, rp % 128)

            def gather_back(b, c):
                r0 = pl.multiple_of(b * tall, tall)
                g = (o1[pl.ds(r0, tall), :] + nn(dns[pl.ds(r0, tall), :], rel_ref[...])) * SCALE
                gs[side, pl.ds(r0, tall), :] = jnp.where(mine, g, gs[side, pl.ds(r0, tall), :].astype(F32)).astype(BF16)
                return c
            lax.fori_loop(0, rp // tall, gather_back, 0)
            acc[side] = jnp.where(mine_down, nn(own_t[:, 0:rp], dns[...]), acc[side])
        return carry
    lax.fori_loop(0, 2, head, 0)

    for side in range(2):
        dqkv_ref[:, pl.ds(pl.multiple_of(side * width + pair * 128, 128), 128)] = gs[side, 0:slots, :]
    gk_ref[...] = acc[0].T * SCALE
    gq_ref[...] = acc[1].T * SCALE
    dqkv_ref[:, pl.ds(pl.multiple_of(2 * width + pair * 128, 128), 128)] = gt[...].T[0:slots, :].astype(BF16)


def attend_backward(qkv, dctx, probs, relk, relq, boxes_col, boxes_row, heads):
    docs, slots, width = qkv.shape
    width = width // 3
    sp = boxes_row.shape[2]
    rp = -(-slots // 64) * 64
    pairs = heads // 2

    def part(t):
        return pl.BlockSpec((None, slots, 128), lambda d, p: (d, 0, t * pairs + p))
    rel = pl.BlockSpec((3 * BUCKETS, 128), lambda d, p: (0, p))
    grel = pl.BlockSpec((None, 3 * BUCKETS, 128), lambda d, p: (d, 0, p))
    return pl.pallas_call(
        functools.partial(bwd_kernel, slots, sp, rp, width),
        grid=(docs, pairs),
        in_specs=[part(0), part(1), part(2),
                  pl.BlockSpec((None, slots, 128), lambda d, p: (d, 0, p)),
                  pl.BlockSpec((None, 2, rp, sp), lambda d, p: (d, p, 0, 0)),
                  rel, rel,
                  pl.BlockSpec((None, sp, 2), lambda d, p: (d, 0, 0)),
                  pl.BlockSpec((None, 2, sp), lambda d, p: (d, 0, 0))],
        out_specs=[pl.BlockSpec((None, slots, 3 * width), lambda d, p: (d, 0, 0)), grel, grel],
        out_shape=[jax.ShapeDtypeStruct((docs, slots, 3 * width), BF16),
                   jax.ShapeDtypeStruct((docs, 3 * BUCKETS, width), F32),
                   jax.ShapeDtypeStruct((docs, 3 * BUCKETS, width), F32)],
        scratch_shapes=[pltpu.VMEM((sp, 128), BF16)] * 6 + [pltpu.VMEM((128, sp), BF16)] * 4
        + [pltpu.VMEM((sp, sp), BF16)] * 2 + [pltpu.VMEM((sp, sp + 256), BF16)] * 2
        + [pltpu.VMEM((sp, 256), BF16), pltpu.VMEM((rp, 128), F32), pltpu.VMEM((rp, 128), F32),
           pltpu.VMEM((rp, 384), BF16), pltpu.VMEM((2, rp, 128), BF16), pltpu.VMEM((128, sp), F32),
           pltpu.VMEM((2, 128, 384), F32)],
        name="attend_backward",
        compiler_params=pltpu.CompilerParams(vmem_limit_bytes=56 << 20),
    )(qkv, qkv, qkv, dctx, probs, relk, relq, boxes_col, boxes_row)


EPSILON = 1e-05
ROOT_HALF = math.sqrt(0.5)
PDF_SCALE = 1.0 / math.sqrt(2.0 * math.pi)


def dot_nt(a, b):
    return lax.dot_general(a, b, (((1,), (1,)), ((), ())), preferred_element_type=F32)


def dot_tn(a, b):
    return lax.dot_general(a, b, (((0,), (0,)), ((), ())), preferred_element_type=F32)


def norm_rows(values, gain, shift):
    mean = jnp.mean(values, axis=1, keepdims=True)
    scale = lax.rsqrt(jnp.mean(values * values, axis=1, keepdims=True) - mean * mean + EPSILON)
    unit = (values - mean) * scale
    return unit * gain + shift, unit, scale


def norm_pull(upstream, unit, scale, gain):
    scaled = upstream * gain
    first = jnp.mean(scaled, axis=1, keepdims=True)
    second = jnp.mean(scaled * unit, axis=1, keepdims=True)
    return scale * (scaled - first - unit * second)


def exchange_sum(parts, bits, size, beside):
    place = lax.axis_index("dp")

    def swap(array, bit):
        return lax.ppermute(array, "dp", [(i, i ^ bit) for i in range(size)])

    def fold(array, bit):
        half = array.shape[0] // 2
        low = (place & bit) == 0
        keep = jnp.where(low, array[:half], array[half:])
        send = jnp.where(low, array[half:], array[:half])
        return (keep.astype(F32) + swap(send, bit).astype(F32)).astype(BF16)

    def unfold(array, bit):
        low = (place & bit) == 0
        other = swap(array, bit)
        return jnp.concatenate([jnp.where(low, array, other), jnp.where(low, other, array)], axis=0)

    arrays = [a for a, _ in parts]
    for step in range(len(bits)):
        arrays = [fold(a, order[step]) for a, (_, order) in zip(arrays, parts)]
    for step in reversed(range(len(bits))):
        if step == 0:
            arrays, beside = lax.optimization_barrier((arrays, beside))
        arrays = [unfold(a, order[step]) for a, (_, order) in zip(arrays, parts)]
    return arrays, beside


def sum_over_documents(table, size, beside):
    if size != 16:
        return lax.psum(table, "dp"), beside
    rows = table.shape[0]
    grain = 256
    pieces = 4
    step = -(-rows // (pieces * grain)) * grain
    padded = jnp.pad(table, ((0, pieces * step - rows), (0, 0)))
    orders = ((1, 2, 4, 8), (1, 4, 8, 2))
    parts = [(padded[i * step:(i + 1) * step], orders[i % 2]) for i in range(pieces)]
    arrays, beside = exchange_sum(parts, orders[0], size, beside)
    return jnp.concatenate(arrays, axis=0)[:rows], beside


def on_device(
    documents,
    shards,
    hidden_in,
    lengths,
    boxes,
    w_qkv,
    w_out,
    w_up,
    w_down,
    rel_keys,
    rel_queries,
    norm_gains,
    norm_shifts,
    out_grad,
):
    doc_count, slot_count, width = hidden_in.shape
    row_count = doc_count * slot_count
    model_width = w_qkv.shape[0]
    heads_here = width // HEAD_DIM
    me = lax.axis_index("tensor")
    pair = [(0, 1), (1, 0)]

    def join(array, axis):
        if shards != 2:
            return lax.all_gather(array, "tensor", axis=axis, tiled=True)
        other = lax.ppermute(array, "tensor", pair)
        first = me == 0
        return jnp.concatenate(
            [jnp.where(first, array, other), jnp.where(first, other, array)], axis=axis)

    def total(partial):
        if shards != 2:
            return lax.psum(partial, "tensor").astype(F32)
        return partial.astype(F32) + lax.ppermute(partial, "tensor", pair).astype(F32)

    def own(array):
        return lax.dynamic_slice_in_dim(array, me * width, width, axis=array.ndim - 1)

    def own_total(partial):
        if shards != 2:
            return lax.psum_scatter(partial, "tensor", scatter_dimension=1, tiled=True).astype(F32)
        send = lax.dynamic_slice_in_dim(partial, (1 - me) * width, width, axis=1)
        return own(partial).astype(F32) + lax.ppermute(send, "tensor", pair).astype(F32)

    rel_k = rel_keys.reshape(3 * BUCKETS, width)
    rel_q = rel_queries.reshape(3 * BUCKETS, width)
    padded = -(-slot_count // 128) * 128
    boxes_col = jnp.pad(boxes, ((0, 0), (0, padded - slot_count), (0, 0)))
    boxes_row = jnp.swapaxes(boxes_col, 1, 2)

    rows = join(hidden_in.reshape(row_count, width), 1)
    weight_qkv = w_qkv.reshape(model_width, 3 * width)
    projected = jnp.dot(rows, weight_qkv, preferred_element_type=F32).astype(BF16)
    norms = join(jnp.concatenate([norm_gains, norm_shifts], axis=0), 1)
    rows, out_rows = lax.optimization_barrier((rows, out_grad.reshape(row_count, width)))
    upstream = join(out_rows, 1)
    out_whole = join(w_out, 0)
    projected = projected.reshape(doc_count, slot_count, 3 * width)
    context, probs = attend_forward(lengths, projected, rel_k.T, rel_q.T, boxes_col, boxes_row, heads_here)
    context, upstream, norms, out_whole = lax.optimization_barrier((context, upstream, norms, out_whole))
    context = context.reshape(row_count, width)

    attn = jnp.dot(join(context, 1), out_whole, preferred_element_type=F32)
    h1, unit_first, scale_first = norm_rows(rows.astype(F32) + attn, norms[0:1], norms[2:3])
    h1_low = h1.astype(BF16)
    upper = jnp.dot(h1_low, w_up, preferred_element_type=F32)
    chance = 0.5 * (1.0 + lax.erf(upper * ROOT_HALF))
    active = (upper * chance).astype(BF16)
    slope = (chance + upper * (PDF_SCALE * jnp.exp(-0.5 * upper * upper))).astype(BF16)
    ffn = total(jnp.dot(active, w_down, preferred_element_type=F32).astype(BF16))
    result, unit_second, scale_second = norm_rows(h1 + ffn, norms[1:2], norms[3:4])
    hidden_out = own(result.astype(BF16)).reshape(doc_count, slot_count, width)

    upstream = upstream.astype(F32)
    grad_second = norm_pull(upstream, unit_second, scale_second, norms[1:2])
    grad_second, ffn_grad = lax.optimization_barrier((grad_second, grad_second.astype(BF16)))
    grad_upper = (dot_nt(ffn_grad, w_down) * slope.astype(F32)).astype(BF16)
    hidden_part = dot_nt(grad_upper, w_up).astype(BF16)
    down_grad = dot_tn(active, ffn_grad).astype(BF16)
    up_grad = dot_tn(h1_low, grad_upper).astype(BF16)
    ffn_sums = lax.psum((down_grad, up_grad), "dp")
    grad_hidden = grad_second + total(hidden_part)
    grad_first = norm_pull(grad_hidden, unit_first, scale_first, norms[0:1])
    attn_grad = grad_first.astype(BF16)
    norm_grads = own(jnp.stack([
        jnp.sum(grad_hidden * unit_first, axis=0),
        jnp.sum(upstream * unit_second, axis=0),
        jnp.sum(grad_hidden, axis=0),
        jnp.sum(upstream, axis=0)]))

    out_weight_grad = dot_tn(context, attn_grad)
    grad_context = dot_nt(attn_grad, w_out).astype(BF16).reshape(doc_count, slot_count, width)
    grad_projected, rel_k_sum, rel_q_sum = attend_backward(
        projected, grad_context, probs, rel_k, rel_q, boxes_col, boxes_row, heads_here
    )
    grad_rows = grad_projected.reshape(row_count, 3 * width)
    input_part = dot_nt(grad_rows, weight_qkv).astype(BF16)
    input_grad = own(grad_first) + own_total(input_part)
    input_grad = input_grad.astype(BF16).reshape(doc_count, slot_count, width)
    qkv_grads = [dot_tn(rows, grad_rows[:, t * width:(t + 1) * width]) for t in range(3)]
    pieces = qkv_grads + [jnp.sum(rel_k_sum, axis=0), jnp.sum(rel_q_sum, axis=0)]
    pieces += [out_weight_grad[:, t * width:(t + 1) * width] for t in range(shards)]
    pieces += [norm_grads]
    table, (down_grad, up_grad) = sum_over_documents(
        jnp.concatenate([p.astype(BF16) for p in pieces], axis=0), documents, ffn_sums)
    table = table.astype(F32)
    found = []
    at = 0
    for p in pieces:
        found.append(table[at:at + p.shape[0]])
        at += p.shape[0]
    qkv_grad = jnp.stack(found[0:3], axis=1)
    rel_keys_grad = found[3].reshape(3, BUCKETS, width)
    rel_queries_grad = found[4].reshape(3, BUCKETS, width)
    out_weight_grad = jnp.concatenate(found[5:5 + shards], axis=1)
    norm_grads = found[5 + shards]
    return (
        hidden_out,
        input_grad,
        qkv_grad,
        out_weight_grad,
        up_grad.astype(F32),
        down_grad.astype(F32),
        rel_keys_grad,
        rel_queries_grad,
        norm_grads[0:2],
        norm_grads[2:4],
    )


def solution(mesh):
    in_specs = (
        P("dp", None, "tensor"),
        P("dp"),
        P("dp", None, None),
        P(None, None, "tensor"),
        P("tensor", None),
        P(None, "tensor"),
        P("tensor", None),
        P(None, None, "tensor"),
        P(None, None, "tensor"),
        P(None, "tensor"),
        P(None, "tensor"),
        P("dp", None, "tensor"),
    )
    out_specs = (
        P("dp", None, "tensor"),
        P("dp", None, "tensor"),
        P(None, None, "tensor"),
        P("tensor", None),
        P(None, "tensor"),
        P("tensor", None),
        P(None, None, "tensor"),
        P(None, None, "tensor"),
        P(None, "tensor"),
        P(None, "tensor"),
    )
    body = functools.partial(on_device, mesh.shape["dp"], mesh.shape["tensor"])
    return jax.shard_map(body, mesh=mesh, in_specs=in_specs, out_specs=out_specs, check_vma=False)
```

```python
import math, functools
import jax, jax.numpy as jnp
from jax import lax
from jax.sharding import PartitionSpec as P
from jax.experimental import pallas as pl
from jax.experimental.pallas import tpu as pltpu

HEAD_DIM = 64
BUCKETS = 128
TEXT = 512
NEG = -1e30
LOG2E = math.log2(math.e)
SCALE = 1.0 / math.sqrt(3 * HEAD_DIM)
F32 = jnp.float32
BF16 = jnp.bfloat16


def nt(a, b):
    return lax.dot_general(a, b, (((1,), (1,)), ((), ())), preferred_element_type=F32)


def nn(a, b):
    return lax.dot_general(a, b, (((1,), (0,)), ((), ())), preferred_element_type=F32)


def iota(shape, d):
    return lax.broadcasted_iota(jnp.int32, shape, d)


def pick(table, index):
    return jnp.take_along_axis(table, index, axis=1, mode="promise_in_bounds")


def pick(table, index):
    dims = lax.GatherDimensionNumbers(
        offset_dims=(), collapsed_slice_dims=(1,), start_index_map=(1,),
        operand_batching_dims=(0,), start_indices_batching_dims=(0,))
    return lax.gather(table, index[..., None], dims, slice_sizes=(1, 1),
                      mode=lax.GatherScatterMode.PROMISE_IN_BOUNDS)


LEVELS = 10900.0
HALF_WORD = 65536.0


def tall_block(rows):
    return next(n for n in (288, 192, 128, 64) if rows % n == 0)


def fwd_kernel(slots, sp, rp, len_ref, q_ref, k_ref, v_ref, relk_ref, relq_ref, bc_ref, br_ref,
               ctx_ref, p_ref, qs, ks, vs, kt, idx, nq, nk, sq, fq, fk, gk, cs):
    pair = pl.program_id(1)
    nb = sp // 128
    tall = tall_block(rp)

    @pl.when(pair == 0)
    def _():
        qs[...] = jnp.zeros_like(qs)
        ks[...] = jnp.zeros_like(ks)
        vs[...] = jnp.zeros_like(vs)

        def rows(b, c):
            r0 = pl.multiple_of(b * 128, 128)
            row = iota((128, sp), 0) + r0
            col = iota((128, sp), 1)
            idx[0, pl.ds(r0, 128), :] = jnp.clip(col - row, -64, 63) + 64
            for t in range(2):
                x_i = bc_ref[pl.ds(r0, 128), t:t + 1]
                x_j = br_ref[t:t + 1, :]
                idx[t + 1, pl.ds(r0, 128), :] = jnp.clip((x_j - x_i) >> 4, -64, 63) + 64
            return c
        lax.fori_loop(0, nb, rows, 0)

    qs[0:slots, :] = q_ref[...]
    ks[0:slots, :] = k_ref[...]
    vs[0:slots, :] = v_ref[...]
    kt[...] = ks[...].astype(F32).T.astype(BF16)
    place = iota((1, sp), 1)
    length = len_ref[pl.program_id(0)]
    barred = jnp.where((place < length) | ((place >= TEXT) & (place < slots)), 0.0, NEG)
    half = iota((1, 128), 1) < 64

    def longest(rel_ref, h):
        rel = rel_ref[h * 64:(h + 1) * 64, :].astype(F32)
        return jnp.max(jnp.sum(rel * rel, axis=0, keepdims=True), axis=1, keepdims=True) * 1.03

    def bound(squares, most):
        return jnp.maximum(squares * most, 1e-30)

    member = jnp.where((iota((128, 256), 0) < 64) == (iota((128, 256), 1) < 128), 1.0, 0.0).astype(BF16)
    for side, (rows_ref, rel_ref, table) in enumerate(((qs, relk_ref, nq), (ks, relq_ref, nk))):
        most = [longest(rel_ref, h) for h in range(2)]
        if side == 1:
            most_k = most

        def pack(b, c):
            r0 = pl.multiple_of(b * tall, tall)
            here = rows_ref[pl.ds(r0, tall), :]
            wide = here.astype(F32)
            squares = nn((wide * wide).astype(BF16), member)
            words = []
            for h in range(2):
                mine = half if h == 0 else jnp.logical_not(half)
                top = bound(squares[:, h * 128:(h + 1) * 128], most[h])
                inverse = lax.rsqrt(top)
                if side == 0:
                    sq[h, pl.ds(r0, tall), :] = top * inverse * (1.0 / (LEVELS * HALF_WORD))
                inverse = inverse * LEVELS
                near = nn(jnp.where(mine, here, 0), rel_ref[...])
                words.append(jnp.round(near * jnp.concatenate([inverse] * 3, axis=1)).astype(jnp.int32))
            table[pl.ds(r0, tall), :] = (words[0] << 16) + words[1]
            return c
        lax.fori_loop(0, rp // tall, pack, 0)

    turned = kt[...].astype(F32)
    turned = (turned * turned).astype(BF16)
    pick_head = jnp.where((iota((16, 128), 0) < 8) == (iota((16, 128), 1) < 64), 1.0, 0.0).astype(BF16)
    squares = nn(pick_head, turned)
    step_k = [jnp.sqrt(bound(squares[h * 8:h * 8 + 1, :], most_k[h])) * (1.0 / (LEVELS * HALF_WORD)) for h in range(2)]

    def near(r0, count):
        for r in range(0, count, 8):
            here = pl.ds(pl.multiple_of(r0 + r, 8), 8)
            for jb in range(nb):
                at = slice(jb * 128, (jb + 1) * 128)
                sums = [None] * 2
                for t in range(3):
                    ix = idx[t, here, at]
                    kind = slice(t * 128, (t + 1) * 128)
                    for n, table in enumerate((nq, nk)):
                        e = pick(table[here, kind], ix)
                        sums[n] = e if sums[n] is None else sums[n] + e
                fq[here, at] = sums[0]
                gk[r:r + 8, at] = sums[1]
        for jb in range(nb):
            at = slice(jb * 128, (jb + 1) * 128)
            fk[at, pl.ds(r0, 128)] = gk[:, at].T

    def near_block(b, c):
        near(pl.multiple_of(b * 128, 128), 128)
        return c
    lax.fori_loop(0, rp // 128, near_block, 0)
    if rp % 128:
        gk[rp % 128:, :] = jnp.zeros((128 - rp % 128, sp), jnp.int32)
        near(rp // 128 * 128, rp % 128)

    def soft(b, c):
        r0 = pl.multiple_of(b * tall, tall)
        for h in range(2):
            mine = half if h == 0 else jnp.logical_not(half)
            q_b = jnp.where(mine, qs[pl.ds(r0, tall), :], 0)
            from_q = fq[pl.ds(r0, tall), :]
            from_k = fk[pl.ds(r0, tall), :]
            if h == 1:
                from_q = from_q << 16
                from_k = from_k << 16
            step_q = jnp.concatenate([sq[h, pl.ds(r0, tall), :]] * nb, axis=1)
            s = (nn(q_b, kt[...]) + barred) + (from_q.astype(F32) * step_q + from_k.astype(F32) * step_k[h])
            m = jnp.max(s, axis=1, keepdims=True)
            e = jnp.exp2((s - m) * (SCALE * LOG2E))
            tot = jnp.sum(e, axis=1, keepdims=True)
            p = (e * (1.0 / tot)).astype(BF16)
            p_ref[h, pl.ds(r0, tall), :] = p
            got = nn(p, vs[...])
            if h == 0:
                first = got
            else:
                cs[pl.ds(r0, tall), :] = jnp.where(mine, got, first).astype(BF16)
        return c
    lax.fori_loop(0, rp // tall, soft, 0)
    ctx_ref[...] = cs[0:slots, :]


def attend_forward(lengths, qkv, relk, relq, boxes_col, boxes_row, heads):
    docs, slots, width = qkv.shape
    width = width // 3
    sp = boxes_row.shape[2]
    rp = -(-slots // 64) * 64
    pairs = heads // 2

    def part(t):
        return pl.BlockSpec((None, slots, 128), lambda d, p, ln: (d, 0, t * pairs + p))
    rel = pl.BlockSpec((128, 3 * BUCKETS), lambda d, p, ln: (p, 0))
    grid_spec = pltpu.PrefetchScalarGridSpec(
        num_scalar_prefetch=1, grid=(docs, pairs),
        in_specs=[part(0), part(1), part(2), rel, rel,
                  pl.BlockSpec((None, sp, 2), lambda d, p, ln: (d, 0, 0)),
                  pl.BlockSpec((None, 2, sp), lambda d, p, ln: (d, 0, 0))],
        out_specs=[pl.BlockSpec((None, slots, 128), lambda d, p, ln: (d, 0, p)),
                   pl.BlockSpec((None, 2, rp, sp), lambda d, p, ln: (d, p, 0, 0))],
        scratch_shapes=[pltpu.VMEM((sp, 128), BF16)] * 3 + [pltpu.VMEM((128, sp), BF16)]
        + [pltpu.VMEM((3, sp, sp), jnp.int32), pltpu.VMEM((sp, 384), jnp.int32), pltpu.VMEM((sp, 384), jnp.int32),
           pltpu.VMEM((2, sp, 128), F32), pltpu.VMEM((sp, sp), jnp.int32), pltpu.VMEM((sp, sp), jnp.int32),
           pltpu.VMEM((128, sp), jnp.int32), pltpu.VMEM((rp, 128), BF16)])
    return pl.pallas_call(
        functools.partial(fwd_kernel, slots, sp, rp),
        out_shape=[jax.ShapeDtypeStruct((docs, slots, width), BF16),
                   jax.ShapeDtypeStruct((docs, heads, rp, sp), BF16)],
        grid_spec=grid_spec, name="attend_forward",
        compiler_params=pltpu.CompilerParams(vmem_limit_bytes=56 << 20),
    )(lengths, qkv, qkv, qkv, relk, relq, boxes_col, boxes_row)


def bwd_kernel(slots, sp, rp, width, q_ref, k_ref, v_ref, dc_ref, p_ref, relk_ref, relq_ref, bc_ref, br_ref,
               dqkv_ref, gk_ref, gq_ref,
               qs, ks, dcs, base, ex, ey, vt, qt, kt, dct, mx, my, ds, dst, w2, o1, hs, dns, gs, gt, acc):
    pair = pl.program_id(1)
    nb = sp // 128
    tall = tall_block(rp)

    @pl.when(pair == 0)
    def _():
        for r in (qs, ks, dcs, ds, dst):
            r[...] = jnp.zeros_like(r)
        lane = iota((sp, 128), 1)
        ax = bc_ref[:, 0:1] >> 4
        ay = bc_ref[:, 1:2] >> 4
        left = lane < 64
        c = lane & 63
        a = jnp.where(left, ax, ay)
        one = jnp.where(c == a, 1.0, 0.0)
        nxt = jnp.where(c == a + 1, 1.0, 0.0)
        base[...] = one.astype(BF16)
        e = nxt - one
        ex[...] = jnp.where(left, e, 0.0).astype(BF16)
        ey[...] = jnp.where(left, 0.0, e).astype(BF16)

        def rows(b, c):
            r0 = pl.multiple_of(b * 128, 128)
            for t, m in ((0, mx), (1, my)):
                r_i = bc_ref[pl.ds(r0, 128), t:t + 1] & 15
                r_j = br_ref[t:t + 1, :] & 15
                m[pl.ds(r0, 128), :] = jnp.where(r_j >= r_i, 1.0, 0.0).astype(BF16)
            return c
        lax.fori_loop(0, nb, rows, 0)

    qs[0:slots, :] = v_ref[...]
    vt[...] = qs[...].astype(F32).T.astype(BF16)
    qs[0:slots, :] = q_ref[...]
    ks[0:slots, :] = k_ref[...]
    dcs[0:slots, :] = dc_ref[...]
    qt[...] = qs[...].astype(F32).T.astype(BF16)
    kt[...] = ks[...].astype(F32).T.astype(BF16)
    dct[...] = dcs[...].astype(F32).T.astype(BF16)

    def head(h, carry):
        mine = (iota((1, 128), 1) < 64) == (h == 0)
        mine_down = (iota((128, 1), 0) < 64) == (h == 0)

        def grad_scores(b, c):
            r0 = pl.multiple_of(b * tall, tall)
            d_b = jnp.where(mine, dcs[pl.ds(r0, tall), :], 0)
            dp = nn(d_b, vt[...])
            p = p_ref[h, pl.ds(r0, tall), :].astype(F32)
            inner = jnp.sum(p * dp, axis=1, keepdims=True)
            ds[pl.ds(r0, tall), 128:128 + sp] = (p * (dp - inner)).astype(BF16)
            return c
        lax.fori_loop(0, rp // tall, grad_scores, 0)

        def turn(b, c):
            r0 = pl.multiple_of(b * 128, 128)
            for jb in range(nb):
                dst[jb * 128:(jb + 1) * 128, pl.ds(pl.multiple_of(r0 + 128, 128), 128)] = \
                    ds[pl.ds(r0, 128), (jb + 1) * 128:(jb + 2) * 128].T
            return c
        lax.fori_loop(0, nb, turn, 0)

        dvt = nn(dct[:, 0:rp], p_ref[h, :, :])
        gt[...] = jnp.where(mine_down, dvt, gt[...])

        for side in range(2):
            mat = ds if side == 0 else dst
            other = ks if side == 0 else qs
            own_t = qt if side == 0 else kt
            rel_ref = relk_ref if side == 0 else relq_ref
            blk = iota((sp, 128), 0) >> 7
            lane_sp = iota((sp, 128), 1) & 63
            w2[:, 0:128] = jnp.where(mine, other[...].astype(F32), jnp.where(blk == lane_sp, 1.0, 0.0)).astype(BF16)
            w2[:, 128:256] = base[...]

            def spread(b, c):
                r0 = pl.multiple_of(b * tall, tall)
                d_b = mat[pl.ds(r0, tall), 128:128 + sp]
                out = nn(d_b, w2[...])
                o1[pl.ds(r0, tall), :] = out[:, :128]
                hs[pl.ds(r0, tall), :] = out[:, 128:] + nn(d_b * mx[pl.ds(r0, tall), :], ex[...]) \
                    + nn(d_b * my[pl.ds(r0, tall), :], ey[...])
                return c
            lax.fori_loop(0, rp // tall, spread, 0)

            def buckets(b, r0, n):
                lane = iota((n, 128), 1)
                row = iota((n, 128), 0)
                before = mat[pl.ds(r0, n), pl.ds(r0, 128)].astype(F32)
                here = mat[pl.ds(r0, n), pl.ds(r0 + 128, 128)].astype(F32)
                after = mat[pl.ds(r0, n), pl.ds(r0 + 256, 128)].astype(F32)
                sums = jnp.where(mine, 0.0, o1[pl.ds(r0, n), :])
                blkno = lane & 63
                low = jnp.where(blkno <= b - 2, sums, 0.0) + jnp.where(lane <= row + 64, before, 0.0) \
                    + jnp.where(lane <= row - 64, here, 0.0)
                high = jnp.where(blkno >= b + 2, sums, 0.0) + jnp.where(lane >= row + 63, here, 0.0) \
                    + jnp.where(lane >= row - 65, after, 0.0)
                low = jnp.sum(low, axis=1, keepdims=True)
                high = jnp.sum(high, axis=1, keepdims=True)
                near = jnp.where(lane >= row + 64, before, jnp.where(lane <= row - 65, after, here))
                mid = pick(near, (lane + row + 64) & 127)
                dn0 = jnp.where(lane == 0, low, jnp.where(lane == 127, high, mid))
                hist = hs[pl.ds(r0, n), :]
                c1 = lane + (bc_ref[pl.ds(r0, n), 0:1] >> 4) - 63
                c2 = lane + (bc_ref[pl.ds(r0, n), 1:2] >> 4) - 63
                dn1 = jnp.where((c1 >= 0) & (c1 < 64), pick(hist, c1 & 127), 0.0)
                dn2 = jnp.where((c2 >= 0) & (c2 < 64), pick(hist, (c2 + 64) & 127), 0.0)
                dns[pl.ds(r0, n), :] = jnp.concatenate([dn0, dn1, dn2], axis=1).astype(BF16)

            def bucket_block(b, c):
                buckets(b, pl.multiple_of(b * 128, 128), 128)
                return c
            lax.fori_loop(0, rp // 128, bucket_block, 0)
            if rp % 128:
                buckets(rp // 128, rp // 128 * 128, rp % 128)

            def gather_back(b, c):
                r0 = pl.multiple_of(b * tall, tall)
                g = (o1[pl.ds(r0, tall), :] + nn(dns[pl.ds(r0, tall), :], rel_ref[...])) * SCALE
                gs[side, pl.ds(r0, tall), :] = jnp.where(mine, g, gs[side, pl.ds(r0, tall), :].astype(F32)).astype(BF16)
                return c
            lax.fori_loop(0, rp // tall, gather_back, 0)
            acc[side] = jnp.where(mine_down, nn(own_t[:, 0:rp], dns[...]), acc[side])
        return carry
    lax.fori_loop(0, 2, head, 0)

    for side in range(2):
        dqkv_ref[:, pl.ds(pl.multiple_of(side * width + pair * 128, 128), 128)] = gs[side, 0:slots, :]
    gk_ref[...] = acc[0].T * SCALE
    gq_ref[...] = acc[1].T * SCALE
    dqkv_ref[:, pl.ds(pl.multiple_of(2 * width + pair * 128, 128), 128)] = gt[...].T[0:slots, :].astype(BF16)


def attend_backward(qkv, dctx, probs, relk, relq, boxes_col, boxes_row, heads):
    docs, slots, width = qkv.shape
    width = width // 3
    sp = boxes_row.shape[2]
    rp = -(-slots // 64) * 64
    pairs = heads // 2

    def part(t):
        return pl.BlockSpec((None, slots, 128), lambda d, p: (d, 0, t * pairs + p))
    rel = pl.BlockSpec((3 * BUCKETS, 128), lambda d, p: (0, p))
    grel = pl.BlockSpec((None, 3 * BUCKETS, 128), lambda d, p: (d, 0, p))
    return pl.pallas_call(
        functools.partial(bwd_kernel, slots, sp, rp, width),
        grid=(docs, pairs),
        in_specs=[part(0), part(1), part(2),
                  pl.BlockSpec((None, slots, 128), lambda d, p: (d, 0, p)),
                  pl.BlockSpec((None, 2, rp, sp), lambda d, p: (d, p, 0, 0)),
                  rel, rel,
                  pl.BlockSpec((None, sp, 2), lambda d, p: (d, 0, 0)),
                  pl.BlockSpec((None, 2, sp), lambda d, p: (d, 0, 0))],
        out_specs=[pl.BlockSpec((None, slots, 3 * width), lambda d, p: (d, 0, 0)), grel, grel],
        out_shape=[jax.ShapeDtypeStruct((docs, slots, 3 * width), BF16),
                   jax.ShapeDtypeStruct((docs, 3 * BUCKETS, width), F32),
                   jax.ShapeDtypeStruct((docs, 3 * BUCKETS, width), F32)],
        scratch_shapes=[pltpu.VMEM((sp, 128), BF16)] * 6 + [pltpu.VMEM((128, sp), BF16)] * 4
        + [pltpu.VMEM((sp, sp), BF16)] * 2 + [pltpu.VMEM((sp, sp + 256), BF16)] * 2
        + [pltpu.VMEM((sp, 256), BF16), pltpu.VMEM((rp, 128), F32), pltpu.VMEM((rp, 128), F32),
           pltpu.VMEM((rp, 384), BF16), pltpu.VMEM((2, rp, 128), BF16), pltpu.VMEM((128, sp), F32),
           pltpu.VMEM((2, 128, 384), F32)],
        name="attend_backward",
        compiler_params=pltpu.CompilerParams(vmem_limit_bytes=56 << 20),
    )(qkv, qkv, qkv, dctx, probs, relk, relq, boxes_col, boxes_row)


EPSILON = 1e-05
ROOT_HALF = math.sqrt(0.5)
PDF_SCALE = 1.0 / math.sqrt(2.0 * math.pi)


def dot_nt(a, b):
    return lax.dot_general(a, b, (((1,), (1,)), ((), ())), preferred_element_type=F32)


def dot_tn(a, b):
    return lax.dot_general(a, b, (((0,), (0,)), ((), ())), preferred_element_type=F32)


def norm_rows(values, gain, shift):
    mean = jnp.mean(values, axis=1, keepdims=True)
    scale = lax.rsqrt(jnp.mean(values * values, axis=1, keepdims=True) - mean * mean + EPSILON)
    unit = (values - mean) * scale
    return unit * gain + shift, unit, scale


def norm_pull(upstream, unit, scale, gain):
    scaled = upstream * gain
    first = jnp.mean(scaled, axis=1, keepdims=True)
    second = jnp.mean(scaled * unit, axis=1, keepdims=True)
    return scale * (scaled - first - unit * second)


def exchange_sum(parts, bits, size, beside):
    place = lax.axis_index("dp")

    def swap(array, bit):
        return lax.ppermute(array, "dp", [(i, i ^ bit) for i in range(size)])

    def fold(array, bit):
        half = array.shape[0] // 2
        low = (place & bit) == 0
        keep = jnp.where(low, array[:half], array[half:])
        send = jnp.where(low, array[half:], array[:half])
        return (keep.astype(F32) + swap(send, bit).astype(F32)).astype(BF16)

    def unfold(array, bit):
        low = (place & bit) == 0
        other = swap(array, bit)
        return jnp.concatenate([jnp.where(low, array, other), jnp.where(low, other, array)], axis=0)

    arrays = [a for a, _ in parts]
    for step in range(len(bits)):
        arrays = [fold(a, order[step]) for a, (_, order) in zip(arrays, parts)]
    for step in reversed(range(len(bits))):
        if step == 0:
            arrays, beside = lax.optimization_barrier((arrays, beside))
        arrays = [unfold(a, order[step]) for a, (_, order) in zip(arrays, parts)]
    return arrays, beside


def sum_over_documents(table, size, beside):
    if size != 16:
        return lax.psum(table, "dp"), beside
    rows = table.shape[0]
    grain = 256
    pieces = 4
    step = -(-rows // (pieces * grain)) * grain
    padded = jnp.pad(table, ((0, pieces * step - rows), (0, 0)))
    orders = ((1, 2, 4, 8), (1, 4, 2, 8))
    parts = [(padded[i * step:(i + 1) * step], orders[i % 2]) for i in range(pieces)]
    arrays, beside = exchange_sum(parts, orders[0], size, beside)
    return jnp.concatenate(arrays, axis=0)[:rows], beside


def on_device(
    documents,
    shards,
    hidden_in,
    lengths,
    boxes,
    w_qkv,
    w_out,
    w_up,
    w_down,
    rel_keys,
    rel_queries,
    norm_gains,
    norm_shifts,
    out_grad,
):
    doc_count, slot_count, width = hidden_in.shape
    row_count = doc_count * slot_count
    model_width = w_qkv.shape[0]
    heads_here = width // HEAD_DIM
    me = lax.axis_index("tensor")
    pair = [(0, 1), (1, 0)]

    def join(array, axis):
        if shards != 2:
            return lax.all_gather(array, "tensor", axis=axis, tiled=True)
        other = lax.ppermute(array, "tensor", pair)
        first = me == 0
        return jnp.concatenate(
            [jnp.where(first, array, other), jnp.where(first, other, array)], axis=axis)

    def total(partial):
        if shards != 2:
            return lax.psum(partial, "tensor").astype(F32)
        return partial.astype(F32) + lax.ppermute(partial, "tensor", pair).astype(F32)

    def own(array):
        return lax.dynamic_slice_in_dim(array, me * width, width, axis=array.ndim - 1)

    def own_total(partial):
        if shards != 2:
            return lax.psum_scatter(partial, "tensor", scatter_dimension=1, tiled=True).astype(F32)
        send = lax.dynamic_slice_in_dim(partial, (1 - me) * width, width, axis=1)
        return own(partial).astype(F32) + lax.ppermute(send, "tensor", pair).astype(F32)

    rel_k = rel_keys.reshape(3 * BUCKETS, width)
    rel_q = rel_queries.reshape(3 * BUCKETS, width)
    padded = -(-slot_count // 128) * 128
    boxes_col = jnp.pad(boxes, ((0, 0), (0, padded - slot_count), (0, 0)))
    boxes_row = jnp.swapaxes(boxes_col, 1, 2)

    rows = join(hidden_in.reshape(row_count, width), 1)
    weight_qkv = w_qkv.reshape(model_width, 3 * width)
    projected = jnp.dot(rows, weight_qkv, preferred_element_type=F32).astype(BF16)
    norms = join(jnp.concatenate([norm_gains, norm_shifts], axis=0), 1)
    rows, out_rows = lax.optimization_barrier((rows, out_grad.reshape(row_count, width)))
    upstream = join(out_rows, 1)
    out_whole = join(w_out, 0)
    projected = projected.reshape(doc_count, slot_count, 3 * width)
    context, probs = attend_forward(lengths, projected, rel_k.T, rel_q.T, boxes_col, boxes_row, heads_here)
    context, upstream, norms, out_whole = lax.optimization_barrier((context, upstream, norms, out_whole))
    context = context.reshape(row_count, width)

    middle = row_count // 2 // 32 * 32 + 32 if row_count > 64 else row_count
    spans = [(a, b) for a, b in ((0, middle), (middle, row_count)) if b > a]
    join_context = [join(context[a:b], 1) for a, b in spans]
    first = []
    for (a, b), whole in zip(spans, join_context):
        attn = jnp.dot(whole, out_whole, preferred_element_type=F32)
        h1, unit, scale = norm_rows(rows[a:b].astype(F32) + attn, norms[0:1], norms[2:3])
        low = h1.astype(BF16)
        upper = jnp.dot(low, w_up, preferred_element_type=F32)
        chance = 0.5 * (1.0 + lax.erf(upper * ROOT_HALF))
        active = (upper * chance).astype(BF16)
        slope = (chance + upper * (PDF_SCALE * jnp.exp(-0.5 * upper * upper))).astype(BF16)
        ffn = total(jnp.dot(active, w_down, preferred_element_type=F32).astype(BF16))
        first.append((h1, unit, scale, low, active, slope, ffn))
    second = []
    for (a, b), (h1, unit, scale, low, active, slope, ffn) in zip(spans, first):
        result, unit_second, scale_second = norm_rows(h1 + ffn, norms[1:2], norms[3:4])
        up = upstream[a:b].astype(F32)
        grad = norm_pull(up, unit_second, scale_second, norms[1:2])
        grad, ffn_grad = lax.optimization_barrier((grad, grad.astype(BF16)))
        grad_upper = (dot_nt(ffn_grad, w_down) * slope.astype(F32)).astype(BF16)
        hidden = total(dot_nt(grad_upper, w_up).astype(BF16))
        sums = jnp.stack([jnp.sum(up * unit_second, axis=0), jnp.sum(up, axis=0)])
        second.append((result, grad, ffn_grad, grad_upper, hidden, sums))
    def stacked(found):
        return jnp.concatenate(found, axis=0)

    hidden_out = own(stacked([f[0].astype(BF16) for f in second])).reshape(doc_count, slot_count, width)
    hidden_out, arrived = lax.optimization_barrier((hidden_out, second[-1][4]))
    second[-1] = second[-1][:4] + (arrived,) + second[-1][5:]
    third = []
    for (h1, unit, scale, low, active, slope, ffn), (result, grad, ffn_grad, grad_upper, hidden, sums) in zip(first, second):
        grad_hidden = grad + hidden
        pulled = norm_pull(grad_hidden, unit, scale, norms[0:1])
        mine = jnp.stack([jnp.sum(grad_hidden * unit, axis=0), jnp.sum(grad_hidden, axis=0)])
        third.append((pulled, mine))

    ffn_grad = stacked([f[2] for f in second])
    grad_upper = stacked([f[3] for f in second])
    h1_low = stacked([f[3] for f in first])
    down_grad = dot_tn(stacked([f[4] for f in first]), ffn_grad).astype(BF16)
    up_grad = dot_tn(h1_low, grad_upper).astype(BF16)
    ffn_sums = lax.psum((down_grad, up_grad), "dp")
    grad_first = stacked([f[0] for f in third])
    attn_grad = grad_first.astype(BF16)
    sums_second = sum(f[5] for f in second)
    sums_first = sum(f[1] for f in third)
    norm_grads = own(jnp.stack([sums_first[0], sums_second[0], sums_first[1], sums_second[1]]))

    out_weight_grad = dot_tn(context, attn_grad)
    grad_context = dot_nt(attn_grad, w_out).astype(BF16).reshape(doc_count, slot_count, width)
    grad_projected, rel_k_sum, rel_q_sum = attend_backward(
        projected, grad_context, probs, rel_k, rel_q, boxes_col, boxes_row, heads_here
    )
    grad_rows = grad_projected.reshape(row_count, 3 * width)
    input_part = dot_nt(grad_rows, weight_qkv).astype(BF16)
    input_grad = own(grad_first) + own_total(input_part)
    input_grad = input_grad.astype(BF16).reshape(doc_count, slot_count, width)
    qkv_grads = [dot_tn(rows, grad_rows[:, t * width:(t + 1) * width]) for t in range(3)]
    pieces = qkv_grads + [jnp.sum(rel_k_sum, axis=0), jnp.sum(rel_q_sum, axis=0)]
    pieces += [out_weight_grad[:, t * width:(t + 1) * width] for t in range(shards)]
    pieces += [norm_grads]
    table, (down_grad, up_grad) = sum_over_documents(
        jnp.concatenate([p.astype(BF16) for p in pieces], axis=0), documents, ffn_sums)
    table = table.astype(F32)
    found = []
    at = 0
    for p in pieces:
        found.append(table[at:at + p.shape[0]])
        at += p.shape[0]
    qkv_grad = jnp.stack(found[0:3], axis=1)
    rel_keys_grad = found[3].reshape(3, BUCKETS, width)
    rel_queries_grad = found[4].reshape(3, BUCKETS, width)
    out_weight_grad = jnp.concatenate(found[5:5 + shards], axis=1)
    norm_grads = found[5 + shards]
    return (
        hidden_out,
        input_grad,
        qkv_grad,
        out_weight_grad,
        up_grad.astype(F32),
        down_grad.astype(F32),
        rel_keys_grad,
        rel_queries_grad,
        norm_grads[0:2],
        norm_grads[2:4],
    )


def solution(mesh):
    in_specs = (
        P("dp", None, "tensor"),
        P("dp"),
        P("dp", None, None),
        P(None, None, "tensor"),
        P("tensor", None),
        P(None, "tensor"),
        P("tensor", None),
        P(None, None, "tensor"),
        P(None, None, "tensor"),
        P(None, "tensor"),
        P(None, "tensor"),
        P("dp", None, "tensor"),
    )
    out_specs = (
        P("dp", None, "tensor"),
        P("dp", None, "tensor"),
        P(None, None, "tensor"),
        P("tensor", None),
        P(None, "tensor"),
        P("tensor", None),
        P(None, None, "tensor"),
        P(None, None, "tensor"),
        P(None, "tensor"),
        P(None, "tensor"),
    )
    body = functools.partial(on_device, mesh.shape["dp"], mesh.shape["tensor"])
    return jax.shard_map(body, mesh=mesh, in_specs=in_specs, out_specs=out_specs, check_vma=False)
```

```python
import math, functools
import jax, jax.numpy as jnp
from jax import lax
from jax.sharding import PartitionSpec as P
from jax.experimental import pallas as pl
from jax.experimental.pallas import tpu as pltpu

HEAD_DIM = 64
BUCKETS = 128
TEXT = 512
NEG = -1e30
LOG2E = math.log2(math.e)
SCALE = 1.0 / math.sqrt(3 * HEAD_DIM)
F32 = jnp.float32
BF16 = jnp.bfloat16


def nt(a, b):
    return lax.dot_general(a, b, (((1,), (1,)), ((), ())), preferred_element_type=F32)


def nn(a, b):
    return lax.dot_general(a, b, (((1,), (0,)), ((), ())), preferred_element_type=F32)


def iota(shape, d):
    return lax.broadcasted_iota(jnp.int32, shape, d)


def each(n, body, straight):
    if straight:
        for b in range(n):
            body(b, 0)
    else:
        lax.fori_loop(0, n, body, 0)


def at_block(b, size):
    return b * size if isinstance(b, int) else pl.multiple_of(b * size, size)


def pick(table, index):
    return jnp.take_along_axis(table, index, axis=1, mode="promise_in_bounds")


def pick(table, index):
    dims = lax.GatherDimensionNumbers(
        offset_dims=(), collapsed_slice_dims=(1,), start_index_map=(1,),
        operand_batching_dims=(0,), start_indices_batching_dims=(0,))
    return lax.gather(table, index[..., None], dims, slice_sizes=(1, 1),
                      mode=lax.GatherScatterMode.PROMISE_IN_BOUNDS)


LEVELS = 10900.0
HALF_WORD = 65536.0


def tall_block(rows):
    return next(n for n in (288, 192, 128, 64) if rows % n == 0)


def fwd_kernel(slots, sp, rp, len_ref, q_ref, k_ref, v_ref, relk_ref, relq_ref, bc_ref, br_ref,
               ctx_ref, p_ref, qs, ks, vs, kt, idx, nq, nk, sq, fq, fk, gk, cs):
    pair = pl.program_id(1)
    nb = sp // 128
    tall = tall_block(rp)

    @pl.when(pair == 0)
    def _():
        qs[...] = jnp.zeros_like(qs)
        ks[...] = jnp.zeros_like(ks)
        vs[...] = jnp.zeros_like(vs)

        def rows(b, c):
            r0 = at_block(b, 128)
            row = iota((128, sp), 0) + r0
            col = iota((128, sp), 1)
            idx[0, pl.ds(r0, 128), :] = jnp.clip(col - row, -64, 63) + 64
            for t in range(2):
                x_i = bc_ref[pl.ds(r0, 128), t:t + 1]
                x_j = br_ref[t:t + 1, :]
                idx[t + 1, pl.ds(r0, 128), :] = jnp.clip((x_j - x_i) >> 4, -64, 63) + 64
            return c
        lax.fori_loop(0, nb, rows, 0)

    qs[0:slots, :] = q_ref[...]
    ks[0:slots, :] = k_ref[...]
    vs[0:slots, :] = v_ref[...]
    kt[...] = ks[...].T
    place = iota((1, sp), 1)
    length = len_ref[pl.program_id(0)]
    barred = jnp.where((place < length) | ((place >= TEXT) & (place < slots)), 0.0, NEG)
    half = iota((1, 128), 1) < 64

    def longest(rel_ref, h):
        rel = rel_ref[h * 64:(h + 1) * 64, :].astype(F32)
        return jnp.max(jnp.sum(rel * rel, axis=0, keepdims=True), axis=1, keepdims=True) * 1.03

    def bound(squares, most):
        return jnp.maximum(squares * most, 1e-30)

    member = jnp.where((iota((128, 256), 0) < 64) == (iota((128, 256), 1) < 128), 1.0, 0.0).astype(BF16)
    for side, (rows_ref, rel_ref, table) in enumerate(((qs, relk_ref, nq), (ks, relq_ref, nk))):
        most = [longest(rel_ref, h) for h in range(2)]
        if side == 1:
            most_k = most

        def pack(b, c):
            r0 = at_block(b, tall)
            here = rows_ref[pl.ds(r0, tall), :]
            wide = here.astype(F32)
            squares = nn((wide * wide).astype(BF16), member)
            words = []
            for h in range(2):
                mine = half if h == 0 else jnp.logical_not(half)
                top = bound(squares[:, h * 128:(h + 1) * 128], most[h])
                inverse = lax.rsqrt(top)
                if side == 0:
                    sq[h, pl.ds(r0, tall), :] = top * inverse * (1.0 / (LEVELS * HALF_WORD))
                inverse = inverse * LEVELS
                near = nn(jnp.where(mine, here, 0), rel_ref[...])
                words.append(jnp.round(near * jnp.concatenate([inverse] * 3, axis=1)).astype(jnp.int32))
            table[pl.ds(r0, tall), :] = (words[0] << 16) + words[1]
            return c
        each(rp // tall, pack, True)

    turned = kt[...].astype(F32)
    turned = (turned * turned).astype(BF16)
    pick_head = jnp.where((iota((16, 128), 0) < 8) == (iota((16, 128), 1) < 64), 1.0, 0.0).astype(BF16)
    squares = nn(pick_head, turned)
    step_k = [jnp.sqrt(bound(squares[h * 8:h * 8 + 1, :], most_k[h])) * (1.0 / (LEVELS * HALF_WORD)) for h in range(2)]

    def near(r0, count):
        for r in range(0, count, 8):
            here = pl.ds(r0 + r if isinstance(r0, int) else pl.multiple_of(r0 + r, 8), 8)
            for jb in range(nb):
                at = slice(jb * 128, (jb + 1) * 128)
                sums = [None] * 2
                for t in range(3):
                    ix = idx[t, here, at]
                    kind = slice(t * 128, (t + 1) * 128)
                    for n, table in enumerate((nq, nk)):
                        e = pick(table[here, kind], ix)
                        sums[n] = e if sums[n] is None else sums[n] + e
                fq[here, at] = sums[0]
                gk[r:r + 8, at] = sums[1]
        for jb in range(nb):
            at = slice(jb * 128, (jb + 1) * 128)
            fk[at, pl.ds(r0, 128)] = gk[:, at].T

    def near_block(b, c):
        near(at_block(b, 128), 128)
        return c
    each(rp // 128, near_block, True)
    if rp % 128:
        gk[rp % 128:, :] = jnp.zeros((128 - rp % 128, sp), jnp.int32)
        near(rp // 128 * 128, rp % 128)

    def soft(b, c):
        r0 = at_block(b, tall)
        for h in range(2):
            mine = half if h == 0 else jnp.logical_not(half)
            q_b = jnp.where(mine, qs[pl.ds(r0, tall), :], 0)
            from_q = fq[pl.ds(r0, tall), :]
            from_k = fk[pl.ds(r0, tall), :]
            if h == 1:
                from_q = from_q << 16
                from_k = from_k << 16
            step_q = jnp.concatenate([sq[h, pl.ds(r0, tall), :]] * nb, axis=1)
            s = (nn(q_b, kt[...]) + barred) + (from_q.astype(F32) * step_q + from_k.astype(F32) * step_k[h])
            m = jnp.max(s, axis=1, keepdims=True)
            e = jnp.exp2((s - m) * (SCALE * LOG2E))
            tot = jnp.sum(e, axis=1, keepdims=True)
            p = (e * (1.0 / tot)).astype(BF16)
            p_ref[h, pl.ds(r0, tall), :] = p
            got = nn(p, vs[...])
            if h == 0:
                first = got
            else:
                cs[pl.ds(r0, tall), :] = jnp.where(mine, got, first).astype(BF16)
        return c
    each(rp // tall, soft, False)
    ctx_ref[...] = cs[0:slots, :]


def attend_forward(lengths, qkv, relk, relq, boxes_col, boxes_row, heads):
    docs, slots, width = qkv.shape
    width = width // 3
    sp = boxes_row.shape[2]
    rp = -(-slots // 64) * 64
    pairs = heads // 2

    def part(t):
        return pl.BlockSpec((None, slots, 128), lambda d, p, ln: (d, 0, t * pairs + p))
    rel = pl.BlockSpec((128, 3 * BUCKETS), lambda d, p, ln: (p, 0))
    grid_spec = pltpu.PrefetchScalarGridSpec(
        num_scalar_prefetch=1, grid=(docs, pairs),
        in_specs=[part(0), part(1), part(2), rel, rel,
                  pl.BlockSpec((None, sp, 2), lambda d, p, ln: (d, 0, 0)),
                  pl.BlockSpec((None, 2, sp), lambda d, p, ln: (d, 0, 0))],
        out_specs=[pl.BlockSpec((None, slots, 128), lambda d, p, ln: (d, 0, p)),
                   pl.BlockSpec((None, 2, rp, sp), lambda d, p, ln: (d, p, 0, 0))],
        scratch_shapes=[pltpu.VMEM((sp, 128), BF16)] * 3 + [pltpu.VMEM((128, sp), BF16)]
        + [pltpu.VMEM((3, sp, sp), jnp.int32), pltpu.VMEM((sp, 384), jnp.int32), pltpu.VMEM((sp, 384), jnp.int32),
           pltpu.VMEM((2, sp, 128), F32), pltpu.VMEM((sp, sp), jnp.int32), pltpu.VMEM((sp, sp), jnp.int32),
           pltpu.VMEM((128, sp), jnp.int32), pltpu.VMEM((rp, 128), BF16)])
    return pl.pallas_call(
        functools.partial(fwd_kernel, slots, sp, rp),
        out_shape=[jax.ShapeDtypeStruct((docs, slots, width), BF16),
                   jax.ShapeDtypeStruct((docs, heads, rp, sp), BF16)],
        grid_spec=grid_spec, name="attend_forward",
        compiler_params=pltpu.CompilerParams(vmem_limit_bytes=56 << 20),
    )(lengths, qkv, qkv, qkv, relk, relq, boxes_col, boxes_row)


def bwd_kernel(slots, sp, rp, width, q_ref, k_ref, v_ref, dc_ref, p_ref, relk_ref, relq_ref, bc_ref, br_ref,
               dqkv_ref, gk_ref, gq_ref,
               qs, ks, dcs, base, ex, ey, vt, qt, kt, dct, mx, my, ds, dst, w2, o1, hs, dns, gs, gt, acc):
    pair = pl.program_id(1)
    nb = sp // 128
    tall = tall_block(rp)

    @pl.when(pair == 0)
    def _():
        for r in (qs, ks, dcs, ds, dst):
            r[...] = jnp.zeros_like(r)
        lane = iota((sp, 128), 1)
        ax = bc_ref[:, 0:1] >> 4
        ay = bc_ref[:, 1:2] >> 4
        left = lane < 64
        c = lane & 63
        a = jnp.where(left, ax, ay)
        one = jnp.where(c == a, 1.0, 0.0)
        nxt = jnp.where(c == a + 1, 1.0, 0.0)
        base[...] = one.astype(BF16)
        e = nxt - one
        ex[...] = jnp.where(left, e, 0.0).astype(BF16)
        ey[...] = jnp.where(left, 0.0, e).astype(BF16)

        def rows(b, c):
            r0 = at_block(b, 128)
            for t, m in ((0, mx), (1, my)):
                r_i = bc_ref[pl.ds(r0, 128), t:t + 1] & 15
                r_j = br_ref[t:t + 1, :] & 15
                m[pl.ds(r0, 128), :] = jnp.where(r_j >= r_i, 1.0, 0.0).astype(BF16)
            return c
        lax.fori_loop(0, nb, rows, 0)

    qs[0:slots, :] = v_ref[...]
    vt[...] = qs[...].T
    qs[0:slots, :] = q_ref[...]
    ks[0:slots, :] = k_ref[...]
    dcs[0:slots, :] = dc_ref[...]
    qt[...] = qs[...].T
    kt[...] = ks[...].T
    dct[...] = dcs[...].T

    def head(h, carry):
        mine = (iota((1, 128), 1) < 64) == (h == 0)
        mine_down = (iota((128, 1), 0) < 64) == (h == 0)

        def grad_scores(b, c):
            r0 = at_block(b, tall)
            d_b = jnp.where(mine, dcs[pl.ds(r0, tall), :], 0)
            dp = nn(d_b, vt[...])
            p = p_ref[h, pl.ds(r0, tall), :].astype(F32)
            inner = jnp.sum(p * dp, axis=1, keepdims=True)
            ds[pl.ds(r0, tall), 128:128 + sp] = (p * (dp - inner)).astype(BF16)
            return c
        each(rp // tall, grad_scores, True)

        def turn(b, c):
            r0 = at_block(b, 128)
            for jb in range(nb):
                dst[jb * 128:(jb + 1) * 128, pl.ds(r0 + 128, 128)] = \
                    ds[pl.ds(r0, 128), (jb + 1) * 128:(jb + 2) * 128].T
            return c
        each(nb, turn, True)

        dvt = nn(dct[:, 0:rp], p_ref[h, :, :])
        gt[...] = jnp.where(mine_down, dvt, gt[...])

        for side in range(2):
            mat = ds if side == 0 else dst
            other = ks if side == 0 else qs
            own_t = qt if side == 0 else kt
            rel_ref = relk_ref if side == 0 else relq_ref
            blk = iota((sp, 128), 0) >> 7
            lane_sp = iota((sp, 128), 1) & 63
            w2[:, 0:128] = jnp.where(mine, other[...].astype(F32), jnp.where(blk == lane_sp, 1.0, 0.0)).astype(BF16)
            w2[:, 128:256] = base[...]

            def spread(b, c):
                r0 = at_block(b, tall)
                d_b = mat[pl.ds(r0, tall), 128:128 + sp]
                out = nn(d_b, w2[...])
                o1[pl.ds(r0, tall), :] = out[:, :128]
                hs[pl.ds(r0, tall), :] = out[:, 128:] + nn(d_b * mx[pl.ds(r0, tall), :], ex[...]) \
                    + nn(d_b * my[pl.ds(r0, tall), :], ey[...])
                return c
            each(rp // tall, spread, True)

            def buckets(b, r0, n):
                lane = iota((n, 128), 1)
                row = iota((n, 128), 0)
                before = mat[pl.ds(r0, n), pl.ds(r0, 128)].astype(F32)
                here = mat[pl.ds(r0, n), pl.ds(r0 + 128, 128)].astype(F32)
                after = mat[pl.ds(r0, n), pl.ds(r0 + 256, 128)].astype(F32)
                sums = jnp.where(mine, 0.0, o1[pl.ds(r0, n), :])
                blkno = lane & 63
                low = jnp.where(blkno <= b - 2, sums, 0.0) + jnp.where(lane <= row + 64, before, 0.0) \
                    + jnp.where(lane <= row - 64, here, 0.0)
                high = jnp.where(blkno >= b + 2, sums, 0.0) + jnp.where(lane >= row + 63, here, 0.0) \
                    + jnp.where(lane >= row - 65, after, 0.0)
                ones = jnp.ones((256, 128), BF16)

                def across(part):
                    top = part.astype(BF16)
                    return nn(jnp.concatenate([top, (part - top.astype(F32)).astype(BF16)], axis=1), ones)
                low = across(low)
                high = across(high)
                near = jnp.where(lane >= row + 64, before, jnp.where(lane <= row - 65, after, here))
                mid = pick(near, (lane + row + 64) & 127)
                dn0 = jnp.where(lane == 0, low, jnp.where(lane == 127, high, mid))
                hist = hs[pl.ds(r0, n), :]
                c1 = lane + (bc_ref[pl.ds(r0, n), 0:1] >> 4) - 63
                c2 = lane + (bc_ref[pl.ds(r0, n), 1:2] >> 4) - 63
                dn1 = jnp.where((c1 >= 0) & (c1 < 64), pick(hist, c1 & 127), 0.0)
                dn2 = jnp.where((c2 >= 0) & (c2 < 64), pick(hist, (c2 + 64) & 127), 0.0)
                dns[pl.ds(r0, n), :] = jnp.concatenate([dn0, dn1, dn2], axis=1).astype(BF16)

            def bucket_block(b, c):
                buckets(b, at_block(b, 128), 128)
                return c
            each(rp // 128, bucket_block, True)
            if rp % 128:
                buckets(rp // 128, rp // 128 * 128, rp % 128)

            def gather_back(b, c):
                r0 = at_block(b, tall)
                g = (o1[pl.ds(r0, tall), :] + nn(dns[pl.ds(r0, tall), :], rel_ref[...])) * SCALE
                gs[side, pl.ds(r0, tall), :] = jnp.where(mine, g, gs[side, pl.ds(r0, tall), :].astype(F32)).astype(BF16)
                return c
            each(rp // tall, gather_back, True)
            acc[side] = jnp.where(mine_down, nn(own_t[:, 0:rp], dns[...]), acc[side])
        return carry
    lax.fori_loop(0, 2, head, 0)

    for side in range(2):
        dqkv_ref[:, pl.ds(pl.multiple_of(side * width + pair * 128, 128), 128)] = gs[side, 0:slots, :]
    gk_ref[...] = acc[0].T * SCALE
    gq_ref[...] = acc[1].T * SCALE
    dqkv_ref[:, pl.ds(pl.multiple_of(2 * width + pair * 128, 128), 128)] = gt[...].T[0:slots, :].astype(BF16)


def attend_backward(qkv, dctx, probs, relk, relq, boxes_col, boxes_row, heads):
    docs, slots, width = qkv.shape
    width = width // 3
    sp = boxes_row.shape[2]
    rp = -(-slots // 64) * 64
    pairs = heads // 2

    def part(t):
        return pl.BlockSpec((None, slots, 128), lambda d, p: (d, 0, t * pairs + p))
    rel = pl.BlockSpec((3 * BUCKETS, 128), lambda d, p: (0, p))
    grel = pl.BlockSpec((None, 3 * BUCKETS, 128), lambda d, p: (d, 0, p))
    return pl.pallas_call(
        functools.partial(bwd_kernel, slots, sp, rp, width),
        grid=(docs, pairs),
        in_specs=[part(0), part(1), part(2),
                  pl.BlockSpec((None, slots, 128), lambda d, p: (d, 0, p)),
                  pl.BlockSpec((None, 2, rp, sp), lambda d, p: (d, p, 0, 0)),
                  rel, rel,
                  pl.BlockSpec((None, sp, 2), lambda d, p: (d, 0, 0)),
                  pl.BlockSpec((None, 2, sp), lambda d, p: (d, 0, 0))],
        out_specs=[pl.BlockSpec((None, slots, 3 * width), lambda d, p: (d, 0, 0)), grel, grel],
        out_shape=[jax.ShapeDtypeStruct((docs, slots, 3 * width), BF16),
                   jax.ShapeDtypeStruct((docs, 3 * BUCKETS, width), F32),
                   jax.ShapeDtypeStruct((docs, 3 * BUCKETS, width), F32)],
        scratch_shapes=[pltpu.VMEM((sp, 128), BF16)] * 6 + [pltpu.VMEM((128, sp), BF16)] * 4
        + [pltpu.VMEM((sp, sp), BF16)] * 2 + [pltpu.VMEM((sp, sp + 256), BF16)] * 2
        + [pltpu.VMEM((sp, 256), BF16), pltpu.VMEM((rp, 128), F32), pltpu.VMEM((rp, 128), F32),
           pltpu.VMEM((rp, 384), BF16), pltpu.VMEM((2, rp, 128), BF16), pltpu.VMEM((128, sp), F32),
           pltpu.VMEM((2, 128, 384), F32)],
        name="attend_backward",
        compiler_params=pltpu.CompilerParams(vmem_limit_bytes=56 << 20),
    )(qkv, qkv, qkv, dctx, probs, relk, relq, boxes_col, boxes_row)


EPSILON = 1e-05
ROOT_HALF = math.sqrt(0.5)
PDF_SCALE = 1.0 / math.sqrt(2.0 * math.pi)


def dot_nt(a, b):
    return lax.dot_general(a, b, (((1,), (1,)), ((), ())), preferred_element_type=F32)


def dot_tn(a, b):
    return lax.dot_general(a, b, (((0,), (0,)), ((), ())), preferred_element_type=F32)


def norm_rows(values, gain, shift):
    mean = jnp.mean(values, axis=1, keepdims=True)
    scale = lax.rsqrt(jnp.mean(values * values, axis=1, keepdims=True) - mean * mean + EPSILON)
    unit = (values - mean) * scale
    return unit * gain + shift, unit, scale


def norm_pull(upstream, unit, scale, gain):
    scaled = upstream * gain
    first = jnp.mean(scaled, axis=1, keepdims=True)
    second = jnp.mean(scaled * unit, axis=1, keepdims=True)
    return scale * (scaled - first - unit * second)


def exchange_sum(parts, bits, size, beside):
    place = lax.axis_index("dp")

    def swap(array, bit):
        return lax.ppermute(array, "dp", [(i, i ^ bit) for i in range(size)])

    def fold(array, bit):
        half = array.shape[0] // 2
        low = (place & bit) == 0
        keep = jnp.where(low, array[:half], array[half:])
        send = jnp.where(low, array[half:], array[:half])
        return (keep.astype(F32) + swap(send, bit).astype(F32)).astype(BF16)

    def unfold(array, bit):
        low = (place & bit) == 0
        other = swap(array, bit)
        return jnp.concatenate([jnp.where(low, array, other), jnp.where(low, other, array)], axis=0)

    arrays = [a for a, _ in parts]
    for step in range(len(bits)):
        arrays = [fold(a, order[step]) for a, (_, order) in zip(arrays, parts)]
    for step in reversed(range(len(bits))):
        if step == 0:
            arrays, beside = lax.optimization_barrier((arrays, beside))
        arrays = [unfold(a, order[step]) for a, (_, order) in zip(arrays, parts)]
    return arrays, beside


def sum_over_documents(table, size, beside):
    if size != 16:
        return lax.psum(table, "dp"), beside
    rows = table.shape[0]
    grain = 256
    pieces = 4
    step = -(-rows // (pieces * grain)) * grain
    padded = jnp.pad(table, ((0, pieces * step - rows), (0, 0)))
    orders = ((1, 2, 4, 8), (1, 4, 2, 8))
    parts = [(padded[i * step:(i + 1) * step], orders[i % 2]) for i in range(pieces)]
    arrays, beside = exchange_sum(parts, orders[0], size, beside)
    return jnp.concatenate(arrays, axis=0)[:rows], beside


def on_device(
    documents,
    shards,
    hidden_in,
    lengths,
    boxes,
    w_qkv,
    w_out,
    w_up,
    w_down,
    rel_keys,
    rel_queries,
    norm_gains,
    norm_shifts,
    out_grad,
):
    doc_count, slot_count, width = hidden_in.shape
    row_count = doc_count * slot_count
    model_width = w_qkv.shape[0]
    heads_here = width // HEAD_DIM
    me = lax.axis_index("tensor")
    pair = [(0, 1), (1, 0)]

    def join(array, axis):
        if shards != 2:
            return lax.all_gather(array, "tensor", axis=axis, tiled=True)
        other = lax.ppermute(array, "tensor", pair)
        first = me == 0
        return jnp.concatenate(
            [jnp.where(first, array, other), jnp.where(first, other, array)], axis=axis)

    def total(partial):
        if shards != 2:
            return lax.psum(partial, "tensor").astype(F32)
        return partial.astype(F32) + lax.ppermute(partial, "tensor", pair).astype(F32)

    def own(array):
        return lax.dynamic_slice_in_dim(array, me * width, width, axis=array.ndim - 1)

    def own_total(partial):
        if shards != 2:
            return lax.psum_scatter(partial, "tensor", scatter_dimension=1, tiled=True).astype(F32)
        send = lax.dynamic_slice_in_dim(partial, (1 - me) * width, width, axis=1)
        return own(partial).astype(F32) + lax.ppermute(send, "tensor", pair).astype(F32)

    rel_k = rel_keys.reshape(3 * BUCKETS, width)
    rel_q = rel_queries.reshape(3 * BUCKETS, width)
    padded = -(-slot_count // 128) * 128
    boxes_col = jnp.pad(boxes, ((0, 0), (0, padded - slot_count), (0, 0)))
    boxes_row = jnp.swapaxes(boxes_col, 1, 2)

    rows = join(hidden_in.reshape(row_count, width), 1)
    weight_qkv = w_qkv.reshape(model_width, 3 * width)
    projected = jnp.dot(rows, weight_qkv, preferred_element_type=F32).astype(BF16)
    norms = join(jnp.concatenate([norm_gains, norm_shifts], axis=0), 1)
    rows, out_rows = lax.optimization_barrier((rows, out_grad.reshape(row_count, width)))
    upstream = join(out_rows, 1)
    out_whole = join(w_out, 0)
    projected = projected.reshape(doc_count, slot_count, 3 * width)
    context, probs = attend_forward(lengths, projected, rel_k.T, rel_q.T, boxes_col, boxes_row, heads_here)
    context, upstream, norms, out_whole = lax.optimization_barrier((context, upstream, norms, out_whole))
    context = context.reshape(row_count, width)

    middle = row_count // 2 // 32 * 32 + 32 if row_count > 64 else row_count
    spans = [(a, b) for a, b in ((0, middle), (middle, row_count)) if b > a]
    join_context = [join(context[a:b], 1) for a, b in spans]
    first = []
    for (a, b), whole in zip(spans, join_context):
        attn = jnp.dot(whole, out_whole, preferred_element_type=F32)
        h1, unit, scale = norm_rows(rows[a:b].astype(F32) + attn, norms[0:1], norms[2:3])
        low = h1.astype(BF16)
        upper = jnp.dot(low, w_up, preferred_element_type=F32)
        chance = 0.5 * (1.0 + lax.erf(upper * ROOT_HALF))
        active = (upper * chance).astype(BF16)
        slope = (chance + upper * (PDF_SCALE * jnp.exp(-0.5 * upper * upper))).astype(BF16)
        ffn = total(jnp.dot(active, w_down, preferred_element_type=F32).astype(BF16))
        first.append((h1, unit, scale, low, active, slope, ffn))
    second = []
    for (a, b), (h1, unit, scale, low, active, slope, ffn) in zip(spans, first):
        result, unit_second, scale_second = norm_rows(h1 + ffn, norms[1:2], norms[3:4])
        up = upstream[a:b].astype(F32)
        grad = norm_pull(up, unit_second, scale_second, norms[1:2])
        grad, ffn_grad = lax.optimization_barrier((grad, grad.astype(BF16)))
        grad_upper = (dot_nt(ffn_grad, w_down) * slope.astype(F32)).astype(BF16)
        hidden = total(dot_nt(grad_upper, w_up).astype(BF16))
        sums = jnp.stack([jnp.sum(up * unit_second, axis=0), jnp.sum(up, axis=0)])
        second.append((result, grad, ffn_grad, grad_upper, hidden, sums))
    def stacked(found):
        return jnp.concatenate(found, axis=0)

    hidden_out = own(stacked([f[0].astype(BF16) for f in second])).reshape(doc_count, slot_count, width)
    hidden_out, arrived = lax.optimization_barrier((hidden_out, second[-1][4]))
    second[-1] = second[-1][:4] + (arrived,) + second[-1][5:]
    third = []
    for (h1, unit, scale, low, active, slope, ffn), (result, grad, ffn_grad, grad_upper, hidden, sums) in zip(first, second):
        grad_hidden = grad + hidden
        pulled = norm_pull(grad_hidden, unit, scale, norms[0:1])
        mine = jnp.stack([jnp.sum(grad_hidden * unit, axis=0), jnp.sum(grad_hidden, axis=0)])
        third.append((pulled, mine))

    ffn_grad = stacked([f[2] for f in second])
    grad_upper = stacked([f[3] for f in second])
    h1_low = stacked([f[3] for f in first])
    down_grad = dot_tn(stacked([f[4] for f in first]), ffn_grad).astype(BF16)
    up_grad = dot_tn(h1_low, grad_upper).astype(BF16)
    ffn_sums = lax.psum((down_grad, up_grad), "dp")
    grad_first = stacked([f[0] for f in third])
    attn_grad = grad_first.astype(BF16)
    sums_second = sum(f[5] for f in second)
    sums_first = sum(f[1] for f in third)
    norm_grads = own(jnp.stack([sums_first[0], sums_second[0], sums_first[1], sums_second[1]]))

    out_weight_grad = dot_tn(context, attn_grad)
    grad_context = dot_nt(attn_grad, w_out).astype(BF16).reshape(doc_count, slot_count, width)
    grad_projected, rel_k_sum, rel_q_sum = attend_backward(
        projected, grad_context, probs, rel_k, rel_q, boxes_col, boxes_row, heads_here
    )
    grad_rows = grad_projected.reshape(row_count, 3 * width)
    input_part = dot_nt(grad_rows, weight_qkv).astype(BF16)
    input_grad = own(grad_first) + own_total(input_part)
    input_grad = input_grad.astype(BF16).reshape(doc_count, slot_count, width)
    qkv_grads = [dot_tn(rows, grad_rows[:, t * width:(t + 1) * width]) for t in range(3)]
    pieces = qkv_grads + [jnp.sum(rel_k_sum, axis=0), jnp.sum(rel_q_sum, axis=0)]
    pieces += [out_weight_grad[:, t * width:(t + 1) * width] for t in range(shards)]
    pieces += [norm_grads]
    table, (down_grad, up_grad) = sum_over_documents(
        jnp.concatenate([p.astype(BF16) for p in pieces], axis=0), documents, ffn_sums)
    table = table.astype(F32)
    found = []
    at = 0
    for p in pieces:
        found.append(table[at:at + p.shape[0]])
        at += p.shape[0]
    qkv_grad = jnp.stack(found[0:3], axis=1)
    rel_keys_grad = found[3].reshape(3, BUCKETS, width)
    rel_queries_grad = found[4].reshape(3, BUCKETS, width)
    out_weight_grad = jnp.concatenate(found[5:5 + shards], axis=1)
    norm_grads = found[5 + shards]
    return (
        hidden_out,
        input_grad,
        qkv_grad,
        out_weight_grad,
        up_grad.astype(F32),
        down_grad.astype(F32),
        rel_keys_grad,
        rel_queries_grad,
        norm_grads[0:2],
        norm_grads[2:4],
    )


def solution(mesh):
    in_specs = (
        P("dp", None, "tensor"),
        P("dp"),
        P("dp", None, None),
        P(None, None, "tensor"),
        P("tensor", None),
        P(None, "tensor"),
        P("tensor", None),
        P(None, None, "tensor"),
        P(None, None, "tensor"),
        P(None, "tensor"),
        P(None, "tensor"),
        P("dp", None, "tensor"),
    )
    out_specs = (
        P("dp", None, "tensor"),
        P("dp", None, "tensor"),
        P(None, None, "tensor"),
        P("tensor", None),
        P(None, "tensor"),
        P("tensor", None),
        P(None, None, "tensor"),
        P(None, None, "tensor"),
        P(None, "tensor"),
        P(None, "tensor"),
    )
    body = functools.partial(on_device, mesh.shape["dp"], mesh.shape["tensor"])
    return jax.shard_map(body, mesh=mesh, in_specs=in_specs, out_specs=out_specs, check_vma=False)
```

```python
import math, functools
import jax, jax.numpy as jnp
from jax import lax
from jax.sharding import PartitionSpec as P
from jax.experimental import pallas as pl
from jax.experimental.pallas import tpu as pltpu

HEAD_DIM = 64
BUCKETS = 128
TEXT = 512
NEG = -1e30
LOG2E = math.log2(math.e)
SCALE = 1.0 / math.sqrt(3 * HEAD_DIM)
F32 = jnp.float32
BF16 = jnp.bfloat16


def nt(a, b):
    return lax.dot_general(a, b, (((1,), (1,)), ((), ())), preferred_element_type=F32)


def nn(a, b):
    return lax.dot_general(a, b, (((1,), (0,)), ((), ())), preferred_element_type=F32)


def iota(shape, d):
    return lax.broadcasted_iota(jnp.int32, shape, d)


def each(n, body, straight):
    if straight:
        for b in range(n):
            body(b, 0)
    else:
        lax.fori_loop(0, n, body, 0)


def at_block(b, size):
    return b * size if isinstance(b, int) else pl.multiple_of(b * size, size)


def pick(table, index):
    return jnp.take_along_axis(table, index, axis=1, mode="promise_in_bounds")


def pick(table, index):
    dims = lax.GatherDimensionNumbers(
        offset_dims=(), collapsed_slice_dims=(1,), start_index_map=(1,),
        operand_batching_dims=(0,), start_indices_batching_dims=(0,))
    return lax.gather(table, index[..., None], dims, slice_sizes=(1, 1),
                      mode=lax.GatherScatterMode.PROMISE_IN_BOUNDS)


LEVELS = 10900.0
HALF_WORD = 65536.0


def tall_block(rows):
    return next(n for n in (288, 192, 128, 64) if rows % n == 0)


def fwd_kernel(slots, sp, rp, len_ref, q_ref, k_ref, v_ref, relk_ref, relq_ref, bc_ref, br_ref,
               ctx_ref, p_ref, qs, ks, vs, kt, idx, nq, nk, sq, fq, fk, gk, cs):
    pair = pl.program_id(1)
    nb = sp // 128
    tall = tall_block(rp)

    @pl.when(pair == 0)
    def _():
        qs[...] = jnp.zeros_like(qs)
        ks[...] = jnp.zeros_like(ks)
        vs[...] = jnp.zeros_like(vs)

        def rows(b, c):
            r0 = at_block(b, 128)
            row = iota((128, sp), 0) + r0
            col = iota((128, sp), 1)
            idx[0, pl.ds(r0, 128), :] = jnp.clip(col - row, -64, 63) + 64
            for t in range(2):
                x_i = bc_ref[pl.ds(r0, 128), t:t + 1]
                x_j = br_ref[t:t + 1, :]
                idx[t + 1, pl.ds(r0, 128), :] = jnp.clip((x_j - x_i) >> 4, -64, 63) + 64
            return c
        lax.fori_loop(0, nb, rows, 0)

    qs[0:slots, :] = q_ref[...]
    ks[0:slots, :] = k_ref[...]
    vs[0:slots, :] = v_ref[...]
    kt[...] = ks[...].T
    place = iota((1, sp), 1)
    length = len_ref[pl.program_id(0)]
    barred = jnp.where((place < length) | ((place >= TEXT) & (place < slots)), 0.0, NEG)
    half = iota((1, 128), 1) < 64

    def longest(rel_ref, h):
        rel = rel_ref[h * 64:(h + 1) * 64, :].astype(F32)
        return jnp.max(jnp.sum(rel * rel, axis=0, keepdims=True), axis=1, keepdims=True) * 1.03

    def bound(squares, most):
        return jnp.maximum(squares * most, 1e-30)

    member = jnp.where((iota((128, 256), 0) < 64) == (iota((128, 256), 1) < 128), 1.0, 0.0).astype(BF16)
    for side, (rows_ref, rel_ref, table) in enumerate(((qs, relk_ref, nq), (ks, relq_ref, nk))):
        most = [longest(rel_ref, h) for h in range(2)]
        if side == 1:
            most_k = most

        def pack(b, c):
            r0 = at_block(b, tall)
            here = rows_ref[pl.ds(r0, tall), :]
            wide = here.astype(F32)
            squares = nn((wide * wide).astype(BF16), member)
            words = []
            for h in range(2):
                mine = half if h == 0 else jnp.logical_not(half)
                top = bound(squares[:, h * 128:(h + 1) * 128], most[h])
                inverse = lax.rsqrt(top)
                if side == 0:
                    sq[h, pl.ds(r0, tall), :] = top * inverse * (1.0 / (LEVELS * HALF_WORD))
                inverse = inverse * LEVELS
                near = nn(jnp.where(mine, here, 0), rel_ref[...])
                words.append(jnp.round(near * jnp.concatenate([inverse] * 3, axis=1)).astype(jnp.int32))
            table[pl.ds(r0, tall), :] = (words[0] << 16) + words[1]
            return c
        each(rp // tall, pack, True)

    turned = kt[...].astype(F32)
    turned = (turned * turned).astype(BF16)
    pick_head = jnp.where((iota((16, 128), 0) < 8) == (iota((16, 128), 1) < 64), 1.0, 0.0).astype(BF16)
    squares = nn(pick_head, turned)
    step_k = [jnp.sqrt(bound(squares[h * 8:h * 8 + 1, :], most_k[h])) * (1.0 / (LEVELS * HALF_WORD)) for h in range(2)]

    def near(r0, count):
        for r in range(0, count, 8):
            here = pl.ds(r0 + r if isinstance(r0, int) else pl.multiple_of(r0 + r, 8), 8)
            for jb in range(nb):
                at = slice(jb * 128, (jb + 1) * 128)
                sums = [None] * 2
                for t in range(3):
                    ix = idx[t, here, at]
                    kind = slice(t * 128, (t + 1) * 128)
                    for n, table in enumerate((nq, nk)):
                        e = pick(table[here, kind], ix)
                        sums[n] = e if sums[n] is None else sums[n] + e
                fq[here, at] = sums[0]
                gk[r:r + 8, at] = sums[1]
        for jb in range(nb):
            at = slice(jb * 128, (jb + 1) * 128)
            fk[at, pl.ds(r0, 128)] = gk[:, at].T

    def near_block(b, c):
        near(at_block(b, 128), 128)
        return c
    each(rp // 128, near_block, True)
    if rp % 128:
        gk[rp % 128:, :] = jnp.zeros((128 - rp % 128, sp), jnp.int32)
        near(rp // 128 * 128, rp % 128)

    def soft(b, c):
        r0 = at_block(b, tall)
        for h in range(2):
            mine = half if h == 0 else jnp.logical_not(half)
            q_b = jnp.where(mine, qs[pl.ds(r0, tall), :], 0)
            from_q = fq[pl.ds(r0, tall), :]
            from_k = fk[pl.ds(r0, tall), :]
            if h == 1:
                from_q = from_q << 16
                from_k = from_k << 16
            step_q = jnp.concatenate([sq[h, pl.ds(r0, tall), :]] * nb, axis=1)
            s = (nn(q_b, kt[...]) + barred) + (from_q.astype(F32) * step_q + from_k.astype(F32) * step_k[h])
            m = jnp.max(s, axis=1, keepdims=True)
            e = jnp.exp2((s - m) * (SCALE * LOG2E))
            tot = jnp.sum(e, axis=1, keepdims=True)
            p = (e * (1.0 / tot)).astype(BF16)
            p_ref[h, pl.ds(r0, tall), :] = p
            got = nn(p, vs[...])
            if h == 0:
                first = got
            else:
                cs[pl.ds(r0, tall), :] = jnp.where(mine, got, first).astype(BF16)
        return c
    each(rp // tall, soft, False)
    ctx_ref[...] = cs[0:slots, :]


def attend_forward(lengths, qkv, relk, relq, boxes_col, boxes_row, heads):
    docs, slots, width = qkv.shape
    width = width // 3
    sp = boxes_row.shape[2]
    rp = -(-slots // 64) * 64
    pairs = heads // 2

    def part(t):
        return pl.BlockSpec((None, slots, 128), lambda d, p, ln: (d, 0, t * pairs + p))
    rel = pl.BlockSpec((128, 3 * BUCKETS), lambda d, p, ln: (p, 0))
    grid_spec = pltpu.PrefetchScalarGridSpec(
        num_scalar_prefetch=1, grid=(docs, pairs),
        in_specs=[part(0), part(1), part(2), rel, rel,
                  pl.BlockSpec((None, sp, 2), lambda d, p, ln: (d, 0, 0)),
                  pl.BlockSpec((None, 2, sp), lambda d, p, ln: (d, 0, 0))],
        out_specs=[pl.BlockSpec((None, slots, 128), lambda d, p, ln: (d, 0, p)),
                   pl.BlockSpec((None, 2, rp, sp), lambda d, p, ln: (d, p, 0, 0))],
        scratch_shapes=[pltpu.VMEM((sp, 128), BF16)] * 3 + [pltpu.VMEM((128, sp), BF16)]
        + [pltpu.VMEM((3, sp, sp), jnp.int32), pltpu.VMEM((sp, 384), jnp.int32), pltpu.VMEM((sp, 384), jnp.int32),
           pltpu.VMEM((2, sp, 128), F32), pltpu.VMEM((sp, sp), jnp.int32), pltpu.VMEM((sp, sp), jnp.int32),
           pltpu.VMEM((128, sp), jnp.int32), pltpu.VMEM((rp, 128), BF16)])
    return pl.pallas_call(
        functools.partial(fwd_kernel, slots, sp, rp),
        out_shape=[jax.ShapeDtypeStruct((docs, slots, width), BF16),
                   jax.ShapeDtypeStruct((docs, heads, rp, sp), BF16)],
        grid_spec=grid_spec, name="attend_forward",
        compiler_params=pltpu.CompilerParams(vmem_limit_bytes=56 << 20),
    )(lengths, qkv, qkv, qkv, relk, relq, boxes_col, boxes_row)


def bwd_kernel(slots, sp, rp, width, q_ref, k_ref, v_ref, dc_ref, p_ref, relk_ref, relq_ref, bc_ref, br_ref,
               dqkv_ref, gk_ref, gq_ref,
               qs, ks, dcs, base, ex, ey, vt, qt, kt, dct, mx, my, ds, dst, w2, o1, hs, dns, gs, gt, acc):
    pair = pl.program_id(1)
    nb = sp // 128
    tall = tall_block(rp)

    @pl.when(pair == 0)
    def _():
        for r in (qs, ks, dcs, ds, dst):
            r[...] = jnp.zeros_like(r)
        lane = iota((sp, 128), 1)
        ax = bc_ref[:, 0:1] >> 4
        ay = bc_ref[:, 1:2] >> 4
        left = lane < 64
        c = lane & 63
        a = jnp.where(left, ax, ay)
        one = jnp.where(c == a, 1.0, 0.0)
        nxt = jnp.where(c == a + 1, 1.0, 0.0)
        base[...] = one.astype(BF16)
        e = nxt - one
        ex[...] = jnp.where(left, e, 0.0).astype(BF16)
        ey[...] = jnp.where(left, 0.0, e).astype(BF16)

        def rows(b, c):
            r0 = at_block(b, 128)
            for t, m in ((0, mx), (1, my)):
                r_i = bc_ref[pl.ds(r0, 128), t:t + 1] & 15
                r_j = br_ref[t:t + 1, :] & 15
                m[pl.ds(r0, 128), :] = jnp.where(r_j >= r_i, 1.0, 0.0).astype(BF16)
            return c
        lax.fori_loop(0, nb, rows, 0)

    qs[0:slots, :] = v_ref[...]
    vt[...] = qs[...].T
    qs[0:slots, :] = q_ref[...]
    ks[0:slots, :] = k_ref[...]
    dcs[0:slots, :] = dc_ref[...]
    qt[...] = qs[...].T
    kt[...] = ks[...].T
    dct[...] = dcs[...].T

    def head(h, carry):
        mine = (iota((1, 128), 1) < 64) == (h == 0)
        mine_down = (iota((128, 1), 0) < 64) == (h == 0)

        def grad_scores(b, c):
            r0 = at_block(b, tall)
            d_b = jnp.where(mine, dcs[pl.ds(r0, tall), :], 0)
            dp = nn(d_b, vt[...])
            p = p_ref[h, pl.ds(r0, tall), :].astype(F32)
            inner = jnp.sum(p * dp, axis=1, keepdims=True)
            ds[pl.ds(r0, tall), 128:128 + sp] = (p * (dp - inner)).astype(BF16)
            return c
        each(rp // tall, grad_scores, True)

        def turn(b, c):
            r0 = at_block(b, 128)
            for jb in range(nb):
                dst[jb * 128:(jb + 1) * 128, pl.ds(r0 + 128, 128)] = \
                    ds[pl.ds(r0, 128), (jb + 1) * 128:(jb + 2) * 128].T
            return c
        each(nb, turn, True)

        dvt = nn(dct[:, 0:rp], p_ref[h, :, :])
        gt[...] = jnp.where(mine_down, dvt, gt[...])

        for side in range(2):
            mat = ds if side == 0 else dst
            other = ks if side == 0 else qs
            own_t = qt if side == 0 else kt
            rel_ref = relk_ref if side == 0 else relq_ref
            blk = iota((sp, 128), 0) >> 7
            lane_sp = iota((sp, 128), 1) & 63
            w2[:, 0:128] = jnp.where(mine, other[...].astype(F32), jnp.where(blk == lane_sp, 1.0, 0.0)).astype(BF16)
            w2[:, 128:256] = base[...]

            def spread(b, c):
                r0 = at_block(b, tall)
                d_b = mat[pl.ds(r0, tall), 128:128 + sp]
                out = nn(d_b, w2[...])
                o1[pl.ds(r0, tall), :] = out[:, :128]
                hs[pl.ds(r0, tall), :] = out[:, 128:] + nn(d_b * mx[pl.ds(r0, tall), :], ex[...]) \
                    + nn(d_b * my[pl.ds(r0, tall), :], ey[...])
                return c
            each(rp // tall, spread, True)

            def buckets(b, r0, n):
                lane = iota((n, 128), 1)
                row = iota((n, 128), 0)
                before = mat[pl.ds(r0, n), pl.ds(r0, 128)].astype(F32)
                here = mat[pl.ds(r0, n), pl.ds(r0 + 128, 128)].astype(F32)
                after = mat[pl.ds(r0, n), pl.ds(r0 + 256, 128)].astype(F32)
                sums = jnp.where(mine, 0.0, o1[pl.ds(r0, n), :])
                blkno = lane & 63
                low = jnp.where(blkno <= b - 2, sums, 0.0) + jnp.where(lane <= row + 64, before, 0.0) \
                    + jnp.where(lane <= row - 64, here, 0.0)
                high = jnp.where(blkno >= b + 2, sums, 0.0) + jnp.where(lane >= row + 63, here, 0.0) \
                    + jnp.where(lane >= row - 65, after, 0.0)
                ones = jnp.ones((256, 128), BF16)

                def across(part):
                    top = part.astype(BF16)
                    return nn(jnp.concatenate([top, (part - top.astype(F32)).astype(BF16)], axis=1), ones)
                low = across(low)
                high = across(high)
                near = jnp.where(lane >= row + 64, before, jnp.where(lane <= row - 65, after, here))
                mid = pick(near, (lane + row + 64) & 127)
                dn0 = jnp.where(lane == 0, low, jnp.where(lane == 127, high, mid))
                hist = hs[pl.ds(r0, n), :]
                c1 = lane + (bc_ref[pl.ds(r0, n), 0:1] >> 4) - 63
                c2 = lane + (bc_ref[pl.ds(r0, n), 1:2] >> 4) - 63
                dn1 = jnp.where((c1 >= 0) & (c1 < 64), pick(hist, c1 & 127), 0.0)
                dn2 = jnp.where((c2 >= 0) & (c2 < 64), pick(hist, (c2 + 64) & 127), 0.0)
                dns[pl.ds(r0, n), :] = jnp.concatenate([dn0, dn1, dn2], axis=1).astype(BF16)

            def bucket_block(b, c):
                buckets(b, at_block(b, 128), 128)
                return c
            each(rp // 128, bucket_block, True)
            if rp % 128:
                buckets(rp // 128, rp // 128 * 128, rp % 128)

            def gather_back(b, c):
                r0 = at_block(b, tall)
                g = (o1[pl.ds(r0, tall), :] + nn(dns[pl.ds(r0, tall), :], rel_ref[...])) * SCALE
                gs[side, pl.ds(r0, tall), :] = jnp.where(mine, g, gs[side, pl.ds(r0, tall), :].astype(F32)).astype(BF16)
                return c
            each(rp // tall, gather_back, True)
            acc[side] = jnp.where(mine_down, nn(own_t[:, 0:rp], dns[...]), acc[side])
        return carry
    for h in range(2):
        head(h, 0)

    for side in range(2):
        dqkv_ref[:, pl.ds(pl.multiple_of(side * width + pair * 128, 128), 128)] = gs[side, 0:slots, :]
    gk_ref[...] = acc[0].T * SCALE
    gq_ref[...] = acc[1].T * SCALE
    dqkv_ref[:, pl.ds(pl.multiple_of(2 * width + pair * 128, 128), 128)] = gt[...].T[0:slots, :].astype(BF16)


def attend_backward(qkv, dctx, probs, relk, relq, boxes_col, boxes_row, heads):
    docs, slots, width = qkv.shape
    width = width // 3
    sp = boxes_row.shape[2]
    rp = -(-slots // 64) * 64
    pairs = heads // 2

    def part(t):
        return pl.BlockSpec((None, slots, 128), lambda d, p: (d, 0, t * pairs + p))
    rel = pl.BlockSpec((3 * BUCKETS, 128), lambda d, p: (0, p))
    grel = pl.BlockSpec((None, 3 * BUCKETS, 128), lambda d, p: (d, 0, p))
    return pl.pallas_call(
        functools.partial(bwd_kernel, slots, sp, rp, width),
        grid=(docs, pairs),
        in_specs=[part(0), part(1), part(2),
                  pl.BlockSpec((None, slots, 128), lambda d, p: (d, 0, p)),
                  pl.BlockSpec((None, 2, rp, sp), lambda d, p: (d, p, 0, 0)),
                  rel, rel,
                  pl.BlockSpec((None, sp, 2), lambda d, p: (d, 0, 0)),
                  pl.BlockSpec((None, 2, sp), lambda d, p: (d, 0, 0))],
        out_specs=[pl.BlockSpec((None, slots, 3 * width), lambda d, p: (d, 0, 0)), grel, grel],
        out_shape=[jax.ShapeDtypeStruct((docs, slots, 3 * width), BF16),
                   jax.ShapeDtypeStruct((docs, 3 * BUCKETS, width), F32),
                   jax.ShapeDtypeStruct((docs, 3 * BUCKETS, width), F32)],
        scratch_shapes=[pltpu.VMEM((sp, 128), BF16)] * 6 + [pltpu.VMEM((128, sp), BF16)] * 4
        + [pltpu.VMEM((sp, sp), BF16)] * 2 + [pltpu.VMEM((sp, sp + 256), BF16)] * 2
        + [pltpu.VMEM((sp, 256), BF16), pltpu.VMEM((rp, 128), F32), pltpu.VMEM((rp, 128), F32),
           pltpu.VMEM((rp, 384), BF16), pltpu.VMEM((2, rp, 128), BF16), pltpu.VMEM((128, sp), F32),
           pltpu.VMEM((2, 128, 384), F32)],
        name="attend_backward",
        compiler_params=pltpu.CompilerParams(vmem_limit_bytes=56 << 20),
    )(qkv, qkv, qkv, dctx, probs, relk, relq, boxes_col, boxes_row)


EPSILON = 1e-05
ROOT_HALF = math.sqrt(0.5)
PDF_SCALE = 1.0 / math.sqrt(2.0 * math.pi)


def dot_nt(a, b):
    return lax.dot_general(a, b, (((1,), (1,)), ((), ())), preferred_element_type=F32)


def dot_tn(a, b):
    return lax.dot_general(a, b, (((0,), (0,)), ((), ())), preferred_element_type=F32)


def norm_rows(values, gain, shift):
    mean = jnp.mean(values, axis=1, keepdims=True)
    scale = lax.rsqrt(jnp.mean(values * values, axis=1, keepdims=True) - mean * mean + EPSILON)
    unit = (values - mean) * scale
    return unit * gain + shift, unit, scale


def norm_pull(upstream, unit, scale, gain):
    scaled = upstream * gain
    first = jnp.mean(scaled, axis=1, keepdims=True)
    second = jnp.mean(scaled * unit, axis=1, keepdims=True)
    return scale * (scaled - first - unit * second)


def exchange_sum(parts, bits, size, beside):
    place = lax.axis_index("dp")

    def swap(array, bit):
        return lax.ppermute(array, "dp", [(i, i ^ bit) for i in range(size)])

    def fold(array, bit):
        half = array.shape[0] // 2
        low = (place & bit) == 0
        keep = jnp.where(low, array[:half], array[half:])
        send = jnp.where(low, array[half:], array[:half])
        return (keep.astype(F32) + swap(send, bit).astype(F32)).astype(BF16)

    def unfold(array, bit):
        low = (place & bit) == 0
        other = swap(array, bit)
        return jnp.concatenate([jnp.where(low, array, other), jnp.where(low, other, array)], axis=0)

    arrays = [a for a, _ in parts]
    for step in range(len(bits)):
        arrays = [fold(a, order[step]) for a, (_, order) in zip(arrays, parts)]
    for step in reversed(range(len(bits))):
        if step == 0:
            arrays, beside = lax.optimization_barrier((arrays, beside))
        arrays = [unfold(a, order[step]) for a, (_, order) in zip(arrays, parts)]
    return arrays, beside


def sum_over_documents(table, size, beside):
    if size != 16:
        return lax.psum(table, "dp"), beside
    rows = table.shape[0]
    grain = 256
    pieces = 4
    step = -(-rows // (pieces * grain)) * grain
    padded = jnp.pad(table, ((0, pieces * step - rows), (0, 0)))
    orders = ((1, 2, 4, 8), (1, 4, 2, 8))
    parts = [(padded[i * step:(i + 1) * step], orders[i % 2]) for i in range(pieces)]
    arrays, beside = exchange_sum(parts, orders[0], size, beside)
    return jnp.concatenate(arrays, axis=0)[:rows], beside


def on_device(
    documents,
    shards,
    hidden_in,
    lengths,
    boxes,
    w_qkv,
    w_out,
    w_up,
    w_down,
    rel_keys,
    rel_queries,
    norm_gains,
    norm_shifts,
    out_grad,
):
    doc_count, slot_count, width = hidden_in.shape
    row_count = doc_count * slot_count
    model_width = w_qkv.shape[0]
    heads_here = width // HEAD_DIM
    me = lax.axis_index("tensor")
    pair = [(0, 1), (1, 0)]

    def join(array, axis):
        if shards != 2:
            return lax.all_gather(array, "tensor", axis=axis, tiled=True)
        other = lax.ppermute(array, "tensor", pair)
        first = me == 0
        return jnp.concatenate(
            [jnp.where(first, array, other), jnp.where(first, other, array)], axis=axis)

    def total(partial):
        if shards != 2:
            return lax.psum(partial, "tensor").astype(F32)
        return partial.astype(F32) + lax.ppermute(partial, "tensor", pair).astype(F32)

    def own(array):
        return lax.dynamic_slice_in_dim(array, me * width, width, axis=array.ndim - 1)

    def own_total(partial):
        if shards != 2:
            return lax.psum_scatter(partial, "tensor", scatter_dimension=1, tiled=True).astype(F32)
        send = lax.dynamic_slice_in_dim(partial, (1 - me) * width, width, axis=1)
        return own(partial).astype(F32) + lax.ppermute(send, "tensor", pair).astype(F32)

    rel_k = rel_keys.reshape(3 * BUCKETS, width)
    rel_q = rel_queries.reshape(3 * BUCKETS, width)
    padded = -(-slot_count // 128) * 128
    boxes_col = jnp.pad(boxes, ((0, 0), (0, padded - slot_count), (0, 0)))
    boxes_row = jnp.swapaxes(boxes_col, 1, 2)

    rows = join(hidden_in.reshape(row_count, width), 1)
    weight_qkv = w_qkv.reshape(model_width, 3 * width)
    projected = jnp.dot(rows, weight_qkv, preferred_element_type=F32).astype(BF16)
    norms = join(jnp.concatenate([norm_gains, norm_shifts], axis=0), 1)
    rows, out_rows = lax.optimization_barrier((rows, out_grad.reshape(row_count, width)))
    upstream = join(out_rows, 1)
    out_whole = join(w_out, 0)
    projected = projected.reshape(doc_count, slot_count, 3 * width)
    context, probs = attend_forward(lengths, projected, rel_k.T, rel_q.T, boxes_col, boxes_row, heads_here)
    context, upstream, norms, out_whole = lax.optimization_barrier((context, upstream, norms, out_whole))
    context = context.reshape(row_count, width)

    middle = row_count // 2 // 32 * 32 + 32 if row_count > 64 else row_count
    spans = [(a, b) for a, b in ((0, middle), (middle, row_count)) if b > a]
    join_context = [join(context[a:b], 1) for a, b in spans]
    first = []
    for (a, b), whole in zip(spans, join_context):
        attn = jnp.dot(whole, out_whole, preferred_element_type=F32)
        h1, unit, scale = norm_rows(rows[a:b].astype(F32) + attn, norms[0:1], norms[2:3])
        low = h1.astype(BF16)
        upper = jnp.dot(low, w_up, preferred_element_type=F32)
        chance = 0.5 * (1.0 + lax.erf(upper * ROOT_HALF))
        active = (upper * chance).astype(BF16)
        slope = (chance + upper * (PDF_SCALE * jnp.exp(-0.5 * upper * upper))).astype(BF16)
        ffn = total(jnp.dot(active, w_down, preferred_element_type=F32).astype(BF16))
        first.append((h1, unit, scale, low, active, slope, ffn))
    second = []
    for (a, b), (h1, unit, scale, low, active, slope, ffn) in zip(spans, first):
        result, unit_second, scale_second = norm_rows(h1 + ffn, norms[1:2], norms[3:4])
        up = upstream[a:b].astype(F32)
        grad = norm_pull(up, unit_second, scale_second, norms[1:2])
        grad, ffn_grad = lax.optimization_barrier((grad, grad.astype(BF16)))
        grad_upper = (dot_nt(ffn_grad, w_down) * slope.astype(F32)).astype(BF16)
        hidden = total(dot_nt(grad_upper, w_up).astype(BF16))
        sums = jnp.stack([jnp.sum(up * unit_second, axis=0), jnp.sum(up, axis=0)])
        second.append((result, grad, ffn_grad, grad_upper, hidden, sums))
    def stacked(found):
        return jnp.concatenate(found, axis=0)

    hidden_out = own(stacked([f[0].astype(BF16) for f in second])).reshape(doc_count, slot_count, width)
    hidden_out, arrived = lax.optimization_barrier((hidden_out, second[-1][4]))
    second[-1] = second[-1][:4] + (arrived,) + second[-1][5:]
    third = []
    for (h1, unit, scale, low, active, slope, ffn), (result, grad, ffn_grad, grad_upper, hidden, sums) in zip(first, second):
        grad_hidden = grad + hidden
        pulled = norm_pull(grad_hidden, unit, scale, norms[0:1])
        mine = jnp.stack([jnp.sum(grad_hidden * unit, axis=0), jnp.sum(grad_hidden, axis=0)])
        third.append((pulled, mine))

    ffn_grad = stacked([f[2] for f in second])
    grad_upper = stacked([f[3] for f in second])
    h1_low = stacked([f[3] for f in first])
    down_grad = dot_tn(stacked([f[4] for f in first]), ffn_grad).astype(BF16)
    up_grad = dot_tn(h1_low, grad_upper).astype(BF16)
    ffn_sums = lax.psum((down_grad, up_grad), "dp")
    grad_first = stacked([f[0] for f in third])
    attn_grad = grad_first.astype(BF16)
    sums_second = sum(f[5] for f in second)
    sums_first = sum(f[1] for f in third)
    norm_grads = own(jnp.stack([sums_first[0], sums_second[0], sums_first[1], sums_second[1]]))

    out_weight_grad = dot_tn(context, attn_grad)
    grad_context = dot_nt(attn_grad, w_out).astype(BF16).reshape(doc_count, slot_count, width)
    grad_projected, rel_k_sum, rel_q_sum = attend_backward(
        projected, grad_context, probs, rel_k, rel_q, boxes_col, boxes_row, heads_here
    )
    grad_rows = grad_projected.reshape(row_count, 3 * width)
    input_part = dot_nt(grad_rows, weight_qkv).astype(BF16)
    input_grad = own(grad_first) + own_total(input_part)
    input_grad = input_grad.astype(BF16).reshape(doc_count, slot_count, width)
    qkv_grads = [dot_tn(rows, grad_rows[:, t * width:(t + 1) * width]) for t in range(3)]
    pieces = qkv_grads + [jnp.sum(rel_k_sum, axis=0), jnp.sum(rel_q_sum, axis=0)]
    pieces += [out_weight_grad[:, t * width:(t + 1) * width] for t in range(shards)]
    pieces += [norm_grads]
    table, (down_grad, up_grad) = sum_over_documents(
        jnp.concatenate([p.astype(BF16) for p in pieces], axis=0), documents, ffn_sums)
    table = table.astype(F32)
    found = []
    at = 0
    for p in pieces:
        found.append(table[at:at + p.shape[0]])
        at += p.shape[0]
    qkv_grad = jnp.stack(found[0:3], axis=1)
    rel_keys_grad = found[3].reshape(3, BUCKETS, width)
    rel_queries_grad = found[4].reshape(3, BUCKETS, width)
    out_weight_grad = jnp.concatenate(found[5:5 + shards], axis=1)
    norm_grads = found[5 + shards]
    return (
        hidden_out,
        input_grad,
        qkv_grad,
        out_weight_grad,
        up_grad.astype(F32),
        down_grad.astype(F32),
        rel_keys_grad,
        rel_queries_grad,
        norm_grads[0:2],
        norm_grads[2:4],
    )


def solution(mesh):
    in_specs = (
        P("dp", None, "tensor"),
        P("dp"),
        P("dp", None, None),
        P(None, None, "tensor"),
        P("tensor", None),
        P(None, "tensor"),
        P("tensor", None),
        P(None, None, "tensor"),
        P(None, None, "tensor"),
        P(None, "tensor"),
        P(None, "tensor"),
        P("dp", None, "tensor"),
    )
    out_specs = (
        P("dp", None, "tensor"),
        P("dp", None, "tensor"),
        P(None, None, "tensor"),
        P("tensor", None),
        P(None, "tensor"),
        P("tensor", None),
        P(None, None, "tensor"),
        P(None, None, "tensor"),
        P(None, "tensor"),
        P(None, "tensor"),
    )
    body = functools.partial(on_device, mesh.shape["dp"], mesh.shape["tensor"])
    return jax.shard_map(body, mesh=mesh, in_specs=in_specs, out_specs=out_specs, check_vma=False)
```
